32 devices in a mesh: dp: 4 (over z), ctx: 8 (over y, x, core).
Axes of the slice: x: 2, y: 2, z: 4, core: 2. Of those that a mesh axis runs over, the one named last changes fastest.
Arguments:
- block_input: bfloat16 [4, 2, 1152, 768], P('dp', None, 'ctx'), may hold values from -6 to 6
- cotangent: bfloat16 [4, 2, 1152, 768], P('dp', None, 'ctx'), may hold values from -6 to 6
- tie_map: int32 [13], replicated, may hold values from 0 to 1
- seq_lengths: int32 [4, 2, 4], P('dp'), may hold values from 1 to 1140, 1152 in all within a row
- span_place: int32 [4, 2, 8], P('dp'), may hold values from 0 to 7, each once within a row
- first_gain: bfloat16 [2, 768], P(None, ('dp', 'ctx')), may hold values from 0.099609375 to 1.8984375
- first_shift: bfloat16 [2, 768], P(None, ('dp', 'ctx')), may hold values from -3 to 3
- qkv_weight: bfloat16 [2, 768, 2304], P(None, None, ('dp', 'ctx')), may hold values from -0.3125 to 0.3125
- query_bias: bfloat16 [2, 768], P(None, ('dp', 'ctx')), may hold values from -3 to 3
- value_bias: bfloat16 [2, 768], P(None, ('dp', 'ctx')), may hold values from -3 to 3
- out_weight: bfloat16 [2, 768, 768], P(None, None, ('dp', 'ctx')), may hold values from -0.875 to 0.875
- out_bias: bfloat16 [2, 768], P(None, ('dp', 'ctx')), may hold values from -3 to 3
- second_gain: bfloat16 [2, 768], P(None, ('dp', 'ctx')), may hold values from 0.099609375 to 1.8984375
- second_shift: bfloat16 [2, 768], P(None, ('dp', 'ctx')), may hold values from -3 to 3
- up_weight: bfloat16 [2, 768, 3072], P(None, None, ('dp', 'ctx')), may hold values from -0.21875 to 0.21875
- up_bias: bfloat16 [2, 3072], P(None, ('dp', 'ctx')), may hold values from -3 to 3
- down_weight: bfloat16 [2, 3072, 768], P(None, ('dp', 'ctx')), may hold values from -0.109375 to 0.109375
- down_bias: bfloat16 [2, 768], P(None, ('dp', 'ctx')), may hold values from -3 to 3
Outputs:
- block_output: bfloat16 [4, 2, 1152, 768], P('dp', None, 'ctx')
- input_grad: bfloat16 [4, 2, 1152, 768], P('dp', None, 'ctx')
- first_gain_grad: float32 [2, 768], P(None, ('dp', 'ctx'))
- first_shift_grad: float32 [2, 768], P(None, ('dp', 'ctx'))
- qkv_weight_grad: float32 [2, 768, 2304], P(None, None, ('dp', 'ctx'))
- query_bias_grad: float32 [2, 768], P(None, ('dp', 'ctx'))
- value_bias_grad: float32 [2, 768], P(None, ('dp', 'ctx'))
- out_weight_grad: float32 [2, 768, 768], P(None, None, ('dp', 'ctx'))
- out_bias_grad: float32 [2, 768], P(None, ('dp', 'ctx'))
- second_gain_grad: float32 [2, 768], P(None, ('dp', 'ctx'))
- second_shift_grad: float32 [2, 768], P(None, ('dp', 'ctx'))
- up_weight_grad: float32 [2, 768, 3072], P(None, None, ('dp', 'ctx'))
- up_bias_grad: float32 [2, 3072], P(None, ('dp', 'ctx'))
- down_weight_grad: float32 [2, 3072, 768], P(None, ('dp', 'ctx'))
- down_bias_grad: float32 [2, 768], P(None, ('dp', 'ctx'))
The draws below stay inside these ranges and needn't reach their ends.
Inputs may be any that keep to these rules, and one draw needn't show every extreme that they name: `seq_lengths`: each row of 4 lengths sums to 1152, and its largest is exactly 1140. `span_place`: each row is a permutation of the 8 block numbers.
All inputs are finite; a program needn't handle non-finite values.
Results may differ from the reference program's by a relative error of at most 0.02.
Values may be sent and summed in bfloat16 or wider, within the bound.
A program may use at most 256 MiB of HBM per device.

```python
import math
import jax
import jax.numpy as jnp
import numpy as np
from jax import lax

D = 768
HEADS = 12
HD = 64
FF = 3072
SRC = 2
MB = 2
SEQS = 4
GROUPS = 4
CTX_DEV = 8
GROUP_TOK = 1152
LONGEST = 1140


def plant(result, key, smallest, top_value):
    shape = result.shape
    index_at = [jax.random.randint(jax.random.fold_in(key, axis), (), 0, shape[axis]) for axis in range(len(shape))]
    result = result.at[tuple(index_at)].set(smallest)
    longest = shape.index(max(shape))
    index_at[longest] = (index_at[longest] + 1) % shape[longest]
    return result.at[tuple(index_at)].set(top_value)


def shard_levels(rng, shape, pieces, low, high):
    loudness = 1.0
    for dim, parts in pieces:
        steps = jax.random.uniform(jax.random.fold_in(jax.random.fold_in(rng, 6), dim), (parts,), jnp.float32, low / len(pieces), high / len(pieces))
        loudness = loudness * jnp.repeat(jnp.exp(steps), shape[dim] // parts).reshape((-1,) + (1,) * (len(shape) - 1 - dim))
    return loudness


def profile(amount, total, most, slope):
    loads = [(1 << 20) // math.isqrt(rank ** slope) + 1 for rank in range(2, amount + 1)]
    surplus, holding = total - most - (amount - 1), [1] * (amount - 1)
    while surplus > 0:
        free = [i for i in range(amount - 1) if holding[i] < most]
        pool, left = sum([loads[i] for i in free]), surplus
        for i in free:
            more = min(most - holding[i], max(1, left * loads[i] // pool), surplus)
            holding[i] = holding[i] + more
            surplus = surplus - more
    return np.array([most] + holding)


def ragged_sizes(rng, count, total, bound, slope):
    if count == 2:
        one = jax.random.randint(rng, (), max(1, total - bound), min(bound, total - 1) + 1)
        return jnp.stack([one, total - one])
    tallies = jnp.asarray(profile(count, total, bound, slope), jnp.int32)
    twos = (count - 1) // 2
    source_of, taker = tallies[1:1 + 2 * twos:2], tallies[2:2 + 2 * twos:2]
    margin = jnp.minimum(source_of - 1, bound - taker)
    shifted = jax.random.randint(jax.random.fold_in(rng, 1), (twos,), 0, 1 << 20) % (margin + 1)
    tallies = tallies.at[1:1 + 2 * twos:2].set(source_of - shifted).at[2:2 + 2 * twos:2].set(taker + shifted)
    return tallies[jax.random.permutation(jax.random.fold_in(rng, 2), count)]


def normal_values(own_key, extent, spread, limit, cuts=(), kind=jnp.bfloat16):
    level = shard_levels(own_key, extent, cuts, -0.22, 0.18) if cuts else 1.0
    result = jax.random.normal(own_key, extent, jnp.float32) * spread * level
    return jnp.minimum(jnp.maximum(result, -limit), limit).astype(kind)


def setup_inputs(seed: int = 0) -> dict:
    streams_of = jax.random.split(jax.random.key(seed), 19)
    return {
        "block_input": normal_values(streams_of[0], (GROUPS, MB, GROUP_TOK, D), 1.0, 6.0, ((0, 4), (2, 8))),
        "cotangent": normal_values(streams_of[1], (GROUPS, MB, GROUP_TOK, D), 1.0, 6.0, ((0, 4), (2, 8))),
        "tie_map": plant(jax.random.randint(streams_of[2], (13,), 0, SRC), jax.random.fold_in(streams_of[2], 1), 0, SRC - 1).astype(jnp.int32),
        "seq_lengths": jax.vmap(lambda own: ragged_sizes(own, SEQS, GROUP_TOK, LONGEST, 2))(jax.random.split(streams_of[3], GROUPS * MB)).reshape((GROUPS, MB, SEQS)).astype(jnp.int32),
        "span_place": jax.vmap(lambda own: jax.random.permutation(own, CTX_DEV))(jax.random.split(streams_of[4], GROUPS * MB)).reshape((GROUPS, MB, CTX_DEV)).astype(jnp.int32),
        "first_gain": jnp.clip(1.0 + 0.18 * jax.random.normal(streams_of[5], (SRC, D), jnp.float32), 0.099609375, 1.8984375).astype(jnp.bfloat16),
        "first_shift": normal_values(streams_of[6], (SRC, D), 0.5, 3.0, ((1, 32),)),
        "qkv_weight": normal_values(streams_of[7], (SRC, D, 3 * D), (D // 2) ** -0.5, 0.3125, ((2, 32),)),
        "query_bias": normal_values(streams_of[8], (SRC, D), 0.5, 3.0, ((1, 32),)),
        "value_bias": normal_values(streams_of[9], (SRC, D), 0.5, 3.0, ((1, 32),)),
        "out_weight": normal_values(streams_of[10], (SRC, D, D), (D // 16) ** -0.5, 0.875, ((2, 32),)),
        "out_bias": normal_values(streams_of[11], (SRC, D), 0.5, 3.0, ((1, 32),)),
        "second_gain": jnp.clip(1.0 + 0.18 * jax.random.normal(streams_of[12], (SRC, D), jnp.float32), 0.099609375, 1.8984375).astype(jnp.bfloat16),
        "second_shift": normal_values(streams_of[13], (SRC, D), 0.5, 3.0, ((1, 32),)),
        "up_weight": normal_values(streams_of[14], (SRC, D, FF), D ** -0.5, 0.21875, ((2, 32),)),
        "up_bias": normal_values(streams_of[15], (SRC, FF), 0.5, 3.0, ((1, 32),)),
        "down_weight": normal_values(streams_of[16], (SRC, FF, D), FF ** -0.5, 0.109375, ((1, 32),)),
        "down_bias": normal_values(streams_of[17], (SRC, D), 0.5, 3.0, ((1, 32),)),
    }


precise = lax.Precision.HIGHEST
epsilon = 1e-05
masked_score = -1e+30
score_scale = 0.125

@jax.custom_vjp
def low(v):
    return lax.optimization_barrier(v.astype(jnp.bfloat16)).astype(jnp.float32)

@jax.custom_vjp
def low_back(v):
    return v

def low_keep(v):
    return (low(v), None)

def low_pass(kept, grad):
    return (grad,)

def back_keep(v):
    return (v, None)

def back_low(kept, grad):
    return (low(grad),)
low.defvjp(low_keep, low_pass)
low_back.defvjp(back_keep, back_low)

def layer_norm(inputs, norm_gain, norm_shift):
    average = lax.optimization_barrier(jnp.mean(inputs, axis=-1, keepdims=True))
    centered = inputs - average
    variance = lax.optimization_barrier(jnp.mean(centered * centered, axis=-1, keepdims=True))
    return centered * lax.rsqrt(variance + epsilon) * norm_gain + norm_shift

def stream_positions(span_row, rows_each):
    lane_total = span_row.shape[0]
    within = jnp.arange(lane_total * rows_each, dtype=jnp.int32) % rows_each
    repeated = jnp.repeat(span_row.astype(jnp.int32), rows_each, total_repeat_length=lane_total * rows_each)
    return (repeated * rows_each + within).astype(jnp.int32)

def segment_ids(positions, seq_ends):
    return lax.optimization_barrier(jnp.sum((positions[:, None] >= seq_ends[None, :]).astype(jnp.int32), axis=1))

def pack_forward(params, pack_rows, span_row, lengths_row):
    gain_before, shift_before, qkv_full, query_add, value_add, out_full, out_add, gain_after, shift_after, up_full, up_add, down_full, down_add = params
    row_count = pack_rows.shape[0]
    model_width = pack_rows.shape[1]
    positions = stream_positions(span_row, row_count // span_row.shape[0])
    segments = segment_ids(positions, jnp.cumsum(lengths_row).astype(jnp.int32))
    first_norm = low(layer_norm(pack_rows, gain_before, shift_before))
    projected = jnp.dot(first_norm, qkv_full, precision=precise)
    queries = low_back(low(projected[:, :model_width] + query_add))
    key_rows = low_back(low(projected[:, model_width:2 * model_width]))
    value_rows = low_back(low(projected[:, 2 * model_width:] + value_add))
    query_heads = queries.reshape(row_count, HEADS, HD)
    key_heads = key_rows.reshape(row_count, HEADS, HD)
    value_heads = value_rows.reshape(row_count, HEADS, HD)
    block_rows = math.gcd(row_count, 512)

    def attend_block(block_index):
        offset = (block_index * block_rows).astype(jnp.int32)
        query_block = lax.dynamic_slice_in_dim(query_heads, offset, block_rows, 0)
        query_pos = lax.dynamic_slice_in_dim(positions, offset, block_rows, 0)
        query_seg = lax.dynamic_slice_in_dim(segments, offset, block_rows, 0)
        scores = low_back(jnp.einsum('qhd,khd->hqk', query_block, key_heads, precision=precise) * score_scale)
        allowed = (query_seg[:, None] == segments[None, :]) & (positions[None, :] <= query_pos[:, None])
        scores = jnp.where(allowed[None], scores, masked_score)
        row_max = lax.optimization_barrier(jnp.max(scores, axis=2, keepdims=True))
        exp_scores = jnp.where(allowed[None], jnp.exp(scores - row_max), 0.0)
        probs = exp_scores / lax.optimization_barrier(jnp.sum(exp_scores, axis=2, keepdims=True))
        return jnp.einsum('hqk,khd->qhd', low(probs), value_heads, precision=precise)
    attended = lax.map(jax.checkpoint(attend_block), jnp.arange(row_count // block_rows, dtype=jnp.int32))
    attended = low_back(low(attended.reshape(row_count, model_width)))
    mixed_out = low_back(jnp.dot(attended, out_full, precision=precise) + out_add)
    residual = pack_rows + mixed_out
    second_norm = low(layer_norm(residual, gain_after, shift_after))
    up_proj = low_back(jnp.dot(second_norm, up_full, precision=precise) + up_add)
    activated = low(jax.nn.gelu(up_proj, approximate=True))
    down_proj = low_back(jnp.dot(activated, down_full, precision=precise) + down_add)
    return residual + down_proj

def reference(block_input, cotangent, tie_map, seq_lengths, span_place, first_gain, first_shift, qkv_weight, query_bias, value_bias, out_weight, out_bias, second_gain, second_shift, up_weight, up_bias, down_weight, down_bias):
    banks = (first_gain, first_shift, qkv_weight, query_bias, value_bias, out_weight, out_bias, second_gain, second_shift, up_weight, up_bias, down_weight, down_bias)
    wide_banks = tuple((weight_bank.astype(jnp.float32) for weight_bank in banks))
    shape_in = block_input.shape
    pack_count = shape_in[0] * shape_in[1]
    packs = block_input.astype(jnp.float32).reshape(pack_count, shape_in[2], shape_in[3])
    span_rows = span_place.reshape(pack_count, span_place.shape[2])
    length_rows = seq_lengths.reshape(pack_count, seq_lengths.shape[2])

    def forward(pack_inputs, bank_values):
        params = tuple((lax.dynamic_index_in_dim(weight_bank, tie_map[bank_number], 0, keepdims=False) for bank_number, weight_bank in enumerate(bank_values)))

        def one_pack(pack_item):
            return pack_forward(params, pack_item[0], pack_item[1], pack_item[2])
        return lax.map(jax.checkpoint(one_pack), (pack_inputs, span_rows, length_rows))
    outputs, pullback = jax.vjp(forward, packs, wide_banks)
    input_grads, bank_grads = pullback(cotangent.astype(jnp.float32).reshape(packs.shape))
    return (outputs.reshape(shape_in).astype(jnp.bfloat16), input_grads.reshape(shape_in).astype(jnp.bfloat16), bank_grads[0], bank_grads[1], bank_grads[2], bank_grads[3], bank_grads[4], bank_grads[5], bank_grads[6], bank_grads[7], bank_grads[8], bank_grads[9], bank_grads[10], bank_grads[11], bank_grads[12])
```

```python
import functools
import math

import jax
import jax.numpy as jnp
from jax import lax
from jax.experimental import pallas as pl
from jax.experimental.pallas import tpu as pltpu
from jax.sharding import PartitionSpec as P

HEADS = 12
HD = 64


epsilon = 1e-05
masked_score = -1e30
score_scale = 0.125
key_block = 1024


def layer_norm(inputs, norm_gain, norm_shift):
    average = jnp.mean(inputs, axis=-1, keepdims=True)
    centered = inputs - average
    variance = jnp.mean(centered * centered, axis=-1, keepdims=True)
    return centered * lax.rsqrt(variance + epsilon) * norm_gain + norm_shift


def gelu_tanh(inputs):
    return jax.nn.gelu(inputs, approximate=True)


def stream_positions(row_index, span_row, rows_each):
    owner_lane = row_index // rows_each
    lane_ids = jnp.arange(span_row.shape[0], dtype=jnp.int32)
    span_ids = jnp.sum(
        jnp.where(owner_lane[:, None] == lane_ids[None, :], span_row[None, :], 0), axis=1
    )
    return span_ids * rows_each + row_index % rows_each


def segment_ids(positions, seq_ends):
    return jnp.sum((positions[:, None] >= seq_ends[None, :]).astype(jnp.int32), axis=1)


def over_blocks(step_fn, state, pieces):
    piece_rows = pieces[0].shape[0]
    block_rows = math.gcd(piece_rows, key_block)
    stacked = tuple(
        (
            member.reshape((piece_rows // block_rows, block_rows) + member.shape[1:])
            for member in pieces
        )
    )

    def inner_step(running, scan_item):
        block_index, sliced = scan_item
        return (step_fn(running, sliced, block_index * block_rows), None)

    finished, ignored = lax.scan(
        inner_step, state, (jnp.arange(piece_rows // block_rows, dtype=jnp.int32), stacked)
    )
    return finished


def score_probs(
    query_heads,
    grad_heads,
    lse_heads,
    delta_heads,
    query_pos,
    query_seg,
    key_heads,
    value_heads,
    key_pos,
    key_seg,
):
    allowed = (query_seg[:, None] == key_seg[None, :]) & (key_pos[None, :] <= query_pos[:, None])
    scores = (
        jnp.einsum("qhd,khd->hqk", query_heads, key_heads, preferred_element_type=jnp.float32)
        * score_scale
    )
    probs = jnp.where(allowed[None], jnp.exp(scores - lse_heads[:, :, None]), 0.0)
    dprobs = jnp.einsum("qhd,khd->hqk", grad_heads, value_heads, preferred_element_type=jnp.float32)
    dscores = (probs * (dprobs - delta_heads[:, :, None])).astype(jnp.bfloat16)
    return (probs.astype(jnp.bfloat16), dscores)


def general_plan(
    block_input,
    cotangent,
    tie_map,
    seq_lengths,
    span_place,
    first_gain,
    first_shift,
    qkv_weight,
    query_bias,
    value_bias,
    out_weight,
    out_bias,
    second_gain,
    second_shift,
    up_weight,
    up_bias,
    down_weight,
    down_bias,
):
    banks = (
        first_gain,
        first_shift,
        qkv_weight,
        query_bias,
        value_bias,
        out_weight,
        out_bias,
        second_gain,
        second_shift,
        up_weight,
        up_bias,
        down_weight,
        down_bias,
    )
    shards = tuple(
        (
            lax.dynamic_index_in_dim(weight_bank, tie_map[bank_number], 0, keepdims=False)
            for bank_number, weight_bank in enumerate(banks)
        )
    )
    micro_count = block_input.shape[1]
    row_count = block_input.shape[2]
    model_width = block_input.shape[3]
    ctx_index = lax.axis_index("ctx")
    local_rows = ctx_index * row_count + jnp.arange(row_count, dtype=jnp.int32)
    totals = None
    outputs = []
    input_grads = []
    for micro_step in range(micro_count):
        params = (
            lax.all_gather(shards[0], ("dp", "ctx"), axis=0, tiled=True),
            lax.all_gather(shards[1], ("dp", "ctx"), axis=0, tiled=True),
            lax.all_gather(shards[2], ("dp", "ctx"), axis=1, tiled=True),
            lax.all_gather(shards[3], ("dp", "ctx"), axis=0, tiled=True),
            lax.all_gather(shards[4], ("dp", "ctx"), axis=0, tiled=True),
            lax.all_gather(shards[5], ("dp", "ctx"), axis=1, tiled=True),
            lax.all_gather(shards[6], ("dp", "ctx"), axis=0, tiled=True),
            lax.all_gather(shards[7], ("dp", "ctx"), axis=0, tiled=True),
            lax.all_gather(shards[8], ("dp", "ctx"), axis=0, tiled=True),
            lax.all_gather(shards[9], ("dp", "ctx"), axis=1, tiled=True),
            lax.all_gather(shards[10], ("dp", "ctx"), axis=0, tiled=True),
            lax.all_gather(shards[11], ("dp", "ctx"), axis=0, tiled=True),
            lax.all_gather(shards[12], ("dp", "ctx"), axis=0, tiled=True),
        )
        (
            gain_before,
            shift_before,
            qkv_full,
            query_add,
            value_add,
            out_full,
            out_add,
            gain_after,
            shift_after,
            up_full,
            up_add,
            down_full,
            down_add,
        ) = params
        span_row = span_place[0, micro_step]
        seq_ends = jnp.cumsum(seq_lengths[0, micro_step])
        query_pos = stream_positions(local_rows, span_row, row_count)
        query_seg = segment_ids(query_pos, seq_ends)
        inputs_wide = block_input[0, micro_step].astype(jnp.float32)
        first_norm = layer_norm(
            inputs_wide, gain_before.astype(jnp.float32), shift_before.astype(jnp.float32)
        ).astype(jnp.bfloat16)
        projected = jnp.dot(first_norm, qkv_full, preferred_element_type=jnp.float32)
        queries = (projected[:, :model_width] + query_add.astype(jnp.float32)).astype(jnp.bfloat16)
        key_rows = projected[:, model_width : 2 * model_width].astype(jnp.bfloat16)
        value_rows = (projected[:, 2 * model_width :] + value_add.astype(jnp.float32)).astype(
            jnp.bfloat16
        )
        query_heads = queries.reshape(row_count, HEADS, HD)
        key_heads_own = key_rows.reshape(row_count, HEADS, HD)
        value_heads_own = value_rows.reshape(row_count, HEADS, HD)

        def attend(state, pieces, offset):
            row_max, row_sum, accumulated = state
            key_part, value_part = pieces
            piece_rows = key_part.shape[0]
            key_pos = stream_positions(
                offset + jnp.arange(piece_rows, dtype=jnp.int32), span_row, row_count
            )
            key_seg = segment_ids(key_pos, seq_ends)
            allowed = (query_seg[:, None] == key_seg[None, :]) & (
                key_pos[None, :] <= query_pos[:, None]
            )
            scores = (
                jnp.einsum(
                    "qhd,khd->hqk",
                    query_heads,
                    key_part.reshape(piece_rows, HEADS, HD),
                    preferred_element_type=jnp.float32,
                )
                * score_scale
            )
            scores = jnp.where(allowed[None], scores, masked_score)
            new_max = jnp.maximum(row_max, jnp.max(scores, axis=2))
            exp_scores = jnp.where(allowed[None], jnp.exp(scores - new_max[:, :, None]), 0.0)
            factor = jnp.exp(row_max - new_max)
            row_sum = row_sum * factor + jnp.sum(exp_scores, axis=2)
            accumulated = accumulated * factor.T[:, :, None] + jnp.einsum(
                "hqk,khd->qhd",
                exp_scores.astype(jnp.bfloat16),
                value_part.reshape(piece_rows, HEADS, HD),
                preferred_element_type=jnp.float32,
            )
            return (new_max, row_sum, accumulated)

        start_state = (
            jnp.full((HEADS, row_count), masked_score, jnp.float32),
            jnp.zeros((HEADS, row_count), jnp.float32),
            jnp.zeros((row_count, HEADS, HD), jnp.float32),
        )
        row_max, row_sum, accumulated = over_blocks(
            attend,
            start_state,
            (
                lax.all_gather(key_rows, "ctx", axis=0, tiled=True),
                lax.all_gather(value_rows, "ctx", axis=0, tiled=True),
            ),
        )
        attended_wide = accumulated / row_sum.T[:, :, None]
        log_sums = row_max + jnp.log(row_sum)
        attended = attended_wide.reshape(row_count, model_width).astype(jnp.bfloat16)
        mixed_out = jnp.dot(
            attended, out_full, preferred_element_type=jnp.float32
        ) + out_add.astype(jnp.float32)
        residual = inputs_wide + mixed_out
        second_norm = layer_norm(
            residual, gain_after.astype(jnp.float32), shift_after.astype(jnp.float32)
        ).astype(jnp.bfloat16)
        up_proj = jnp.dot(second_norm, up_full, preferred_element_type=jnp.float32) + up_add.astype(
            jnp.float32
        )
        activated = gelu_tanh(up_proj).astype(jnp.bfloat16)
        down_proj = jnp.dot(
            activated, down_full, preferred_element_type=jnp.float32
        ) + down_add.astype(jnp.float32)
        outputs.append((residual + down_proj).astype(jnp.bfloat16))
        params = (
            lax.all_gather(shards[0], ("dp", "ctx"), axis=0, tiled=True),
            lax.all_gather(shards[1], ("dp", "ctx"), axis=0, tiled=True),
            lax.all_gather(shards[2], ("dp", "ctx"), axis=1, tiled=True),
            lax.all_gather(shards[3], ("dp", "ctx"), axis=0, tiled=True),
            lax.all_gather(shards[4], ("dp", "ctx"), axis=0, tiled=True),
            lax.all_gather(shards[5], ("dp", "ctx"), axis=1, tiled=True),
            lax.all_gather(shards[6], ("dp", "ctx"), axis=0, tiled=True),
            lax.all_gather(shards[7], ("dp", "ctx"), axis=0, tiled=True),
            lax.all_gather(shards[8], ("dp", "ctx"), axis=0, tiled=True),
            lax.all_gather(shards[9], ("dp", "ctx"), axis=1, tiled=True),
            lax.all_gather(shards[10], ("dp", "ctx"), axis=0, tiled=True),
            lax.all_gather(shards[11], ("dp", "ctx"), axis=0, tiled=True),
            lax.all_gather(shards[12], ("dp", "ctx"), axis=0, tiled=True),
        )
        (
            gain_before,
            shift_before,
            qkv_full,
            query_add,
            value_add,
            out_full,
            out_add,
            gain_after,
            shift_after,
            up_full,
            up_add,
            down_full,
            down_add,
        ) = params
        grad_out = cotangent[0, micro_step].astype(jnp.float32)
        grad_down = grad_out.astype(jnp.bfloat16)
        down_weight_grad = jnp.einsum(
            "rf,rd->fd", activated, grad_down, preferred_element_type=jnp.float32
        )
        down_bias_grad = jnp.sum(grad_down.astype(jnp.float32), axis=0)
        grad_act = jnp.einsum("rd,fd->rf", grad_down, down_full, preferred_element_type=jnp.float32)
        unused_gelu, gelu_back = jax.vjp(gelu_tanh, up_proj)
        grad_up = gelu_back(grad_act)[0].astype(jnp.bfloat16)
        up_weight_grad = jnp.einsum(
            "rd,rf->df", second_norm, grad_up, preferred_element_type=jnp.float32
        )
        up_bias_grad = jnp.sum(grad_up.astype(jnp.float32), axis=0)
        grad_second = jnp.einsum("rf,df->rd", grad_up, up_full, preferred_element_type=jnp.float32)
        unused_second, second_back = jax.vjp(
            layer_norm, residual, gain_after.astype(jnp.float32), shift_after.astype(jnp.float32)
        )
        grad_resid, second_gain_grad, second_shift_grad = second_back(grad_second)
        grad_resid = grad_resid + grad_out
        grad_mixed = grad_resid.astype(jnp.bfloat16)
        out_weight_grad = jnp.einsum(
            "rc,rd->cd", attended, grad_mixed, preferred_element_type=jnp.float32
        )
        out_bias_grad = jnp.sum(grad_mixed.astype(jnp.float32), axis=0)
        grad_attended = jnp.einsum(
            "rd,cd->rc", grad_mixed, out_full, preferred_element_type=jnp.float32
        ).astype(jnp.bfloat16)
        grad_heads = grad_attended.reshape(row_count, HEADS, HD)
        delta_rows = jnp.sum(grad_heads.astype(jnp.float32) * attended_wide, axis=2)
        delta_heads = delta_rows.T
        empty_heads = jnp.zeros((row_count, HEADS, HD), jnp.float32)
        stats_whole = (
            lax.all_gather(log_sums.T, "ctx", axis=0, tiled=True),
            lax.all_gather(delta_rows, "ctx", axis=0, tiled=True),
        )

        def mutual(state, pieces, offset):
            grad_query, grad_key, grad_value = state
            key_part, value_part, query_part, gradout_part = pieces
            piece_rows = key_part.shape[0]
            lse_part = lax.dynamic_slice_in_dim(stats_whole[0], offset, piece_rows, 0)
            delta_part = lax.dynamic_slice_in_dim(stats_whole[1], offset, piece_rows, 0)
            key_pos = stream_positions(
                offset + jnp.arange(piece_rows, dtype=jnp.int32), span_row, row_count
            )
            key_seg = segment_ids(key_pos, seq_ends)
            key_part_heads = key_part.reshape(piece_rows, HEADS, HD)
            value_part_heads = value_part.reshape(piece_rows, HEADS, HD)
            query_part_heads = query_part.reshape(piece_rows, HEADS, HD)
            gradout_heads = gradout_part.reshape(piece_rows, HEADS, HD)
            probs, dscores = score_probs(
                query_heads,
                grad_heads,
                log_sums,
                delta_heads,
                query_pos,
                query_seg,
                key_part_heads,
                value_part_heads,
                key_pos,
                key_seg,
            )
            grad_query = grad_query + score_scale * jnp.einsum(
                "hqk,khd->qhd", dscores, key_part_heads, preferred_element_type=jnp.float32
            )
            probs_other, dscores_other = score_probs(
                query_part_heads,
                gradout_heads,
                lse_part.T,
                delta_part.T,
                key_pos,
                key_seg,
                key_heads_own,
                value_heads_own,
                query_pos,
                query_seg,
            )
            grad_key = grad_key + score_scale * jnp.einsum(
                "hqk,qhd->khd", dscores_other, query_part_heads, preferred_element_type=jnp.float32
            )
            grad_value = grad_value + jnp.einsum(
                "hqk,qhd->khd", probs_other, gradout_heads, preferred_element_type=jnp.float32
            )
            return (grad_query, grad_key, grad_value)

        grad_query, grad_key, grad_value = over_blocks(
            mutual,
            (empty_heads, empty_heads, empty_heads),
            (
                lax.all_gather(key_rows, "ctx", axis=0, tiled=True),
                lax.all_gather(value_rows, "ctx", axis=0, tiled=True),
                lax.all_gather(queries, "ctx", axis=0, tiled=True),
                lax.all_gather(grad_attended, "ctx", axis=0, tiled=True),
            ),
        )
        grad_proj = jnp.concatenate(
            [
                grad_query.reshape(row_count, model_width),
                grad_key.reshape(row_count, model_width),
                grad_value.reshape(row_count, model_width),
            ],
            axis=1,
        ).astype(jnp.bfloat16)
        qkv_weight_grad = jnp.einsum(
            "rc,rp->cp", first_norm, grad_proj, preferred_element_type=jnp.float32
        )
        query_bias_grad = jnp.sum(grad_proj[:, :model_width].astype(jnp.float32), axis=0)
        value_bias_grad = jnp.sum(grad_proj[:, 2 * model_width :].astype(jnp.float32), axis=0)
        grad_first = jnp.einsum(
            "rp,cp->rc", grad_proj, qkv_full, preferred_element_type=jnp.float32
        )
        unused_first, first_back = jax.vjp(
            layer_norm,
            inputs_wide,
            gain_before.astype(jnp.float32),
            shift_before.astype(jnp.float32),
        )
        grad_input, first_gain_grad, first_shift_grad = first_back(grad_first)
        input_grads.append((grad_input + grad_resid).astype(jnp.bfloat16))
        micro_grads = (
            first_gain_grad,
            first_shift_grad,
            qkv_weight_grad,
            query_bias_grad,
            value_bias_grad,
            out_weight_grad,
            out_bias_grad,
            second_gain_grad,
            second_shift_grad,
            up_weight_grad,
            up_bias_grad,
            down_weight_grad,
            down_bias_grad,
        )
        if totals is None:
            totals = micro_grads
        else:
            totals = tuple(
                (left_sum + right_sum for left_sum, right_sum in zip(totals, micro_grads))
            )
    owned = (
        lax.psum_scatter(totals[0], ("dp", "ctx"), scatter_dimension=0, tiled=True),
        lax.psum_scatter(totals[1], ("dp", "ctx"), scatter_dimension=0, tiled=True),
        lax.psum_scatter(totals[2], ("dp", "ctx"), scatter_dimension=1, tiled=True),
        lax.psum_scatter(totals[3], ("dp", "ctx"), scatter_dimension=0, tiled=True),
        lax.psum_scatter(totals[4], ("dp", "ctx"), scatter_dimension=0, tiled=True),
        lax.psum_scatter(totals[5], ("dp", "ctx"), scatter_dimension=1, tiled=True),
        lax.psum_scatter(totals[6], ("dp", "ctx"), scatter_dimension=0, tiled=True),
        lax.psum_scatter(totals[7], ("dp", "ctx"), scatter_dimension=0, tiled=True),
        lax.psum_scatter(totals[8], ("dp", "ctx"), scatter_dimension=0, tiled=True),
        lax.psum_scatter(totals[9], ("dp", "ctx"), scatter_dimension=1, tiled=True),
        lax.psum_scatter(totals[10], ("dp", "ctx"), scatter_dimension=0, tiled=True),
        lax.psum_scatter(totals[11], ("dp", "ctx"), scatter_dimension=0, tiled=True),
        lax.psum_scatter(totals[12], ("dp", "ctx"), scatter_dimension=0, tiled=True),
    )
    bank_grads = tuple(
        (
            lax.dynamic_update_index_in_dim(
                jnp.zeros(weight_bank.shape, jnp.float32), owned_piece, tie_map[bank_number], 0
            )
            for bank_number, (weight_bank, owned_piece) in enumerate(zip(banks, owned))
        )
    )
    block_output = jnp.stack(outputs)[None]
    input_grad = jnp.stack(input_grads)[None]
    return (block_output, input_grad) + bank_grads


BF = jnp.bfloat16
F32 = jnp.float32
MESH = pl.DeviceIdType.MESH
ANY = pl.ANY
SMALL = 8
VMEM_BYTES = 60 * 2**20


def params(collective_id=None):
    if collective_id is None:
        return pltpu.CompilerParams(vmem_limit_bytes=VMEM_BYTES)
    return pltpu.CompilerParams(
        vmem_limit_bytes=VMEM_BYTES, collective_id=collective_id, has_side_effects=True
    )


def vmem():
    return pl.BlockSpec(memory_space=pltpu.VMEM)


def smem():
    return pl.BlockSpec(memory_space=pltpu.SMEM)


def anywhere():
    return pl.BlockSpec(memory_space=ANY)


def shape(dims, dtype):
    return jax.ShapeDtypeStruct(dims, dtype)


def nn(left, right):
    return lax.dot_general(left, right, (((1,), (0,)), ((), ())), preferred_element_type=F32)


def nt(left, right):
    return lax.dot_general(left, right, (((1,), (1,)), ((), ())), preferred_element_type=F32)


def tn(left, right):
    return lax.dot_general(left, right, (((0,), (0,)), ((), ())), preferred_element_type=F32)


def iota(dims, axis):
    return lax.broadcasted_iota(jnp.int32, dims, axis)


class Place:
    def __init__(self, depth):
        self.depth = depth
        self.z = lax.axis_index("dp")
        self.r = lax.axis_index("ctx")
        self.core = self.r % 2
        self.j = self.r // 2
        self.a = self.r // 4
        self.b = (self.r // 2) % 2
        self.by_a = (1 - self.a) * 4 + self.b * 2 + self.core
        self.by_b = self.a * 4 + (1 - self.b) * 2 + self.core
        self.both = (1 - self.a) * 4 + (1 - self.b) * 2 + self.core
        self.mate = self.j * 2 + 1 - self.core

    def slot(self, z, r):
        return z * 8 + r


def greet(here, whole_plane, line, axes=True):
    bar = pltpu.get_barrier_semaphore()
    count = 0
    if whole_plane:
        for k in range(1, 8):
            pl.semaphore_signal(
                bar, inc=1, device_id=(here.z, (here.r + k) % 8), device_id_type=MESH
            )
        count = 7
    if line:
        for k in range(1, here.depth):
            pl.semaphore_signal(
                bar, inc=1, device_id=((here.z + k) % here.depth, here.r), device_id_type=MESH
            )
        count = count + here.depth - 1
    pl.semaphore_wait(bar, count)


def greet_all(here):
    bar = pltpu.get_barrier_semaphore()
    total = here.depth * 8
    me = here.z * 8 + here.r

    def signal(k, carry):
        other = (me + k) % total
        pl.semaphore_signal(bar, inc=1, device_id=(other // 8, other % 8), device_id_type=MESH)
        return carry

    lax.fori_loop(1, total, signal, 0)
    pl.semaphore_wait(bar, total - 1)


def remote(source, target, send, recv, z, r):
    return pltpu.make_async_remote_copy(
        src_ref=source,
        dst_ref=target,
        send_sem=send,
        recv_sem=recv,
        device_id=(z, r),
        device_id_type=MESH,
    )


def pack_kernel(tie, g1, s1, wq, bq, bv, wo, bo, g2, s2, wu, bu, wd, bd, f_out, q_out):
    width = wq.shape[1]
    unit = g1.shape[1]
    hidden = wu.shape[2]

    def turned(bank, index):
        return bank[tie[index]].astype(F32).T.astype(BF)

    f_out[0:hidden, :] = turned(wu, 9)
    f_out[hidden : 2 * hidden, :] = wd[tie[11]]
    f_out[2 * hidden : 2 * hidden + unit, :] = turned(wo, 5)
    q_out[...] = turned(wq, 2)
    f_out[2 * hidden + unit :, :] = jnp.zeros((SMALL, width), BF)
    base = 2 * hidden + unit
    banks = ((g1, 0), (s1, 1), (bq, 3), (bv, 4), (bo, 6), (g2, 7), (s2, 8), (bd, 12))
    rows = []
    for bank, index in banks:
        both = bank[...].astype(F32)
        chosen = jnp.zeros((1, unit), F32)
        for layer in range(bank.shape[0]):
            chosen = jnp.where(tie[index] == layer, both[layer : layer + 1, :], chosen)
        rows.append(chosen)
    f_out[base : base + SMALL, 0:unit] = jnp.concatenate(rows, axis=0).astype(BF)
    both = bu[...].astype(F32)
    chosen = jnp.zeros((1, hidden), F32)
    for layer in range(bu.shape[0]):
        chosen = jnp.where(tie[10] == layer, both[layer : layer + 1, :], chosen)
    tall = jnp.concatenate([chosen, jnp.zeros((SMALL - 1, hidden), F32)], axis=0)
    f_out[base : base + SMALL, 128 : 128 + hidden] = tall.astype(BF)


def pack(tie_map, banks):
    width = banks[2].shape[1]
    unit = banks[0].shape[1]
    hidden = banks[9].shape[2]
    packed_rows = 2 * hidden + unit + SMALL
    return pl.pallas_call(
        pack_kernel,
        name="pack",
        out_shape=(shape((packed_rows, width), BF), shape((banks[2].shape[2], width), BF)),
        in_specs=[smem()] + [vmem()] * 13,
        out_specs=(vmem(), vmem()),
        compiler_params=params(),
    )(tie_map, *banks)


def gather_kernel(
    depth,
    pieces,
    q_in,
    f_in,
    x_in,
    q_all,
    f_all,
    x_all,
    zsend,
    zrecv,
    send1,
    recv1,
    send2,
    recv2,
    csend,
    crecv,
    xsend,
    xrecv,
    own_sem,
):
    here = Place(depth)
    z, r = here.z, here.r
    ins, alls = (q_in, f_in), (q_all, f_all)
    greet(here, True, True)

    def move(p, zz, rr, own, send, recv, to_z, to_r):
        which, start, rows, _ = pieces[p]
        target = alls[which].at[here.slot(zz, rr), pl.ds(start, rows)]
        source = ins[which].at[pl.ds(start, rows)] if own else target
        return remote(source, target, send, recv, to_z, to_r)

    def first(p):
        return here.by_b if pieces[p][3] == "b" else here.by_a

    def second(p):
        return here.by_a if pieces[p][3] == "b" else here.by_b

    count = len(pieces)
    every = range(count)

    for k in range(1, 8):
        to = (r + k) % 8
        remote(x_in.at[to % 2], x_all.at[r], xsend.at[to], xrecv.at[r], z, to).start()
    own_x = pltpu.make_async_copy(x_in.at[here.core], x_all.at[r], own_sem.at[0])
    own_x.start()
    own_q = pltpu.make_async_copy(q_in, q_all.at[here.slot(z, r)], own_sem.at[1])
    own_q.start()
    own_f = pltpu.make_async_copy(f_in, f_all.at[here.slot(z, r)], own_sem.at[2])
    own_f.start()

    def up(p, o, own=False):
        return move(p, o, r, own, zsend.at[p, o, 0], zrecv.at[p, o], z + 1, r)

    def down(p, o, own=False):
        return move(p, o, r, own, zsend.at[p, o, 1], zrecv.at[p, o], z - 1, r)

    def one(p, o, own=False):
        return move(p, o, r, own, send1.at[p, o], recv1.at[p, o], z, first(p))

    def two(p, o, rr, lane, own=False):
        return move(p, o, rr, own, send2.at[p, o, lane], recv2.at[p, o, lane], z, second(p))

    def across(p, o, rr, lane, own=False):
        return move(p, o, rr, own, csend.at[p, o, lane], crecv.at[p, o, lane], z, here.mate)

    for p in every:

        @pl.when(z + 1 < depth)
        def _():
            up(p, z, True).start()

        @pl.when(z > 0)
        def _():
            down(p, z, True).start()

        one(p, z, True).start()
        two(p, z, r, 0, True).start()
        across(p, z, r, 0, True).start()

    def spread_first(o):
        for p in every:
            one(p, o).wait_recv()
            two(p, o, first(p), 1).start()
            across(p, o, first(p), 1).start()

    def spread_line(o, below):
        for p in every:
            up(p, o).wait_recv()
            if below:

                @pl.when(z + 1 < depth)
                def _():
                    up(p, o).start()

            else:

                @pl.when(z > 0)
                def _():
                    down(p, o).start()

            one(p, o).start()
            two(p, o, r, 0).start()
            across(p, o, r, 0).start()

    def both_ways(distance, act):
        @pl.when(z - distance >= 0)
        def _():
            act(z - distance, True)

        @pl.when(z + distance < depth)
        def _():
            act(z + distance, False)

    for distance in range(1, depth):
        both_ways(distance, spread_line)
        if distance == 1:
            spread_first(z)
        else:
            both_ways(distance - 1, lambda o, below: spread_first(o))
    both_ways(depth - 1, lambda o, below: spread_first(o))

    def spread_second(o):
        for p in every:
            two(p, o, second(p), 0).wait_recv()
            across(p, o, second(p), 2).start()
            two(p, o, here.both, 1).wait_recv()
            across(p, o, here.both, 3).start()

    spread_second(z)
    for distance in range(1, depth):
        both_ways(distance, lambda o, below: spread_second(o))

    mates = lambda p: (here.mate,)
    for o in range(depth):
        for p in every:
            for lane in range(4):
                across(p, o, r, lane).wait_recv()
    for k in range(1, 8):
        frm = (r + k) % 8
        remote(x_in.at[0], x_all.at[frm], xsend.at[frm], xrecv.at[frm], z, frm).wait()
    own_x.wait()
    own_q.wait()
    own_f.wait()
    for p in every:
        for o in range(depth):
            one(p, o).wait_send()
            for lane in range(2):
                two(p, o, r, lane).wait_send()
            for lane in range(4):
                across(p, o, r, lane).wait_send()

            @pl.when((o <= z) & (z + 1 < depth))
            def _():
                up(p, o).wait_send()

            @pl.when((o >= z) & (z > 0))
            def _():
                down(p, o).wait_send()


def gather(depth, q_own, f_own, rows):
    q_rows, width = q_own.shape
    f_rows = f_own.shape[0]
    q_cut = (q_rows // 2 + 7) // 8 * 8
    f_cut = (f_rows // 2 + 7) // 8 * 8
    pieces = (
        (0, 0, q_cut, "b"),
        (0, q_cut, q_rows - q_cut, "a"),
        (1, 0, f_cut, "b"),
        (1, f_cut, f_rows - f_cut, "a"),
    )
    n = len(pieces)
    dma = pltpu.SemaphoreType.DMA
    total = depth * 8
    return pl.pallas_call(
        functools.partial(gather_kernel, depth, pieces),
        name="gather",
        out_shape=(
            shape((total, q_rows, width), BF),
            shape((total, f_rows, width), BF),
            shape((8,) + rows.shape[1:], BF),
        ),
        in_specs=[anywhere()] * 3,
        out_specs=(anywhere(),) * 3,
        scratch_shapes=[
            dma((n, depth, 2)),
            dma((n, depth)),
            dma((n, depth)),
            dma((n, depth)),
            dma((n, depth, 2)),
            dma((n, depth, 2)),
            dma((n, depth, 4)),
            dma((n, depth, 4)),
            dma((8,)),
            dma((8,)),
            dma((3,)),
        ],
        compiler_params=params(1),
    )(q_own, f_own, rows)


def exchange_kernel(depth, block, out, send, recv, own):
    here = Place(depth)
    z, r = here.z, here.r
    greet(here, True, False)
    mine = pltpu.make_async_copy(block.at[r], out.at[r], own)
    mine.start()
    for k in range(1, 8):
        to = (r + k) % 8
        remote(block.at[to], out.at[r], send.at[to], recv.at[r], z, to).start()
    for k in range(1, 8):
        frm = (r + k) % 8
        remote(block.at[frm], out.at[frm], send.at[frm], recv.at[frm], z, frm).wait()
    mine.wait()


def exchange(depth, blocks, collective_id):
    dma = pltpu.SemaphoreType.DMA
    return pl.pallas_call(
        functools.partial(exchange_kernel, depth),
        name="exchange",
        out_shape=shape(blocks.shape, blocks.dtype),
        in_specs=[vmem()],
        out_specs=vmem(),
        scratch_shapes=[dma((8,)), dma((8,)), dma],
        compiler_params=params(collective_id),
    )(blocks)


def spread_units(small, width, hidden_total):
    devices = small.shape[0]
    unit = width // devices
    per = hidden_total // devices
    flat = small.reshape(devices * SMALL, width)
    lane = iota((128, width), 1)
    pick = (lane % unit == iota((128, width), 0)).astype(F32).astype(BF)
    tall = nn(flat[:, 0:128], pick)
    row = iota((devices * SMALL, width), 0)
    col = iota((devices * SMALL, width), 1)
    tall = jnp.where(col // unit == row // SMALL, tall, 0.0)
    vectors = jnp.sum(tall.reshape(devices, SMALL, width), axis=0)
    chosen = (
        iota((devices, devices * SMALL), 1) == iota((devices, devices * SMALL), 0) * SMALL
    ).astype(F32).astype(BF)
    firsts = nn(chosen, flat[:, 128:256]).astype(BF)
    lane = iota((128, hidden_total), 1)
    pick = (lane % per == iota((128, hidden_total), 0)).astype(F32).astype(BF)
    wide = nn(firsts, pick)
    keep = iota((devices, hidden_total), 1) // per == iota((devices, hidden_total), 0)
    return vectors, jnp.sum(jnp.where(keep, wide, 0.0), axis=0, keepdims=True)


def gather_units(vectors, hidden_row, devices):
    width = vectors.shape[1]
    hidden_total = hidden_row.shape[1]
    unit = width // devices
    per = hidden_total // devices
    tall = jnp.broadcast_to(vectors[None], (devices, SMALL, width)).reshape(devices * SMALL, width)
    row = iota((devices * SMALL, width), 0)
    col = iota((devices * SMALL, width), 1)
    tall = jnp.where(col // unit == row // SMALL, tall, 0.0).astype(BF)
    pick = (iota((width, 128), 0) % unit == iota((width, 128), 1)).astype(F32).astype(BF)
    left = nn(tall, pick)
    wide = jnp.broadcast_to(hidden_row, (devices, hidden_total))
    keep = iota((devices, hidden_total), 1) // per == iota((devices, hidden_total), 0)
    wide = jnp.where(keep, wide, 0.0).astype(BF)
    pick = (iota((hidden_total, 128), 0) % per == iota((hidden_total, 128), 1)).astype(F32)
    firsts = nn(wide, pick.astype(BF)).astype(BF)
    chosen = (
        iota((devices * SMALL, devices), 0) == iota((devices * SMALL, devices), 1) * SMALL
    ).astype(F32).astype(BF)
    right = nn(chosen, firsts)
    return (
        left.astype(BF).reshape(devices, SMALL, 128),
        right.astype(BF).reshape(devices, SMALL, 128),
    )


def group_slice(row, j, groups):
    width = row.shape[1] // groups
    out = jnp.zeros((1, width), F32)
    for g in range(groups):
        out = jnp.where(j == g, row[:, g * width : (g + 1) * width], out)
    return out


def group_spread(part, j, groups):
    return jnp.concatenate([jnp.where(j == g, part, 0.0) for g in range(groups)], axis=1)


def block_at(place_ref, micro, position, blocks):
    found = jnp.int32(0)
    for s in range(blocks):
        found = jnp.where(place_ref[0, micro, s] == position, s, found)
    return found


def stack_heads(rows, heads):
    lane = iota(rows.shape, 1) // HD
    zero = jnp.zeros_like(rows)
    return jnp.concatenate([jnp.where(lane == h, rows, zero) for h in range(heads)], axis=0)


def unstack_heads(tall, heads):
    rows = tall.shape[0] // heads
    lane = iota((rows, tall.shape[1]), 1) // HD
    out = tall[0:rows]
    for h in range(1, heads):
        out = jnp.where(lane == h, tall[h * rows : (h + 1) * rows], out)
    return out


def visible_bias(lens, micro, start, rows, key_start, keys):
    query = start + iota((rows, 1), 0)
    begin = jnp.zeros((rows, 1), jnp.int32)
    end = jnp.int32(0)
    for s in range(lens.shape[2]):
        end = end + lens[0, micro, s]
        begin = jnp.where(query >= end, end, begin)
    key = key_start + iota((rows, keys), 1)
    return jnp.where((key >= begin) & (key <= query), 0.0, masked_score)


def row_norm(wide):
    average = jnp.mean(wide, axis=-1, keepdims=True)
    centered = wide - average
    variance = jnp.mean(centered * centered, axis=-1, keepdims=True)
    scale = lax.rsqrt(variance + epsilon)
    return centered * scale, scale


def norm_back(grad, unit, scale):
    first = jnp.mean(grad, axis=-1, keepdims=True)
    second = jnp.mean(grad * unit, axis=-1, keepdims=True)
    return (grad - first - unit * second) * scale


QROWS = 128
KCOLS = 384


def forward_kernel(
    depth,
    lens,
    spans,
    x_all,
    small,
    q_all,
    ao,
    q_out,
    k_out,
    v_out,
    h_out,
    u_out,
    o_out,
    lse_out,
    vec_out,
    hid_out,
    weights,
    sems,
):
    here = Place(depth)
    micro = here.core
    blocks, rows, width = x_all.shape
    group = weights.shape[1]
    groups = width // group
    heads = group // HD
    fetches = []
    for t in range(3):
        fetch = pltpu.make_async_copy(
            q_all.at[pl.ds(t * width + here.j * group, group)], weights.at[t], sems.at[t]
        )
        fetch.start()
        fetches.append(fetch)
    vectors, hidden = spread_units(small[...], width, hid_out.shape[1])
    vec_out[...] = vectors
    hid_out[...] = hidden
    gain, shift = vectors[0:1], vectors[1:2]
    query_add = group_slice(vectors[2:3], here.j, groups)
    value_add = group_slice(vectors[3:4], here.j, groups)
    for fetch in fetches:
        fetch.wait()

    def project(p, carry):
        source = block_at(spans, micro, p, blocks)
        unit, scale = row_norm(x_all[source].astype(F32))
        h = (unit * gain + shift).astype(BF)
        at = pl.ds(pl.multiple_of(p * rows, 16), rows)
        u_out[at, :] = unit.astype(BF)
        h_out[at, :] = h
        q_out[at, :] = (nt(h, weights[0]) + query_add).astype(BF)
        k_out[at, :] = nt(h, weights[1]).astype(BF)
        v_out[at, :] = (nt(h, weights[2]) + value_add).astype(BF)
        return carry

    lax.fori_loop(0, blocks, project, 0)

    def attend(i, carry):
        start = pl.multiple_of(i * QROWS, QROWS)
        stacked = stack_heads(q_out[pl.ds(start, QROWS), :] * BF(score_scale), heads)

        def step(kc, state):
            top, total, acc = state
            at = pl.ds(pl.multiple_of(kc * KCOLS, KCOLS), KCOLS)
            bias = visible_bias(lens, micro, start, QROWS, kc * KCOLS, KCOLS)
            scores = nt(stacked, k_out[at, :])
            scores = (scores.reshape(heads, QROWS, KCOLS) + bias[None]).reshape(
                heads * QROWS, KCOLS
            )
            new_top = jnp.maximum(top, jnp.max(scores, axis=1, keepdims=True))
            probs = jnp.exp(scores - new_top)
            factor = jnp.exp(top - new_top)
            total = total * factor + jnp.sum(probs, axis=1, keepdims=True)
            acc = acc * factor + nn(probs.astype(BF), v_out[at, :])
            return new_top, total, acc

        tall = heads * QROWS
        top, total, acc = lax.fori_loop(
            0,
            (i * QROWS) // KCOLS + 1,
            step,
            (
                jnp.full((tall, 1), masked_score, F32),
                jnp.zeros((tall, 1), F32),
                jnp.zeros((tall, group), F32),
            ),
        )
        o_out[pl.ds(start, QROWS), :] = unstack_heads(acc / total, heads)
        lse_out[i] = top + jnp.log(total)
        return carry

    lax.fori_loop(0, blocks * rows // QROWS, attend, 0)
    for s in range(blocks):
        at = pl.ds(pl.multiple_of(spans[0, micro, s] * rows, 16), rows)
        ao[s] = o_out[at, :].astype(BF)


def attend_forward(depth, lens, spans, x_all, q_all, f_all, hidden_total):
    blocks, rows, width = x_all.shape
    total = depth * 8
    group = width // 4
    pack_rows = blocks * rows
    small_at = f_all.shape[1] // SMALL - 1
    whole = lambda *dims: pl.BlockSpec(dims, lambda i: (0,) * len(dims))
    heads = group // HD
    outs = (
        shape((blocks, rows, group), BF),
        shape((pack_rows, group), BF),
        shape((pack_rows, group), BF),
        shape((pack_rows, group), BF),
        shape((pack_rows, width), BF),
        shape((pack_rows, width), BF),
        shape((pack_rows, group), F32),
        shape((pack_rows // QROWS, heads * QROWS, 1), F32),
        shape((SMALL, width), F32),
        shape((1, hidden_total), F32),
    )
    return pl.pallas_call(
        functools.partial(forward_kernel, depth),
        name="attend_forward",
        grid=(1,),
        out_shape=outs,
        in_specs=[
            smem(),
            smem(),
            whole(blocks, rows, width),
            pl.BlockSpec((total, SMALL, width), lambda i: (0, small_at, 0)),
            anywhere(),
        ],
        out_specs=tuple(whole(*o.shape) for o in outs),
        scratch_shapes=[pltpu.VMEM((3, group, width), BF), pltpu.SemaphoreType.DMA((3,))],
        compiler_params=params(),
    )(lens, spans, x_all, f_all, q_all.reshape(-1, width))


def middle_kernel(
    x_ref,
    dy_ref,
    at_ref,
    wo_ref,
    up_ref,
    down_ref,
    vec_ref,
    hid_ref,
    y_out,
    da_out,
    dr_out,
    grad_out,
    go_out,
    vec_out,
    hid_out,
    attn,
    resid,
    unit2,
    h2,
    scale2,
    y_acc,
    dh_acc,
):
    i = pl.program_id(0)
    last = pl.num_programs(0) - 1
    micros, rows, width = x_ref.shape
    group = at_ref.shape[2]
    devices, per = up_ref.shape[0], up_ref.shape[1]
    chunk = devices * per
    all_rows = micros * rows
    g_down = dy_ref[...].reshape(all_rows, width)

    @pl.when(i == 0)
    def _():
        for m in range(micros):
            pieces = [at_ref[2 * j + m] for j in range(width // group)]
            attn[m * rows : (m + 1) * rows, :] = jnp.concatenate(pieces, axis=1)
        wo = wo_ref[...].reshape(width, width)
        wide = x_ref[...].reshape(all_rows, width).astype(F32)
        res = wide + nt(attn[...], wo) + vec_ref[4:5, :]
        resid[...] = res
        unit, scale = row_norm(res)
        unit2[...] = unit
        scale2[...] = scale
        h2[...] = (unit * vec_ref[5:6, :] + vec_ref[6:7, :]).astype(BF)
        y_acc[...] = jnp.zeros_like(y_acc)
        dh_acc[...] = jnp.zeros_like(dh_acc)

    up_w = up_ref[...].reshape(chunk, width)
    down_w = down_ref[...].reshape(chunk, width)
    up = nt(h2[...], up_w) + hid_ref[...]
    square = up * up
    tanh = jnp.tanh(GELU_A * (up + GELU_B * square * up))
    half = 0.5 * (1.0 + tanh)
    act = (up * half).astype(BF)
    y_acc[...] += nn(act, down_w)
    slope = half + 0.5 * up * (1.0 - tanh * tanh) * (GELU_A * (1.0 + 3.0 * GELU_B * square))
    d_up32 = nt(g_down, down_w) * slope
    d_up = d_up32.astype(BF)
    hid_out[...] = jnp.sum(d_up.astype(F32), axis=0, keepdims=True)
    dh_acc[...] += nn(d_up, up_w)
    grad_out[:, 0:per, :] = tn(d_up, h2[...]).astype(BF).reshape(devices, per, width)
    grad_out[:, per : 2 * per, :] = tn(act, g_down).astype(BF).reshape(devices, per, width)

    @pl.when(i == last)
    def _():
        dy = g_down.astype(F32)
        y = resid[...] + (y_acc[...] + vec_ref[7:8, :])
        y_out[...] = y.astype(BF).reshape(micros, rows, width)
        d_h2 = dh_acc[...]
        unit = unit2[...]
        d_res = dy + norm_back(d_h2 * vec_ref[5:6, :], unit, scale2[...])
        dr_out[...] = d_res.reshape(micros, rows, width)
        g_mix = d_res.astype(BF)
        wo = wo_ref[...].reshape(width, width)
        d_attn = nn(g_mix, wo).astype(BF)
        for m in range(micros):
            for j in range(width // group):
                da_out[2 * j + m] = d_attn[m * rows : (m + 1) * rows, j * group : (j + 1) * group]
        go_out[...] = tn(g_mix, attn[...]).astype(BF).reshape(go_out.shape)
        zero = jnp.zeros((1, width), F32)
        vec_out[...] = jnp.concatenate(
            [
                zero,
                zero,
                zero,
                zero,
                jnp.sum(g_mix.astype(F32), axis=0, keepdims=True),
                jnp.sum(d_h2 * unit, axis=0, keepdims=True),
                jnp.sum(d_h2, axis=0, keepdims=True),
                jnp.sum(dy, axis=0, keepdims=True),
            ],
            axis=0,
        )


GELU_A = math.sqrt(2.0 / math.pi)
GELU_B = 0.044715
MIDDLE_DEVICES = 4


def middle(x_own, dy_own, at_recv, f_all, vectors, hidden):
    micros, rows, width = x_own.shape
    total, f_rows, _ = f_all.shape
    hidden_total = hidden.shape[1]
    per = hidden_total // total
    unit = width // total
    chunk = MIDDLE_DEVICES * per
    whole = lambda *dims: pl.BlockSpec(dims, lambda i: (0,) * len(dims))
    all_rows = micros * rows
    outs = (
        shape((micros, rows, width), BF),
        shape(at_recv.shape, BF),
        shape((micros, rows, width), F32),
        shape((total, 2 * per, width), BF),
        shape((total, unit, width), BF),
        shape((SMALL, width), F32),
        shape((1, hidden_total), F32),
    )
    return pl.pallas_call(
        middle_kernel,
        name="middle",
        grid=(total // MIDDLE_DEVICES,),
        out_shape=outs,
        in_specs=[
            whole(micros, rows, width),
            whole(micros, rows, width),
            whole(*at_recv.shape),
            pl.BlockSpec((total, unit, width), lambda i: (0, 2 * per // unit, 0)),
            pl.BlockSpec((MIDDLE_DEVICES, per, width), lambda i: (i, 0, 0)),
            pl.BlockSpec((MIDDLE_DEVICES, per, width), lambda i: (i, 1, 0)),
            whole(SMALL, width),
            pl.BlockSpec((1, chunk), lambda i: (0, i)),
        ],
        out_specs=(
            whole(micros, rows, width),
            whole(*at_recv.shape),
            whole(micros, rows, width),
            pl.BlockSpec((MIDDLE_DEVICES, 2 * per, width), lambda i: (i, 0, 0)),
            whole(total, unit, width),
            whole(SMALL, width),
            pl.BlockSpec((1, chunk), lambda i: (0, i)),
        ),
        scratch_shapes=[
            pltpu.VMEM((all_rows, width), BF),
            pltpu.VMEM((all_rows, width), F32),
            pltpu.VMEM((all_rows, width), F32),
            pltpu.VMEM((all_rows, width), BF),
            pltpu.VMEM((all_rows, 1), F32),
            pltpu.VMEM((all_rows, width), F32),
            pltpu.VMEM((all_rows, width), F32),
        ],
        compiler_params=params(),
    )(x_own, dy_own, at_recv, f_all, f_all, f_all, vectors, hidden)


def backward_kernel(
    depth,
    lens,
    spans,
    da_ref,
    q_ref,
    k_ref,
    v_ref,
    h_ref,
    u_ref,
    o_ref,
    lse_ref,
    vec_ref,
    hid_ref,
    q_all,
    gq_out,
    dh_out,
    small_out,
    weights,
    da,
    dq_acc,
    dk_acc,
    dv_acc,
    dq,
    dk,
    dv,
    sums,
    sems,
):
    here = Place(depth)
    micro = here.core
    blocks, rows, group = da_ref.shape
    width = h_ref.shape[1]
    groups = width // group
    heads = group // HD
    pack_rows = blocks * rows
    fetches = []
    for t in range(3):
        fetch = pltpu.make_async_copy(
            q_all.at[pl.ds(t * width + here.j * group, group)], weights.at[t], sems.at[t]
        )
        fetch.start()
        fetches.append(fetch)
    for p in range(blocks):
        da[p * rows : (p + 1) * rows, :] = da_ref[block_at(spans, micro, p, blocks)]
    dk_acc[...] = jnp.zeros_like(dk_acc)
    dv_acc[...] = jnp.zeros_like(dv_acc)

    def query_block(i, carry):
        start = pl.multiple_of(i * QROWS, QROWS)
        at_q = pl.ds(start, QROWS)
        stacked = stack_heads(q_ref[at_q, :] * BF(score_scale), heads)
        d_rows = da[at_q, :]
        d_stacked = stack_heads(d_rows, heads)
        product = d_rows.astype(F32) * o_ref[at_q, :]
        delta = jnp.sum(stack_heads(product, heads), axis=1, keepdims=True)
        lse = lse_ref[i]

        def step(kc, acc):
            at = pl.ds(pl.multiple_of(kc * KCOLS, KCOLS), KCOLS)
            bias = visible_bias(lens, micro, start, QROWS, kc * KCOLS, KCOLS)
            keys = k_ref[at, :]
            scores = nt(stacked, keys)
            scores = (scores.reshape(heads, QROWS, KCOLS) + bias[None]).reshape(
                heads * QROWS, KCOLS
            )
            probs = jnp.exp(scores - lse)
            d_probs = nt(d_stacked, v_ref[at, :])
            d_scores = (probs * (d_probs - delta)).astype(BF)
            dk_acc[at, :] += tn(d_scores, stacked)
            dv_acc[at, :] += tn(probs.astype(BF), d_stacked)
            return acc + nn(d_scores, keys)

        acc = lax.fori_loop(
            0, (i * QROWS) // KCOLS + 1, step, jnp.zeros((heads * QROWS, group), F32)
        )
        dq_acc[at_q, :] = unstack_heads(acc, heads) * score_scale
        return carry

    lax.fori_loop(0, pack_rows // QROWS, query_block, 0)
    dq[...] = dq_acc[...].astype(BF)
    dk[...] = dk_acc[...].astype(BF)
    dv[...] = dv_acc[...].astype(BF)
    for t, part in enumerate((dq, dk, dv)):
        gq_out[t] = tn(part[...], h_ref[...]).astype(BF).reshape(gq_out.shape[1:])
    query_bias = jnp.sum(dq[...].astype(F32), axis=0, keepdims=True)
    value_bias = jnp.sum(dv[...].astype(F32), axis=0, keepdims=True)
    for fetch in fetches:
        fetch.wait()
    sums[...] = jnp.zeros_like(sums)

    def unsort(s, carry):
        at = pl.ds(pl.multiple_of(spans[0, micro, s] * rows, 16), rows)
        part = (
            nn(dq[at, :], weights[0]) + nn(dk[at, :], weights[1]) + nn(dv[at, :], weights[2])
        )
        dh_out[s] = part.astype(BF)
        sums[0:1, :] += jnp.sum(part * u_ref[at, :].astype(F32), axis=0, keepdims=True)
        sums[1:2, :] += jnp.sum(part, axis=0, keepdims=True)
        return carry

    lax.fori_loop(0, blocks, unsort, 0)
    vectors = jnp.concatenate(
        [
            sums[0:2, :],
            group_spread(query_bias, here.j, groups),
            group_spread(value_bias, here.j, groups),
            vec_ref[4:8, :],
        ],
        axis=0,
    )
    left, right = gather_units(vectors, hid_ref[...], depth * 8)
    small_out[...] = jnp.zeros_like(small_out)
    small_out[:, :, 0:128] = left
    small_out[:, :, 128:256] = right


def attend_backward(depth, lens, spans, da_recv, saved, vec_grads, hid_grads, q_all):
    q, k, v, h, u, o, lse = saved
    blocks, rows, group = da_recv.shape
    pack_rows, width = h.shape
    total = depth * 8
    unit = width // total
    wide = lambda dtype: pltpu.VMEM((pack_rows, group), dtype)
    return pl.pallas_call(
        functools.partial(backward_kernel, depth),
        name="attend_backward",
        out_shape=(
            shape((3, group // unit, unit, width), BF),
            shape((blocks, rows, width), BF),
            shape((total, SMALL, width), BF),
        ),
        in_specs=[smem(), smem()] + [vmem()] * 10 + [anywhere()],
        out_specs=(vmem(),) * 3,
        scratch_shapes=[
            pltpu.VMEM((3, group, width), BF),
            wide(BF),
            wide(F32),
            wide(F32),
            wide(F32),
            wide(BF),
            wide(BF),
            wide(BF),
            pltpu.VMEM((SMALL, width), F32),
            pltpu.SemaphoreType.DMA((3,)),
        ],
        compiler_params=params(),
    )(lens, spans, da_recv, q, k, v, h, u, o, lse, vec_grads, hid_grads, q_all.reshape(-1, width))


def reduce_kernel(
    depth,
    grad_ref,
    out_ref,
    small_ref,
    gq_ref,
    dh_ref,
    f_sum,
    q_sum,
    dh_sum,
    held,
    from_mate,
    from_one,
    from_two,
    from_below,
    from_above,
    q_held,
    q_mate,
    q_line,
    dh_recv,
    load_sem,
    csend,
    crecv,
    send1,
    recv1,
    send2,
    recv2,
    zsend,
    zrecv_up,
    zrecv_down,
    qc_sem,
    q_send,
    q_recv,
    dh_send,
    dh_recv_sem,
):
    here = Place(depth)
    z, r = here.z, here.r
    a, b, core, j = here.a, here.b, here.core, here.j
    half = held.shape[4]
    width = held.shape[5]
    per = grad_ref.shape[4] // 2
    unit = out_ref.shape[4]
    greet_all(here)

    spans = (
        ((grad_ref, 0, per, 0), (out_ref, 0, half - per, per)),
        (
            (grad_ref, per, per, 0),
            (out_ref, half - per, unit - (half - per), per),
            (small_ref, 0, SMALL, per + unit - (half - per)),
        ),
    )

    def order(k):
        out = jnp.int32(0)
        for zz in range(depth):
            line = sorted(range(depth), key=lambda t: (-abs(t - zz), t))
            out = jnp.where(z == zz, line[k], out)
        return out

    def pieces(p, t, which, target):
        for n, (ref, start, rows, at) in enumerate(spans[p]):
            yield n, ref.at[t, :, :, which, pl.ds(start, rows)], target.at[
                p, t, :, :, pl.ds(at, rows)
            ]

    for k in range(depth):
        t = order(k)
        for p in range(2):
            for n, source, target in pieces(p, t, 1 - core, from_mate):
                remote(source, target, csend.at[p, t, n], crecv.at[p, t, n], z, here.mate).start()
            for n, source, target in pieces(p, t, core, held):
                pltpu.make_async_copy(source, target, load_sem.at[p, t, n]).start()

    for k in range(1, 8):
        to = (r + k) % 8
        remote(
            dh_ref.at[to], dh_recv.at[r], dh_send.at[to], dh_recv_sem.at[r], z, to
        ).start()
    own_dh = pltpu.make_async_copy(dh_ref.at[r], dh_recv.at[r], dh_send.at[r])
    own_dh.start()

    to_mate = remote(
        gq_ref.at[:, :, 1 - core], q_mate, qc_sem.at[0], qc_sem.at[1], z, here.mate
    )
    to_mate.start()
    keep = pltpu.make_async_copy(gq_ref.at[:, :, core], q_held, qc_sem.at[2])
    keep.start()
    keep.wait()
    to_mate.wait_recv()
    kinds, pairs = q_held.shape[0], q_held.shape[1]
    for kind in range(kinds):
        for m in range(pairs):
            q_held[kind, m] = (
                q_held[kind, m].astype(F32) + q_mate[kind, m].astype(F32)
            ).astype(BF)

    units_each = 3
    per_kind = depth * 8 * units_each // kinds

    def q_route(kind, m):
        block = kind * per_kind + j * (pairs * 2) + m * 2 + core
        owner = block // units_each
        return owner // 8, owner % 8, block % units_each

    def q_moves(act_remote, act_local):
        for kind in range(kinds):
            for m in range(pairs):
                oz, orr, at = q_route(kind, m)
                mine = (oz == z) & (orr == r)

                @pl.when(jnp.logical_not(mine))
                def _():
                    act_remote(
                        remote(
                            q_held.at[kind, m],
                            q_line.at[at, z],
                            q_send.at[kind, m],
                            q_recv.at[at, z],
                            oz,
                            orr,
                        )
                    )

                @pl.when(mine)
                def _():
                    act_local(
                        pltpu.make_async_copy(
                            q_held.at[kind, m], q_line.at[at, z], q_send.at[kind, m]
                        )
                    )

    q_moves(lambda c: c.start(), lambda c: c.start())

    def add(target, source):
        target[...] = (target[...].astype(F32) + source[...].astype(F32)).astype(BF)

    def add_blocks(pairs_of_refs):
        for target, source in pairs_of_refs:
            add(target, source)

    def stage_mate(t):
        for p in range(2):
            for n, source, target in pieces(p, t, core, held):
                pltpu.make_async_copy(source, target, load_sem.at[p, t, n]).wait()
            for n, source, target in pieces(p, t, 1 - core, from_mate):
                remote(
                    source, target, csend.at[p, t, n], crecv.at[p, t, n], z, here.mate
                ).wait_recv()
            for aa in range(2):
                for bb in range(2):
                    add(held.at[p, t, aa, bb], from_mate.at[p, t, aa, bb])
        first(0, t).start()
        first(1, t).start()

    def first(p, t):
        if p == 0:
            return remote(
                held.at[0, t, 1 - a], from_one.at[0, t], send1.at[0, t], recv1.at[0, t], z, here.by_a
            )
        return remote(
            held.at[1, t, :, 1 - b], from_one.at[1, t], send1.at[1, t], recv1.at[1, t], z, here.by_b
        )

    def second(p, t):
        if p == 0:
            return remote(
                held.at[0, t, a, 1 - b],
                from_two.at[0, t],
                send2.at[0, t],
                recv2.at[0, t],
                z,
                here.by_b,
            )
        return remote(
            held.at[1, t, 1 - a, b], from_two.at[1, t], send2.at[1, t], recv2.at[1, t], z, here.by_a
        )

    def stage_one(t):
        for p in range(2):
            first(p, t).wait_recv()
            for n in range(2):
                mine = held.at[0, t, a, n] if p == 0 else held.at[1, t, n, b]
                add(mine, from_one.at[p, t, n])
            second(p, t).start()

    def upward(p, t):
        return remote(
            held.at[p, t, a, b],
            from_below.at[p, t],
            zsend.at[p, t],
            zrecv_up.at[p, t],
            z + 1,
            r,
        )

    def downward(p, t):
        return remote(
            held.at[p, t, a, b],
            from_above.at[p, t],
            zsend.at[p, t],
            zrecv_down.at[p, t],
            z - 1,
            r,
        )

    def stage_two(t):
        for p in range(2):
            mine = held.at[p, t, a, b]
            second(p, t).wait_recv()
            add(mine, from_two.at[p, t])

            @pl.when((t >= z) & (z > 0))
            def _():
                upward(p, t).wait_recv()
                add(mine, from_below.at[p, t])

            @pl.when((t <= z) & (z < depth - 1))
            def _():
                downward(p, t).wait_recv()
                add(mine, from_above.at[p, t])

            @pl.when(t > z)
            def _():
                upward(p, t).start()

            @pl.when(t < z)
            def _():
                downward(p, t).start()

    for step in range(depth + 2):
        if step < depth:
            stage_mate(order(step))
        if 0 <= step - 1 < depth:
            stage_one(order(step - 1))
        if 0 <= step - 2 < depth:
            stage_two(order(step - 2))
    for p in range(2):
        f_sum[p] = held[p, z, a, b].astype(F32)

    own_dh.wait()
    for k in range(1, 8):
        frm = (r + k) % 8
        remote(
            dh_ref.at[frm], dh_recv.at[frm], dh_send.at[frm], dh_recv_sem.at[frm], z, frm
        ).wait()
    for m in range(2):
        part = dh_recv[m].astype(F32)
        for chip in range(1, 4):
            part = part + dh_recv[2 * chip + m].astype(F32)
        dh_sum[m] = part

    me = here.slot(z, r)
    for at in range(units_each):
        block = me * units_each + at
        inside = block % per_kind
        from_r = (inside // (pairs * 2)) * 2 + inside % 2
        for zz in range(depth):
            @pl.when(jnp.logical_not((from_r == r) & (zz == z)))
            def _():
                remote(
                    q_held.at[0, 0], q_line.at[at, zz], q_send.at[0, 0], q_recv.at[at, zz], zz, from_r
                ).wait_recv()
    q_moves(lambda c: c.wait_send(), lambda c: c.wait())
    for at in range(units_each):
        part = q_line[at, 0].astype(F32)
        for zz in range(1, depth):
            part = part + q_line[at, zz].astype(F32)
        q_sum[at] = part

    to_mate.wait_send()
    for t in range(depth):
        for p in range(2):
            for n, source, target in pieces(p, t, 1 - core, from_mate):
                remote(
                    source, target, csend.at[p, t, n], crecv.at[p, t, n], z, here.mate
                ).wait_send()
            first(p, t).wait_send()
            second(p, t).wait_send()

            @pl.when(z != t)
            def _():
                upward(p, t).wait_send()


def reduce(depth, grads, out_grads, small, gq, dh):
    total, two_per, width = grads.shape
    per = two_per // 2
    unit = out_grads.shape[1]
    half = (two_per + unit + SMALL) // 2
    kinds, units, _, _ = gq.shape
    rows = dh.shape[1]
    dma = pltpu.SemaphoreType.DMA
    line = lambda ref: ref.reshape((depth, 2, 2, 2) + ref.shape[1:])
    return pl.pallas_call(
        functools.partial(reduce_kernel, depth),
        name="reduce",
        out_shape=(
            shape((2, half, width), F32),
            shape((3, unit, width), F32),
            shape((2, rows, width), F32),
        ),
        in_specs=[anywhere()] * 5,
        out_specs=(vmem(),) * 3,
        scratch_shapes=[
            pltpu.VMEM((2, depth, 2, 2, half, width), BF),
            pltpu.VMEM((2, depth, 2, 2, half, width), BF),
            pltpu.VMEM((2, depth, 2, half, width), BF),
            pltpu.VMEM((2, depth, half, width), BF),
            pltpu.VMEM((2, depth, half, width), BF),
            pltpu.VMEM((2, depth, half, width), BF),
            pltpu.VMEM((kinds, units // 2, unit, width), BF),
            pltpu.VMEM((kinds, units // 2, unit, width), BF),
            pltpu.VMEM((3, depth, unit, width), BF),
            pltpu.VMEM((8, rows, width), BF),
            dma((2, depth, 3)),
            dma((2, depth, 3)),
            dma((2, depth, 3)),
            dma((2, depth)),
            dma((2, depth)),
            dma((2, depth)),
            dma((2, depth)),
            dma((2, depth)),
            dma((2, depth)),
            dma((2, depth)),
            dma((3,)),
            dma((kinds, units // 2)),
            dma((3, depth)),
            dma((8,)),
            dma((8,)),
        ],
        compiler_params=params(4),
    )(
        line(grads),
        line(out_grads),
        line(small),
        gq.reshape(kinds, units // 2, 2, unit, width),
        dh,
    )


def final_kernel(
    tie,
    x_ref,
    dh_ref,
    dr_ref,
    vec_ref,
    f_ref,
    q_ref,
    dx_out,
    g1,
    s1,
    wq,
    bq,
    bv,
    wo,
    bo,
    g2,
    s2,
    wu,
    bu,
    wd,
    bd,
):
    micros = x_ref.shape[0]
    for m in range(micros):
        unit, scale = row_norm(x_ref[m].astype(F32))
        back = norm_back(dh_ref[m] * vec_ref[0:1, :], unit, scale)
        dx_out[m] = (dr_ref[m] + back).astype(BF)
    layers = wq.shape[0]
    per = wu.shape[2]
    unit = wo.shape[2]
    half = f_ref.shape[1]
    width = wq.shape[1]

    def put(ref, index, value):
        for layer in range(layers):
            ref[layer] = jnp.where(tie[index] == layer, value, 0.0)

    put(wu, 9, f_ref[0, 0:per, :].T)
    put(wd, 11, f_ref[1, 0:per, :])
    split = half - per
    out_rows = jnp.concatenate(
        [f_ref[0, per:half, :], f_ref[1, per : per + unit - split, :]], axis=0
    )
    put(wo, 5, out_rows.T)
    put(wq, 2, q_ref[...].reshape(3 * unit, width).T)
    small = f_ref[1, per + unit - split :, :]
    names = ((g1, 0), (s1, 1), (bq, 3), (bv, 4), (bo, 6), (g2, 7), (s2, 8), (bd, 12))
    for n, (ref, index) in enumerate(names):
        for layer in range(layers):
            ref[layer : layer + 1, :] = jnp.where(
                tie[index] == layer, small[n : n + 1, 0:unit], 0.0
            )
    for layer in range(layers):
        bu[layer : layer + 1, :] = jnp.where(tie[10] == layer, small[0:1, 128 : 128 + per], 0.0)


def finish(tie_map, x_own, dh_sum, d_resid, vectors, f_sum, q_sum, banks):
    outs = (shape(x_own.shape, BF),) + tuple(shape(bank.shape, F32) for bank in banks)
    return pl.pallas_call(
        final_kernel,
        name="finish",
        out_shape=outs,
        in_specs=[smem()] + [vmem()] * 6,
        out_specs=(vmem(),) * len(outs),
        compiler_params=params(),
    )(tie_map, x_own, dh_sum, d_resid, vectors, f_sum, q_sum)


def grouped_plan(depth, *args):
    block_input, cotangent, tie_map, seq_lengths, span_place = args[:5]
    banks = args[5:]
    x_own, dy_own = block_input[0], cotangent[0]
    f_own, q_own = pack(tie_map, banks)
    q_all, f_all, x_all = gather(depth, q_own, f_own, x_own)
    hidden_total = banks[10].shape[1] * depth * 8
    ao, q, k, v, h, u, o, lse, vectors, hidden = attend_forward(
        depth, seq_lengths, span_place, x_all, q_all, f_all, hidden_total
    )
    at_recv = exchange(depth, ao, 2)
    y, da, d_resid, grads, out_grads, vec_grads, hid_grads = middle(
        x_own, dy_own, at_recv, f_all, vectors, hidden
    )
    da_recv = exchange(depth, da, 3)
    gq, dh, small = attend_backward(
        depth, seq_lengths, span_place, da_recv, (q, k, v, h, u, o, lse), vec_grads, hid_grads, q_all
    )
    f_sum, q_sum, dh_sum = reduce(depth, grads, out_grads, small, gq, dh)
    final = finish(tie_map, x_own, dh_sum, d_resid, vectors, f_sum, q_sum, banks)
    return (y[None], final[0][None]) + tuple(final[1:])
def fits_grouped(mesh, block_input, span_place, qkv_weight):
    width = qkv_weight.shape[1]
    rows = block_input.shape[2] // mesh.shape["ctx"]
    total = mesh.shape["ctx"] * mesh.shape["dp"]
    return (
        mesh.shape["ctx"] == 8
        and block_input.shape[1] == 2
        and HEADS % 4 == 0
        and HEADS * HD == width
        and rows % 16 == 0
        and block_input.shape[2] % KCOLS == 0
        and width % total == 0
        and (width // total) % 8 == 0
        and (width // 4) % (2 * (width // total)) == 0
    )


def solution(mesh):
    replicated_rows = P("dp", None, "ctx", None)
    vector = P(None, ("dp", "ctx"))
    columns = P(None, None, ("dp", "ctx"))
    bank_specs = (
        vector,
        vector,
        columns,
        vector,
        vector,
        columns,
        vector,
        vector,
        vector,
        columns,
        vector,
        P(None, ("dp", "ctx"), None),
        vector,
    )

    def step(*args):
        if fits_grouped(mesh, args[0], args[4], args[7]):
            plan = functools.partial(grouped_plan, mesh.shape["dp"])
        else:
            plan = general_plan
        return jax.shard_map(
            plan,
            mesh=mesh,
            in_specs=(
                replicated_rows,
                replicated_rows,
                P(),
                P("dp", None, None),
                P("dp", None, None),
            )
            + bank_specs,
            out_specs=(replicated_rows, replicated_rows) + bank_specs,
            check_vma=False,
        )(*args)

    return step
```

```python
import functools
import math
import types

import jax
import jax.numpy as jnp
from jax import lax
from jax.experimental import pallas as pl
from jax.experimental.pallas import tpu as pltpu
from jax.sharding import PartitionSpec as P

HEADS = 12
HD = 64


epsilon = 1e-05
masked_score = -1e30
score_scale = 0.125
key_block = 1024


def layer_norm(inputs, norm_gain, norm_shift):
    average = jnp.mean(inputs, axis=-1, keepdims=True)
    centered = inputs - average
    variance = jnp.mean(centered * centered, axis=-1, keepdims=True)
    return centered * lax.rsqrt(variance + epsilon) * norm_gain + norm_shift


def gelu_tanh(inputs):
    return jax.nn.gelu(inputs, approximate=True)


def stream_positions(row_index, span_row, rows_each):
    owner_lane = row_index // rows_each
    lane_ids = jnp.arange(span_row.shape[0], dtype=jnp.int32)
    span_ids = jnp.sum(
        jnp.where(owner_lane[:, None] == lane_ids[None, :], span_row[None, :], 0), axis=1
    )
    return span_ids * rows_each + row_index % rows_each


def segment_ids(positions, seq_ends):
    return jnp.sum((positions[:, None] >= seq_ends[None, :]).astype(jnp.int32), axis=1)


def over_blocks(step_fn, state, pieces):
    piece_rows = pieces[0].shape[0]
    block_rows = math.gcd(piece_rows, key_block)
    stacked = tuple(
        (
            member.reshape((piece_rows // block_rows, block_rows) + member.shape[1:])
            for member in pieces
        )
    )

    def inner_step(running, scan_item):
        block_index, sliced = scan_item
        return (step_fn(running, sliced, block_index * block_rows), None)

    finished, ignored = lax.scan(
        inner_step, state, (jnp.arange(piece_rows // block_rows, dtype=jnp.int32), stacked)
    )
    return finished


def score_probs(
    query_heads,
    grad_heads,
    lse_heads,
    delta_heads,
    query_pos,
    query_seg,
    key_heads,
    value_heads,
    key_pos,
    key_seg,
):
    allowed = (query_seg[:, None] == key_seg[None, :]) & (key_pos[None, :] <= query_pos[:, None])
    scores = (
        jnp.einsum("qhd,khd->hqk", query_heads, key_heads, preferred_element_type=jnp.float32)
        * score_scale
    )
    probs = jnp.where(allowed[None], jnp.exp(scores - lse_heads[:, :, None]), 0.0)
    dprobs = jnp.einsum("qhd,khd->hqk", grad_heads, value_heads, preferred_element_type=jnp.float32)
    dscores = (probs * (dprobs - delta_heads[:, :, None])).astype(jnp.bfloat16)
    return (probs.astype(jnp.bfloat16), dscores)


def general_plan(
    block_input,
    cotangent,
    tie_map,
    seq_lengths,
    span_place,
    first_gain,
    first_shift,
    qkv_weight,
    query_bias,
    value_bias,
    out_weight,
    out_bias,
    second_gain,
    second_shift,
    up_weight,
    up_bias,
    down_weight,
    down_bias,
):
    banks = (
        first_gain,
        first_shift,
        qkv_weight,
        query_bias,
        value_bias,
        out_weight,
        out_bias,
        second_gain,
        second_shift,
        up_weight,
        up_bias,
        down_weight,
        down_bias,
    )
    shards = tuple(
        (
            lax.dynamic_index_in_dim(weight_bank, tie_map[bank_number], 0, keepdims=False)
            for bank_number, weight_bank in enumerate(banks)
        )
    )
    micro_count = block_input.shape[1]
    row_count = block_input.shape[2]
    model_width = block_input.shape[3]
    ctx_index = lax.axis_index("ctx")
    local_rows = ctx_index * row_count + jnp.arange(row_count, dtype=jnp.int32)
    totals = None
    outputs = []
    input_grads = []
    for micro_step in range(micro_count):
        params = (
            lax.all_gather(shards[0], ("dp", "ctx"), axis=0, tiled=True),
            lax.all_gather(shards[1], ("dp", "ctx"), axis=0, tiled=True),
            lax.all_gather(shards[2], ("dp", "ctx"), axis=1, tiled=True),
            lax.all_gather(shards[3], ("dp", "ctx"), axis=0, tiled=True),
            lax.all_gather(shards[4], ("dp", "ctx"), axis=0, tiled=True),
            lax.all_gather(shards[5], ("dp", "ctx"), axis=1, tiled=True),
            lax.all_gather(shards[6], ("dp", "ctx"), axis=0, tiled=True),
            lax.all_gather(shards[7], ("dp", "ctx"), axis=0, tiled=True),
            lax.all_gather(shards[8], ("dp", "ctx"), axis=0, tiled=True),
            lax.all_gather(shards[9], ("dp", "ctx"), axis=1, tiled=True),
            lax.all_gather(shards[10], ("dp", "ctx"), axis=0, tiled=True),
            lax.all_gather(shards[11], ("dp", "ctx"), axis=0, tiled=True),
            lax.all_gather(shards[12], ("dp", "ctx"), axis=0, tiled=True),
        )
        (
            gain_before,
            shift_before,
            qkv_full,
            query_add,
            value_add,
            out_full,
            out_add,
            gain_after,
            shift_after,
            up_full,
            up_add,
            down_full,
            down_add,
        ) = params
        span_row = span_place[0, micro_step]
        seq_ends = jnp.cumsum(seq_lengths[0, micro_step])
        query_pos = stream_positions(local_rows, span_row, row_count)
        query_seg = segment_ids(query_pos, seq_ends)
        inputs_wide = block_input[0, micro_step].astype(jnp.float32)
        first_norm = layer_norm(
            inputs_wide, gain_before.astype(jnp.float32), shift_before.astype(jnp.float32)
        ).astype(jnp.bfloat16)
        projected = jnp.dot(first_norm, qkv_full, preferred_element_type=jnp.float32)
        queries = (projected[:, :model_width] + query_add.astype(jnp.float32)).astype(jnp.bfloat16)
        key_rows = projected[:, model_width : 2 * model_width].astype(jnp.bfloat16)
        value_rows = (projected[:, 2 * model_width :] + value_add.astype(jnp.float32)).astype(
            jnp.bfloat16
        )
        query_heads = queries.reshape(row_count, HEADS, HD)
        key_heads_own = key_rows.reshape(row_count, HEADS, HD)
        value_heads_own = value_rows.reshape(row_count, HEADS, HD)

        def attend(state, pieces, offset):
            row_max, row_sum, accumulated = state
            key_part, value_part = pieces
            piece_rows = key_part.shape[0]
            key_pos = stream_positions(
                offset + jnp.arange(piece_rows, dtype=jnp.int32), span_row, row_count
            )
            key_seg = segment_ids(key_pos, seq_ends)
            allowed = (query_seg[:, None] == key_seg[None, :]) & (
                key_pos[None, :] <= query_pos[:, None]
            )
            scores = (
                jnp.einsum(
                    "qhd,khd->hqk",
                    query_heads,
                    key_part.reshape(piece_rows, HEADS, HD),
                    preferred_element_type=jnp.float32,
                )
                * score_scale
            )
            scores = jnp.where(allowed[None], scores, masked_score)
            new_max = jnp.maximum(row_max, jnp.max(scores, axis=2))
            exp_scores = jnp.where(allowed[None], jnp.exp(scores - new_max[:, :, None]), 0.0)
            factor = jnp.exp(row_max - new_max)
            row_sum = row_sum * factor + jnp.sum(exp_scores, axis=2)
            accumulated = accumulated * factor.T[:, :, None] + jnp.einsum(
                "hqk,khd->qhd",
                exp_scores.astype(jnp.bfloat16),
                value_part.reshape(piece_rows, HEADS, HD),
                preferred_element_type=jnp.float32,
            )
            return (new_max, row_sum, accumulated)

        start_state = (
            jnp.full((HEADS, row_count), masked_score, jnp.float32),
            jnp.zeros((HEADS, row_count), jnp.float32),
            jnp.zeros((row_count, HEADS, HD), jnp.float32),
        )
        row_max, row_sum, accumulated = over_blocks(
            attend,
            start_state,
            (
                lax.all_gather(key_rows, "ctx", axis=0, tiled=True),
                lax.all_gather(value_rows, "ctx", axis=0, tiled=True),
            ),
        )
        attended_wide = accumulated / row_sum.T[:, :, None]
        log_sums = row_max + jnp.log(row_sum)
        attended = attended_wide.reshape(row_count, model_width).astype(jnp.bfloat16)
        mixed_out = jnp.dot(
            attended, out_full, preferred_element_type=jnp.float32
        ) + out_add.astype(jnp.float32)
        residual = inputs_wide + mixed_out
        second_norm = layer_norm(
            residual, gain_after.astype(jnp.float32), shift_after.astype(jnp.float32)
        ).astype(jnp.bfloat16)
        up_proj = jnp.dot(second_norm, up_full, preferred_element_type=jnp.float32) + up_add.astype(
            jnp.float32
        )
        activated = gelu_tanh(up_proj).astype(jnp.bfloat16)
        down_proj = jnp.dot(
            activated, down_full, preferred_element_type=jnp.float32
        ) + down_add.astype(jnp.float32)
        outputs.append((residual + down_proj).astype(jnp.bfloat16))
        params = (
            lax.all_gather(shards[0], ("dp", "ctx"), axis=0, tiled=True),
            lax.all_gather(shards[1], ("dp", "ctx"), axis=0, tiled=True),
            lax.all_gather(shards[2], ("dp", "ctx"), axis=1, tiled=True),
            lax.all_gather(shards[3], ("dp", "ctx"), axis=0, tiled=True),
            lax.all_gather(shards[4], ("dp", "ctx"), axis=0, tiled=True),
            lax.all_gather(shards[5], ("dp", "ctx"), axis=1, tiled=True),
            lax.all_gather(shards[6], ("dp", "ctx"), axis=0, tiled=True),
            lax.all_gather(shards[7], ("dp", "ctx"), axis=0, tiled=True),
            lax.all_gather(shards[8], ("dp", "ctx"), axis=0, tiled=True),
            lax.all_gather(shards[9], ("dp", "ctx"), axis=1, tiled=True),
            lax.all_gather(shards[10], ("dp", "ctx"), axis=0, tiled=True),
            lax.all_gather(shards[11], ("dp", "ctx"), axis=0, tiled=True),
            lax.all_gather(shards[12], ("dp", "ctx"), axis=0, tiled=True),
        )
        (
            gain_before,
            shift_before,
            qkv_full,
            query_add,
            value_add,
            out_full,
            out_add,
            gain_after,
            shift_after,
            up_full,
            up_add,
            down_full,
            down_add,
        ) = params
        grad_out = cotangent[0, micro_step].astype(jnp.float32)
        grad_down = grad_out.astype(jnp.bfloat16)
        down_weight_grad = jnp.einsum(
            "rf,rd->fd", activated, grad_down, preferred_element_type=jnp.float32
        )
        down_bias_grad = jnp.sum(grad_down.astype(jnp.float32), axis=0)
        grad_act = jnp.einsum("rd,fd->rf", grad_down, down_full, preferred_element_type=jnp.float32)
        unused_gelu, gelu_back = jax.vjp(gelu_tanh, up_proj)
        grad_up = gelu_back(grad_act)[0].astype(jnp.bfloat16)
        up_weight_grad = jnp.einsum(
            "rd,rf->df", second_norm, grad_up, preferred_element_type=jnp.float32
        )
        up_bias_grad = jnp.sum(grad_up.astype(jnp.float32), axis=0)
        grad_second = jnp.einsum("rf,df->rd", grad_up, up_full, preferred_element_type=jnp.float32)
        unused_second, second_back = jax.vjp(
            layer_norm, residual, gain_after.astype(jnp.float32), shift_after.astype(jnp.float32)
        )
        grad_resid, second_gain_grad, second_shift_grad = second_back(grad_second)
        grad_resid = grad_resid + grad_out
        grad_mixed = grad_resid.astype(jnp.bfloat16)
        out_weight_grad = jnp.einsum(
            "rc,rd->cd", attended, grad_mixed, preferred_element_type=jnp.float32
        )
        out_bias_grad = jnp.sum(grad_mixed.astype(jnp.float32), axis=0)
        grad_attended = jnp.einsum(
            "rd,cd->rc", grad_mixed, out_full, preferred_element_type=jnp.float32
        ).astype(jnp.bfloat16)
        grad_heads = grad_attended.reshape(row_count, HEADS, HD)
        delta_rows = jnp.sum(grad_heads.astype(jnp.float32) * attended_wide, axis=2)
        delta_heads = delta_rows.T
        empty_heads = jnp.zeros((row_count, HEADS, HD), jnp.float32)
        stats_whole = (
            lax.all_gather(log_sums.T, "ctx", axis=0, tiled=True),
            lax.all_gather(delta_rows, "ctx", axis=0, tiled=True),
        )

        def mutual(state, pieces, offset):
            grad_query, grad_key, grad_value = state
            key_part, value_part, query_part, gradout_part = pieces
            piece_rows = key_part.shape[0]
            lse_part = lax.dynamic_slice_in_dim(stats_whole[0], offset, piece_rows, 0)
            delta_part = lax.dynamic_slice_in_dim(stats_whole[1], offset, piece_rows, 0)
            key_pos = stream_positions(
                offset + jnp.arange(piece_rows, dtype=jnp.int32), span_row, row_count
            )
            key_seg = segment_ids(key_pos, seq_ends)
            key_part_heads = key_part.reshape(piece_rows, HEADS, HD)
            value_part_heads = value_part.reshape(piece_rows, HEADS, HD)
            query_part_heads = query_part.reshape(piece_rows, HEADS, HD)
            gradout_heads = gradout_part.reshape(piece_rows, HEADS, HD)
            probs, dscores = score_probs(
                query_heads,
                grad_heads,
                log_sums,
                delta_heads,
                query_pos,
                query_seg,
                key_part_heads,
                value_part_heads,
                key_pos,
                key_seg,
            )
            grad_query = grad_query + score_scale * jnp.einsum(
                "hqk,khd->qhd", dscores, key_part_heads, preferred_element_type=jnp.float32
            )
            probs_other, dscores_other = score_probs(
                query_part_heads,
                gradout_heads,
                lse_part.T,
                delta_part.T,
                key_pos,
                key_seg,
                key_heads_own,
                value_heads_own,
                query_pos,
                query_seg,
            )
            grad_key = grad_key + score_scale * jnp.einsum(
                "hqk,qhd->khd", dscores_other, query_part_heads, preferred_element_type=jnp.float32
            )
            grad_value = grad_value + jnp.einsum(
                "hqk,qhd->khd", probs_other, gradout_heads, preferred_element_type=jnp.float32
            )
            return (grad_query, grad_key, grad_value)

        grad_query, grad_key, grad_value = over_blocks(
            mutual,
            (empty_heads, empty_heads, empty_heads),
            (
                lax.all_gather(key_rows, "ctx", axis=0, tiled=True),
                lax.all_gather(value_rows, "ctx", axis=0, tiled=True),
                lax.all_gather(queries, "ctx", axis=0, tiled=True),
                lax.all_gather(grad_attended, "ctx", axis=0, tiled=True),
            ),
        )
        grad_proj = jnp.concatenate(
            [
                grad_query.reshape(row_count, model_width),
                grad_key.reshape(row_count, model_width),
                grad_value.reshape(row_count, model_width),
            ],
            axis=1,
        ).astype(jnp.bfloat16)
        qkv_weight_grad = jnp.einsum(
            "rc,rp->cp", first_norm, grad_proj, preferred_element_type=jnp.float32
        )
        query_bias_grad = jnp.sum(grad_proj[:, :model_width].astype(jnp.float32), axis=0)
        value_bias_grad = jnp.sum(grad_proj[:, 2 * model_width :].astype(jnp.float32), axis=0)
        grad_first = jnp.einsum(
            "rp,cp->rc", grad_proj, qkv_full, preferred_element_type=jnp.float32
        )
        unused_first, first_back = jax.vjp(
            layer_norm,
            inputs_wide,
            gain_before.astype(jnp.float32),
            shift_before.astype(jnp.float32),
        )
        grad_input, first_gain_grad, first_shift_grad = first_back(grad_first)
        input_grads.append((grad_input + grad_resid).astype(jnp.bfloat16))
        micro_grads = (
            first_gain_grad,
            first_shift_grad,
            qkv_weight_grad,
            query_bias_grad,
            value_bias_grad,
            out_weight_grad,
            out_bias_grad,
            second_gain_grad,
            second_shift_grad,
            up_weight_grad,
            up_bias_grad,
            down_weight_grad,
            down_bias_grad,
        )
        if totals is None:
            totals = micro_grads
        else:
            totals = tuple(
                (left_sum + right_sum for left_sum, right_sum in zip(totals, micro_grads))
            )
    owned = (
        lax.psum_scatter(totals[0], ("dp", "ctx"), scatter_dimension=0, tiled=True),
        lax.psum_scatter(totals[1], ("dp", "ctx"), scatter_dimension=0, tiled=True),
        lax.psum_scatter(totals[2], ("dp", "ctx"), scatter_dimension=1, tiled=True),
        lax.psum_scatter(totals[3], ("dp", "ctx"), scatter_dimension=0, tiled=True),
        lax.psum_scatter(totals[4], ("dp", "ctx"), scatter_dimension=0, tiled=True),
        lax.psum_scatter(totals[5], ("dp", "ctx"), scatter_dimension=1, tiled=True),
        lax.psum_scatter(totals[6], ("dp", "ctx"), scatter_dimension=0, tiled=True),
        lax.psum_scatter(totals[7], ("dp", "ctx"), scatter_dimension=0, tiled=True),
        lax.psum_scatter(totals[8], ("dp", "ctx"), scatter_dimension=0, tiled=True),
        lax.psum_scatter(totals[9], ("dp", "ctx"), scatter_dimension=1, tiled=True),
        lax.psum_scatter(totals[10], ("dp", "ctx"), scatter_dimension=0, tiled=True),
        lax.psum_scatter(totals[11], ("dp", "ctx"), scatter_dimension=0, tiled=True),
        lax.psum_scatter(totals[12], ("dp", "ctx"), scatter_dimension=0, tiled=True),
    )
    bank_grads = tuple(
        (
            lax.dynamic_update_index_in_dim(
                jnp.zeros(weight_bank.shape, jnp.float32), owned_piece, tie_map[bank_number], 0
            )
            for bank_number, (weight_bank, owned_piece) in enumerate(zip(banks, owned))
        )
    )
    block_output = jnp.stack(outputs)[None]
    input_grad = jnp.stack(input_grads)[None]
    return (block_output, input_grad) + bank_grads


BF = jnp.bfloat16
F32 = jnp.float32
MESH = pl.DeviceIdType.MESH
ANY = pl.ANY
SMALL = 8
VMEM_BYTES = 62 * 2**20


def params(collective_id=None):
    if collective_id is None:
        return pltpu.CompilerParams(vmem_limit_bytes=VMEM_BYTES)
    return pltpu.CompilerParams(
        vmem_limit_bytes=VMEM_BYTES, collective_id=collective_id, has_side_effects=True
    )


def vmem():
    return pl.BlockSpec(memory_space=pltpu.VMEM)


def smem():
    return pl.BlockSpec(memory_space=pltpu.SMEM)


def anywhere():
    return pl.BlockSpec(memory_space=ANY)


def shape(dims, dtype):
    return jax.ShapeDtypeStruct(dims, dtype)


def nn(left, right):
    return lax.dot_general(left, right, (((1,), (0,)), ((), ())), preferred_element_type=F32)


def nt(left, right):
    return lax.dot_general(left, right, (((1,), (1,)), ((), ())), preferred_element_type=F32)


def tn(left, right):
    return lax.dot_general(left, right, (((0,), (0,)), ((), ())), preferred_element_type=F32)


def iota(dims, axis):
    return lax.broadcasted_iota(jnp.int32, dims, axis)


class Place:
    def __init__(self, depth):
        self.depth = depth
        self.z = lax.axis_index("dp")
        self.r = lax.axis_index("ctx")
        self.core = self.r % 2
        self.j = self.r // 2
        self.a = self.r // 4
        self.b = (self.r // 2) % 2
        self.by_a = (1 - self.a) * 4 + self.b * 2 + self.core
        self.by_b = self.a * 4 + (1 - self.b) * 2 + self.core
        self.both = (1 - self.a) * 4 + (1 - self.b) * 2 + self.core
        self.mate = self.j * 2 + 1 - self.core

    def slot(self, z, r):
        return z * 8 + r


def greet_all(here):
    bar = pltpu.get_barrier_semaphore()
    total = here.depth * 8
    me = here.z * 8 + here.r

    def signal(k, carry):
        other = (me + k) % total
        pl.semaphore_signal(bar, inc=1, device_id=(other // 8, other % 8), device_id_type=MESH)
        return carry

    lax.fori_loop(1, total, signal, 0)
    pl.semaphore_wait(bar, total - 1)


def remote(source, target, send, recv, z, r):
    return pltpu.make_async_remote_copy(
        src_ref=source,
        dst_ref=target,
        send_sem=send,
        recv_sem=recv,
        device_id=(z, r),
        device_id_type=MESH,
    )


def spread_units(small, width, hidden_total):
    devices = small.shape[0]
    unit = width // devices
    per = hidden_total // devices
    flat = small.reshape(devices * SMALL, 256)
    lane = iota((128, width), 1)
    pick = (lane % unit == iota((128, width), 0)).astype(F32).astype(BF)
    tall = nn(flat[:, 0:128], pick)
    row = iota((devices * SMALL, width), 0)
    col = iota((devices * SMALL, width), 1)
    tall = jnp.where(col // unit == row // SMALL, tall, 0.0)
    vectors = jnp.sum(tall.reshape(devices, SMALL, width), axis=0)
    chosen = (
        (iota((devices, devices * SMALL), 1) == iota((devices, devices * SMALL), 0) * SMALL)
        .astype(F32)
        .astype(BF)
    )
    firsts = nn(chosen, flat[:, 128:256]).astype(BF)
    lane = iota((128, hidden_total), 1)
    pick = (lane % per == iota((128, hidden_total), 0)).astype(F32).astype(BF)
    wide = nn(firsts, pick)
    keep = iota((devices, hidden_total), 1) // per == iota((devices, hidden_total), 0)
    return vectors, jnp.sum(jnp.where(keep, wide, 0.0), axis=0, keepdims=True)


def gather_units(vectors, hidden_row, devices):
    width = vectors.shape[1]
    hidden_total = hidden_row.shape[1]
    unit = width // devices
    per = hidden_total // devices
    tall = jnp.broadcast_to(vectors[None], (devices, SMALL, width)).reshape(devices * SMALL, width)
    row = iota((devices * SMALL, width), 0)
    col = iota((devices * SMALL, width), 1)
    tall = jnp.where(col // unit == row // SMALL, tall, 0.0).astype(BF)
    pick = (iota((width, 128), 0) % unit == iota((width, 128), 1)).astype(F32).astype(BF)
    left = nn(tall, pick)
    wide = jnp.broadcast_to(hidden_row, (devices, hidden_total))
    keep = iota((devices, hidden_total), 1) // per == iota((devices, hidden_total), 0)
    wide = jnp.where(keep, wide, 0.0).astype(BF)
    pick = (iota((hidden_total, 128), 0) % per == iota((hidden_total, 128), 1)).astype(F32)
    firsts = nn(wide, pick.astype(BF)).astype(BF)
    chosen = (
        iota((devices * SMALL, devices), 0) == iota((devices * SMALL, devices), 1) * SMALL
    ).astype(F32).astype(BF)
    right = nn(chosen, firsts)
    return (
        left.astype(BF).reshape(devices, SMALL, 128),
        right.astype(BF).reshape(devices, SMALL, 128),
    )


def group_slice(row, j, groups):
    width = row.shape[1] // groups
    out = jnp.zeros((1, width), F32)
    for g in range(groups):
        out = jnp.where(j == g, row[:, g * width : (g + 1) * width], out)
    return out


def group_spread(part, j, groups):
    return jnp.concatenate([jnp.where(j == g, part, 0.0) for g in range(groups)], axis=1)


def block_at(place_ref, micro, position, blocks):
    found = jnp.int32(0)
    for s in range(blocks):
        found = jnp.where(place_ref[0, micro, s] == position, s, found)
    return found


def stack_heads(rows, heads):
    lane = iota(rows.shape, 1) // HD
    zero = jnp.zeros_like(rows)
    return jnp.concatenate([jnp.where(lane == h, rows, zero) for h in range(heads)], axis=0)


def unstack_heads(tall, heads):
    rows = tall.shape[0] // heads
    lane = iota((rows, tall.shape[1]), 1) // HD
    out = tall[0:rows]
    for h in range(1, heads):
        out = jnp.where(lane == h, tall[h * rows : (h + 1) * rows], out)
    return out


def visible_bias(lens, micro, start, rows, key_start, keys):
    query = start + iota((rows, 1), 0)
    begin = jnp.zeros((rows, 1), jnp.int32)
    end = jnp.int32(0)
    for s in range(lens.shape[2]):
        end = end + lens[0, micro, s]
        begin = jnp.where(query >= end, end, begin)
    key = key_start + iota((rows, keys), 1)
    return jnp.where((key >= begin) & (key <= query), 0.0, masked_score)


def row_norm(wide):
    average = jnp.mean(wide, axis=-1, keepdims=True)
    centered = wide - average
    variance = jnp.mean(centered * centered, axis=-1, keepdims=True)
    scale = lax.rsqrt(variance + epsilon)
    return centered * scale, scale


def norm_back(grad, unit, scale):
    first = jnp.mean(grad, axis=-1, keepdims=True)
    second = jnp.mean(grad * unit, axis=-1, keepdims=True)
    return (grad - first - unit * second) * scale


QROWS = 128
KCOLS = 384
GELU_A = math.sqrt(2.0 / math.pi)
GELU_B = 0.044715


class Sizes:
    def __init__(self, depth, rows, width, hidden_total):
        self.depth = depth
        self.rows = rows
        self.width = width
        self.total = depth * 8
        self.unit = width // self.total
        self.per = hidden_total // self.total
        self.group = width // 4
        self.heads = self.group // HD
        self.pack = 8 * rows
        self.packed = self.unit + 2 * self.per
        self.units = self.group // self.unit
        cut = self.per - 8
        self.parts = (
            (0, self.unit, "b"),
            (self.unit, cut, "b"),
            (self.unit + cut, 2 * self.per - cut, "a"),
        )


def block_scratch(n):
    vm = lambda dims, dtype=BF: pltpu.VMEM(dims, dtype)
    dma = lambda dims: pltpu.SemaphoreType.DMA(dims)
    d, w, g, pack, rows = n.depth, n.width, n.group, n.pack, n.rows
    p = len(n.parts)
    both = 2 * rows
    halves = 2 * d
    chunk = n.per * 4
    return {
        "f_all": vm((n.total, n.packed, w)),
        "gr": vm((d, 2, 2, 2, n.packed, w)),
        "from_mate": vm((d, 2, 2, n.packed, w)),
        "from_one": vm((d, 2, n.packed, w)),
        "from_two": vm((d, n.packed, w)),
        "from_z": vm((d, n.packed, w)),
        "q_own": vm((3, n.unit, w)),
        "wts": vm((3, n.units, n.unit, w)),
        "small_all": vm((n.total, SMALL, 256)),
        "x_all": vm((2, 2, 2, rows, w)),
        "h": vm((pack, w)),
        "u": vm((pack, w)),
        "qkv": vm((3, pack, g)),
        "o": vm((pack, -(-(g + n.heads) // 128) * 128), F32),
        "vec": vm((SMALL, w), F32),
        "hid": vm((halves, 1, chunk), F32),
        "hid_grad": vm((halves, 1, chunk), F32),
        "stage": vm((8, rows, g)),
        "at_recv": vm((8, rows, g)),
        "da_recv": vm((8, rows, g)),
        "resid": vm((both, w), F32),
        "unit2": vm((both, w), F32),
        "h2": vm((both, w)),
        "scale2": vm((both, 1), F32),
        "vec_grad": vm((SMALL, w), F32),
        "da": vm((pack, g)),
        "dk_acc": vm((pack, g), F32),
        "dv_acc": vm((pack, g), F32),
        "gq": vm((3, n.units // 2, 2, n.unit, w)),
        "q_mate": vm((3, n.units // 2, n.unit, w)),
        "q_line": vm((3, d, n.unit, w)),
        "dh_a1": vm((2, rows, w)),
        "dh_b1": vm((2, rows, w)),
        "dh_a2": vm((rows, w)),
        "dh_b2": vm((rows, w)),
        "dh_mate": vm((rows, w)),
        "sums": vm((SMALL, w), F32),
        "sg": vm((n.total, SMALL, 256)),
        "sg_recv": vm((n.total, SMALL, 256)),
        "s_zsend": dma((p, d)),
        "s_zrecv": dma((p, d)),
        "s_send1": dma((p, d)),
        "s_recv1": dma((p, d)),
        "s_send2": dma((p, d, 2)),
        "s_recv2": dma((p, d, 2)),
        "s_csend": dma((p, d, 4)),
        "s_crecv": dma((p, d, 4)),
        "s_xsend": dma((7,)),
        "s_xrecv": dma((8,)),
        "s_qsend": dma((3, d)),
        "s_qrecv": dma((3, n.units)),
        "s_qcsend": dma((3, n.units)),
        "s_smsend": dma((n.total,)),
        "s_smrecv": dma((n.total,)),
        "s_asend": dma((8,)),
        "s_arecv": dma((8,)),
        "s_dsend": dma((8,)),
        "s_drecv": dma((8,)),
        "s_rcs": dma((p, d)),
        "s_rcr": dma((p, d)),
        "s_r1s": dma((p, d)),
        "s_r1r": dma((p, d)),
        "s_r2s": dma((p, d)),
        "s_r2r": dma((p, d)),
        "s_rzs": dma((p, d)),
        "s_rzr": dma((p, d)),
        "s_gqc": dma((2,)),
        "s_gqs": dma((3, n.units // 2)),
        "s_gqr": dma((3, d)),
        "s_dhs": dma((5,)),
        "s_dhr": dma((5,)),
        "s_sgs": dma((n.total,)),
        "s_sgr": dma((n.total,)),
    }


def add_into(target, source):
    target[...] = (target[...].astype(F32) + source[...].astype(F32)).astype(BF)


def block_kernel(n, names, tie, lens, spans, x_ref, dy_ref, *refs):
    banks = refs[:13]
    y_out, dr_out, dh_out, f_sum, q_sum, small_sum, vec_out = refs[13:20]
    s = types.SimpleNamespace(**dict(zip(names, refs[20:])))
    g1, s1, wq, bq, bv, wo, bo, g2, s2, wu, bu, wd, bd = banks
    depth, unit, per, rows, width, group, heads = (
        n.depth, n.unit, n.per, n.rows, n.width, n.group, n.heads
    )
    here = Place(depth)
    z, r, a, b, core, j = here.z, here.r, here.a, here.b, here.core, here.j
    me = here.slot(z, r)
    micro = core
    mate, by_a, by_b, both = here.mate, here.by_a, here.by_b, here.both
    parts = n.parts
    main = (1, 2)
    groups = 4

    bar = pltpu.get_barrier_semaphore()

    def signal(k, carry):
        other = (me + k) % n.total
        pl.semaphore_signal(bar, inc=1, device_id=(other // 8, other % 8), device_id_type=MESH)
        return carry

    lax.fori_loop(1, n.total, signal, 0)

    f_own = s.f_all.at[me]
    f_own[0:unit, :] = wo[tie[5]]
    f_own[unit : unit + per, :] = wu[tie[9]]
    f_own[unit + per :, :] = wd[tie[11]]
    s.q_own[...] = wq[tie[2]].reshape(3, unit, width)
    chosen_rows = []
    for bank, index in ((g1, 0), (s1, 1), (bq, 3), (bv, 4), (bo, 6), (g2, 7), (s2, 8), (bd, 12)):
        wide = bank[...].astype(F32)
        chosen = jnp.zeros((1, unit), F32)
        for layer in range(bank.shape[0]):
            chosen = jnp.where(tie[index] == layer, wide[layer : layer + 1, :], chosen)
        chosen_rows.append(chosen)
    small_own = s.small_all.at[me]
    small_own[...] = jnp.zeros((SMALL, 256), BF)
    small_own[:, 0:unit] = jnp.concatenate(chosen_rows, axis=0).astype(BF)
    wide = bu[...].astype(F32)
    chosen = jnp.zeros((1, per), F32)
    for layer in range(bu.shape[0]):
        chosen = jnp.where(tie[10] == layer, wide[layer : layer + 1, :], chosen)
    tall = jnp.concatenate([chosen, jnp.zeros((SMALL - 1, per), F32)], axis=0)
    small_own[:, 128 : 128 + per] = tall.astype(BF)

    pl.semaphore_wait(bar, n.total - 1)

    def to_all(buffer_of, send, recv, target):
        def go(k, carry):
            other = (me + k) % n.total
            remote(
                buffer_of(other), target.at[me], send.at[other], recv.at[me], other // 8, other % 8
            ).start()
            return carry

        lax.fori_loop(1, n.total, go, 0)

    def from_all(buffer, send, recv, target):
        def go(k, carry):
            other = (me + k) % n.total
            remote(
                buffer, target.at[other], send.at[other], recv.at[other], other // 8, other % 8
            ).wait()
            return carry

        lax.fori_loop(1, n.total, go, 0)

    def row_block(block):
        return s.x_all.at[block // 4, (block // 2) % 2, block % 2]

    def row_move(source, block, lane, to):
        return remote(source, row_block(block), s.s_xsend.at[lane], s.s_xrecv.at[block], z, to)

    mate_a = by_a + 1 - 2 * core
    row_move(x_ref.at[1 - core], r, 0, mate).start()
    row_move(x_ref.at[core], r, 1, by_b).start()
    row_move(x_ref.at[core], r, 2, by_a).start()
    to_all(lambda other: small_own, s.s_smsend, s.s_smrecv, s.small_all)
    row_block(r)[...] = x_ref[core]

    def q_unit(t):
        block = me * 3 + t
        kind = block // n.total
        inside = block % n.total
        return kind, inside // n.units, inside % n.units

    def q_first(t, zz):
        kind, chip, at = q_unit(t)
        to = chip * 2 + core
        source, target, recv = s.q_own.at[t], s.wts.at[kind, at], s.s_qrecv.at[kind, at]
        go = lambda: remote(source, target, s.s_qsend.at[t, zz], recv, zz, to)
        stay = lambda: pltpu.make_async_copy(source, target, recv)
        return go, stay, (zz == z) & (to == r)

    for t in range(3):
        for zz in range(depth):
            go, stay, mine = q_first(t, zz)

            @pl.when(jnp.logical_not(mine))
            def _():
                go().start()

            @pl.when(mine)
            def _():
                stay().start()

    def order(k):
        out = jnp.int32(0)
        for zz in range(depth):
            line = sorted(range(depth), key=lambda t: (abs(t - zz), t))
            for kk in range(depth):
                out = jnp.where((z == zz) & (k == kk), line[kk], out)
        return out

    def move(p, zz, rr, send, recv, to_z, to_r):
        start, count, _ = parts[p]
        ref = s.f_all.at[here.slot(zz, rr), pl.ds(start, count)]
        return remote(ref, ref, send, recv, to_z, to_r)

    def first_axis(p):
        return by_b if parts[p][2] == "b" else by_a

    def second_axis(p):
        return by_a if parts[p][2] == "b" else by_b

    def line_move(p, o, to_z):
        return move(p, o, r, s.s_zsend.at[p, to_z], s.s_zrecv.at[p, o], to_z, r)

    def one(p, o):
        return move(p, o, r, s.s_send1.at[p, o], s.s_recv1.at[p, o], z, first_axis(p))

    def two(p, o, rr, lane):
        return move(
            p, o, rr, s.s_send2.at[p, o, lane], s.s_recv2.at[p, o, lane], z, second_axis(p)
        )

    def across(p, o, rr, lane):
        return move(p, o, rr, s.s_csend.at[p, o, lane], s.s_crecv.at[p, o, lane], z, mate)

    every = range(len(parts))
    for p in every:
        for k in range(1, depth):
            line_move(p, z, order(k)).start()

    def row_arrived(block):
        row_move(x_ref.at[0], block, 0, mate).wait_recv()

    row_arrived(mate)
    row_move(row_block(mate), mate, 3, by_a).start()
    row_move(row_block(mate), mate, 4, by_b).start()
    row_arrived(by_b)
    row_move(row_block(by_b), by_b, 5, by_a).start()
    row_arrived(mate_a)
    row_move(row_block(mate_a), mate_a, 6, by_b).start()

    def q_relay(e, carry):
        kind, at = e // n.units, e % n.units
        owner = (kind * n.total + j * n.units + at) // 3
        unit_ref = s.wts.at[kind, at]

        @pl.when(owner % 2 == core)
        def _():
            pltpu.make_async_copy(unit_ref, unit_ref, s.s_qrecv.at[kind, at]).wait()
            remote(
                unit_ref, unit_ref, s.s_qcsend.at[kind, at], s.s_qrecv.at[kind, at], z, mate
            ).start()

        return carry

    lax.fori_loop(0, 3 * n.units, q_relay, 0)

    def spread_own(p):
        one(p, z).start()
        two(p, z, r, 0).start()
        across(p, z, r, 0).start()

    for p in every:
        spread_own(p)

    from_all(small_own, s.s_smsend, s.s_smrecv, s.small_all)
    vectors, hidden = spread_units(s.small_all[...], width, per * n.total)
    s.vec[...] = vectors
    vec_out[...] = vectors
    chunk = 4 * per
    for c in range(2 * depth):
        s.hid[c] = hidden[:, c * chunk : (c + 1) * chunk]

    row_arrived(by_a)
    row_arrived(both)
    row_arrived(by_b + 1 - 2 * core)
    row_arrived(both + 1 - 2 * core)

    def q_rest(e, carry):
        kind, at = e // n.units, e % n.units
        owner = (kind * n.total + j * n.units + at) // 3
        unit_ref = s.wts.at[kind, at]

        @pl.when(owner % 2 != core)
        def _():
            remote(
                unit_ref, unit_ref, s.s_qcsend.at[kind, at], s.s_qrecv.at[kind, at], z, mate
            ).wait_recv()

        return carry

    lax.fori_loop(0, 3 * n.units, q_rest, 0)

    gain, shift = s.vec[0:1, :], s.vec[1:2, :]
    query_add = group_slice(s.vec[2:3, :], j, groups)
    value_add = group_slice(s.vec[3:4, :], j, groups)

    def weight(kind):
        return s.wts[kind].reshape(group, width)

    def project(p, carry):
        source = block_at(spans, micro, p, 8)
        unit_rows, _ = row_norm(
            s.x_all[source // 4, (source // 2) % 2, source % 2].astype(F32)
        )
        normed = (unit_rows * gain + shift).astype(BF)
        at = pl.ds(pl.multiple_of(p * rows, 16), rows)
        s.u[at, :] = unit_rows.astype(BF)
        s.h[at, :] = normed
        s.qkv[0, at, :] = (nt(normed, weight(0)) + query_add).astype(BF)
        s.qkv[1, at, :] = nt(normed, weight(1)).astype(BF)
        s.qkv[2, at, :] = (nt(normed, weight(2)) + value_add).astype(BF)
        return carry

    lax.fori_loop(0, 8, project, 0)

    def line_event(k, which):
        o = order(k)
        for p in which:
            line_move(p, o, z).wait_recv()
            one(p, o).start()
            two(p, o, r, 0).start()
            across(p, o, r, 0).start()

    def first_event(k, which):
        o = order(k)
        for p in which:
            one(p, o).wait_recv()
            two(p, o, first_axis(p), 1).start()
            across(p, o, first_axis(p), 1).start()

    def second_event(o, which):
        for p in which:
            two(p, o, r, 0).wait_recv()
            across(p, o, second_axis(p), 2).start()
            two(p, o, r, 1).wait_recv()
            across(p, o, both, 3).start()

    def all_here(o, which):
        for p in which:
            for lane in range(4):
                across(p, o, r, lane).wait_recv()

    gather_events = {
        0: [lambda: line_event(1, (0,)), lambda: line_event(1, main)],
        1: [lambda: line_event(2, (0,)), lambda: first_event(0, (0,))],
        2: [lambda: line_event(3, (0,)), lambda: first_event(0, main)],
        3: [lambda: line_event(2, main)],
        4: [lambda: first_event(1, (0,)), lambda: first_event(1, main)],
        5: [lambda: first_event(2, (0,))],
        6: [lambda: line_event(3, main), lambda: first_event(3, (0,))],
        7: [lambda: first_event(2, main)],
        8: [lambda: first_event(3, main)],
    }

    def run_events(events, i):
        for at, acts in events.items():

            @pl.when(i == at)
            def _(acts=acts):
                for act in acts:
                    act()

    tall = heads * QROWS
    q_blocks = n.pack // QROWS

    def attend(i, carry):
        start = pl.multiple_of(i * QROWS, QROWS)
        stacked = stack_heads(s.qkv[0, pl.ds(start, QROWS), :] * BF(score_scale), heads)

        def step(kc, state):
            top, total, acc = state
            at = pl.ds(pl.multiple_of(kc * KCOLS, KCOLS), KCOLS)
            bias = visible_bias(lens, micro, start, QROWS, kc * KCOLS, KCOLS)
            scores = nt(stacked, s.qkv[1, at, :])
            scores = (scores.reshape(heads, QROWS, KCOLS) + bias[None]).reshape(tall, KCOLS)
            new_top = jnp.maximum(top, jnp.max(scores, axis=1, keepdims=True))
            probs = jnp.exp(scores - new_top)
            factor = jnp.exp(top - new_top)
            total = total * factor + jnp.sum(probs, axis=1, keepdims=True)
            acc = acc * factor + nn(probs.astype(BF), s.qkv[2, at, :])
            return new_top, total, acc

        top, total, acc = lax.fori_loop(
            0,
            (i * QROWS) // KCOLS + 1,
            step,
            (
                jnp.full((tall, 1), masked_score, F32),
                jnp.zeros((tall, 1), F32),
                jnp.zeros((tall, group), F32),
            ),
        )
        at_q = pl.ds(start, QROWS)
        s.o[at_q, 0:group] = unstack_heads(acc / total, heads)
        lse = top + jnp.log(total)
        for head in range(heads):
            s.o[at_q, group + head : group + head + 1] = lse[head * QROWS : (head + 1) * QROWS]
        run_events(gather_events, i)
        return carry

    lax.fori_loop(0, q_blocks, attend, 0)

    for e in range(8):
        at = pl.ds(spans[0, micro, e] * rows, rows)
        s.stage[e] = s.o[at, 0:group].astype(BF)

    def exchange_start(stage, target, send, recv):
        for k in range(1, 8):
            to = (r + k) % 8
            remote(stage.at[to], target.at[r], send.at[to], recv.at[r], z, to).start()
        target[r] = stage[r]

    def exchange_wait(stage, target, send, recv):
        for k in range(1, 8):
            frm = (r + k) % 8
            remote(stage.at[frm], target.at[frm], send.at[frm], recv.at[frm], z, frm).wait()

    exchange_start(s.stage, s.at_recv, s.s_asend, s.s_arecv)
    for k in range(depth):
        second_event(order(k), (0,))
    second_event(z, main)
    for k in range(depth):
        all_here(order(k), (0,))
    exchange_wait(s.stage, s.at_recv, s.s_asend, s.s_arecv)

    full = 2 * rows
    def attended():
        pieces = [
            jnp.concatenate([s.at_recv[2 * g], s.at_recv[2 * g + 1]], axis=0)
            for g in range(groups)
        ]
        return jnp.concatenate(pieces, axis=1)

    out_w = s.f_all[:, 0:unit, :].reshape(width, width)
    res = (
        x_ref[...].reshape(full, width).astype(F32) + nt(attended(), out_w) + s.vec[4:5, :]
    )
    s.resid[...] = res + s.vec[7:8, :]
    unit_rows, scale = row_norm(res)
    s.unit2[...] = unit_rows
    s.scale2[...] = scale
    s.h2[...] = (unit_rows * s.vec[5:6, :] + s.vec[6:7, :]).astype(BF)
    dr_out[...] = jnp.zeros_like(dr_out)

    def cut(p):
        return pl.ds(parts[p][0], parts[p][1])

    def sum_mate(p, t):
        return remote(
            s.gr.at[t, :, :, 1 - core, cut(p)],
            s.from_mate.at[t, :, :, cut(p)],
            s.s_rcs.at[p, t],
            s.s_rcr.at[p, t],
            z,
            mate,
        )

    def sum_first(p, t):
        if parts[p][2] == "b":
            source, to = s.gr.at[t, 1 - a, :, core, cut(p)], by_a
        else:
            source, to = s.gr.at[t, :, 1 - b, core, cut(p)], by_b
        target = s.from_one.at[t, :, cut(p)]
        return remote(source, target, s.s_r1s.at[p, t], s.s_r1r.at[p, t], z, to)

    def sum_second(p, t):
        if parts[p][2] == "b":
            source, to = s.gr.at[t, a, 1 - b, core, cut(p)], by_b
        else:
            source, to = s.gr.at[t, 1 - a, b, core, cut(p)], by_a
        target = s.from_two.at[t, cut(p)]
        return remote(source, target, s.s_r2s.at[p, t], s.s_r2r.at[p, t], z, to)

    def sum_line(p, t, origin):
        return remote(
            s.gr.at[t, a, b, core, cut(p)],
            s.from_z.at[origin, cut(p)],
            s.s_rzs.at[p, t],
            s.s_rzr.at[p, origin],
            t,
            r,
        )

    def start_sum(t, which):
        for p in which:
            sum_mate(p, t).start()

    def event_one(t, which):
        for p in which:
            sum_mate(p, t).wait_recv()
            for aa in range(2):
                for bb in range(2):
                    add_into(s.gr.at[t, aa, bb, core, cut(p)], s.from_mate.at[t, aa, bb, cut(p)])
            sum_first(p, t).start()

    def event_two(t, which):
        for p in which:
            sum_first(p, t).wait_recv()
            for e in range(2):
                mine = (
                    s.gr.at[t, a, e, core, cut(p)]
                    if parts[p][2] == "b"
                    else s.gr.at[t, e, b, core, cut(p)]
                )
                add_into(mine, s.from_one.at[t, e, cut(p)])
            sum_second(p, t).start()

    def event_three(t, which):
        for p in which:
            sum_second(p, t).wait_recv()
            add_into(s.gr.at[t, a, b, core, cut(p)], s.from_two.at[t, cut(p)])

            @pl.when(t != z)
            def _(p=p):
                sum_line(p, t, z).start()

    g_down = dy_ref[...].reshape(full, width)

    def feed(c, carry):
        k, half = c // 2, c % 2
        o = order(k)

        @pl.when((half == 0) & (k > 0))
        def _():
            second_event(o, main)

        @pl.when(half == 0)
        def _():
            all_here(o, main)

        devices = pl.ds(o * 8 + half * 4, 4)
        up_w = s.f_all[devices, unit : unit + per, :].reshape(chunk, width)
        down_w = s.f_all[devices, unit + per : unit + 2 * per, :].reshape(chunk, width)
        where = o * 2 + half
        up = nt(s.h2[...], up_w) + s.hid[where]
        square = up * up
        tanh = jnp.tanh(GELU_A * (up + GELU_B * square * up))
        side = 0.5 * (1.0 + tanh)
        act = (up * side).astype(BF)
        s.resid[...] += nn(act, down_w)
        slope = side + 0.5 * up * (1.0 - tanh * tanh) * (GELU_A * (1.0 + 3.0 * GELU_B * square))
        grad = dy_ref[...].reshape(full, width)
        d_up = (nt(grad, down_w) * slope).astype(BF)
        s.hid_grad[where] = jnp.sum(d_up.astype(F32), axis=0, keepdims=True)
        dr_out[...] += nn(d_up, up_w).reshape(2, rows, width)
        s.gr[o, half, :, :, unit : unit + per, :] = (
            tn(d_up, s.h2[...]).astype(BF).reshape(2, 2, per, width)
        )
        s.gr[o, half, :, :, unit + per : unit + 2 * per, :] = (
            tn(act, grad).astype(BF).reshape(2, 2, per, width)
        )

        @pl.when(half == 1)
        def _():
            start_sum(o, main)

            @pl.when(k > 0)
            def _():
                event_one(order(k - 1), main)

        return carry

    lax.fori_loop(0, 2 * depth, feed, 0)

    dy = g_down.astype(F32)
    y_out[...] = s.resid[...].astype(BF).reshape(2, rows, width)
    d_h2 = dr_out[...].reshape(full, width)
    unit_rows = s.unit2[...]
    d_res = dy + norm_back(d_h2 * s.vec[5:6, :], unit_rows, s.scale2[...])
    dr_out[...] = d_res.reshape(2, rows, width)
    g_mix = d_res.astype(BF)
    d_attn = nn(g_mix, s.f_all[:, 0:unit, :].reshape(width, width)).astype(BF)
    for m in range(2):
        for g in range(groups):
            s.stage[2 * g + m] = d_attn[
                m * rows : (m + 1) * rows, g * group : (g + 1) * group
            ]
    exchange_start(s.stage, s.da_recv, s.s_dsend, s.s_drecv)
    out_grad = tn(g_mix, attended()).astype(BF).reshape(depth, 2, 2, 2, unit, width)
    s.gr[:, :, :, :, 0:unit, :] = out_grad
    for k in range(depth):
        start_sum(order(k), (0,))
    s.vec_grad[...] = jnp.zeros_like(s.vec_grad)
    s.vec_grad[4:5, :] = jnp.sum(g_mix.astype(F32), axis=0, keepdims=True)
    s.vec_grad[5:6, :] = jnp.sum(d_h2 * unit_rows, axis=0, keepdims=True)
    s.vec_grad[6:7, :] = jnp.sum(d_h2, axis=0, keepdims=True)
    s.vec_grad[7:8, :] = jnp.sum(dy, axis=0, keepdims=True)
    event_one(order(depth - 1), main)
    exchange_wait(s.stage, s.da_recv, s.s_dsend, s.s_drecv)

    for p in range(8):
        s.da[p * rows : (p + 1) * rows, :] = s.da_recv[block_at(spans, micro, p, 8)]
    s.dk_acc[...] = jnp.zeros_like(s.dk_acc)
    s.dv_acc[...] = jnp.zeros_like(s.dv_acc)

    def out_events(act):
        def go():
            for k in range(depth):
                act(order(k), (0,))

        return go

    sum_events = {
        0: [lambda: event_two(order(0), main)],
        1: [lambda: event_two(order(1), main)],
        2: [lambda: event_two(order(2), main), lambda: event_three(order(0), main)],
        3: [out_events(event_one), lambda: event_three(order(1), main)],
        4: [lambda: event_two(order(3), main)],
        5: [out_events(event_two), lambda: event_three(order(2), main)],
        6: [lambda: event_three(order(3), main)],
        8: [out_events(event_three)],
    }

    def query_block(i, carry):
        start = pl.multiple_of(i * QROWS, QROWS)
        at_q = pl.ds(start, QROWS)
        stacked = stack_heads(s.qkv[0, at_q, :] * BF(score_scale), heads)
        d_rows = s.da[at_q, :]
        d_stacked = stack_heads(d_rows, heads)
        product = d_rows.astype(F32) * s.o[at_q, 0:group]
        delta = jnp.sum(stack_heads(product, heads), axis=1, keepdims=True)
        lse = jnp.concatenate(
            [s.o[at_q, group + head : group + head + 1] for head in range(heads)], axis=0
        )

        def step(kc, acc):
            at = pl.ds(pl.multiple_of(kc * KCOLS, KCOLS), KCOLS)
            bias = visible_bias(lens, micro, start, QROWS, kc * KCOLS, KCOLS)
            keys = s.qkv[1, at, :]
            scores = nt(stacked, keys)
            scores = (scores.reshape(heads, QROWS, KCOLS) + bias[None]).reshape(tall, KCOLS)
            probs = jnp.exp(scores - lse)
            d_probs = nt(d_stacked, s.qkv[2, at, :])
            d_scores = (probs * (d_probs - delta)).astype(BF)
            s.dk_acc[at, :] += tn(d_scores, stacked)
            s.dv_acc[at, :] += tn(probs.astype(BF), d_stacked)
            return acc + nn(d_scores, keys)

        acc = lax.fori_loop(0, (i * QROWS) // KCOLS + 1, step, jnp.zeros((tall, group), F32))
        s.qkv[0, at_q, :] = (unstack_heads(acc, heads) * score_scale).astype(BF)
        run_events(sum_events, i)
        return carry

    lax.fori_loop(0, q_blocks, query_block, 0)
    s.qkv[1] = s.dk_acc[...].astype(BF)
    s.qkv[2] = s.dv_acc[...].astype(BF)

    pairs = n.units // 2
    for kind in range(3):
        s.gq[kind] = tn(s.qkv[kind], s.h[...]).astype(BF).reshape(pairs, 2, unit, width)
    q_mate = remote(
        s.gq.at[:, :, 1 - core], s.q_mate, s.s_gqc.at[0], s.s_gqc.at[1], z, mate
    )
    q_mate.start()

    def q_route(kind, m):
        block = kind * n.total + j * n.units + m * 2 + core
        owner = block // 3
        return owner // 8, owner % 8, block % 3

    def q_out(kind, m):
        oz, orr, at = q_route(kind, m)
        source = s.gq.at[kind, m, core]
        target, send = s.q_line.at[at, z], s.s_gqs.at[kind, m]
        go = lambda: remote(source, target, send, s.s_gqr.at[at, z], oz, orr)
        stay = lambda: pltpu.make_async_copy(source, target, send)
        return go, stay, (oz == z) & (orr == r)

    def q_sums(act):
        def each(e, carry):
            kind, m = e // pairs, e % pairs
            go, stay, mine = q_out(kind, m)
            act(kind, m, go, stay, mine)
            return carry

        lax.fori_loop(0, 3 * pairs, each, 0)

    def q_send(kind, m, go, stay, mine):
        add_into(s.gq.at[kind, m, core], s.q_mate.at[kind, m])

        @pl.when(jnp.logical_not(mine))
        def _():
            go().start()

        @pl.when(mine)
        def _():
            stay().start()

    def q_sent(kind, m, go, stay, mine):
        @pl.when(jnp.logical_not(mine))
        def _():
            go().wait_send()

        @pl.when(mine)
        def _():
            stay().wait()

    for lane in range(7):
        row_move(x_ref.at[0], r, lane, mate).wait_send()
    s.sums[...] = jnp.zeros_like(s.sums)

    def dh_a1():
        return remote(s.x_all.at[1 - a, :, core], s.dh_a1, s.s_dhs.at[0], s.s_dhr.at[0], z, by_a)

    def dh_b1():
        return remote(s.x_all.at[:, 1 - b, 1 - core], s.dh_b1, s.s_dhs.at[1], s.s_dhr.at[1], z, by_b)

    def dh_a2():
        return remote(s.x_all.at[a, 1 - b, core], s.dh_a2, s.s_dhs.at[2], s.s_dhr.at[2], z, by_b)

    def dh_b2():
        return remote(s.x_all.at[1 - a, b, 1 - core], s.dh_b2, s.s_dhs.at[3], s.s_dhr.at[3], z, by_a)

    def dh_m():
        return remote(s.x_all.at[a, b, 1 - core], s.dh_mate, s.s_dhs.at[4], s.s_dhr.at[4], z, mate)

    def unsort(e, carry):
        late, kind, lane = e // 4, (e % 4) // 2, e % 2
        aa = jnp.where(kind == 0, jnp.where(late == 1, a, 1 - a), lane)
        bb = jnp.where(kind == 0, lane, jnp.where(late == 1, b, 1 - b))
        cc = jnp.where(kind == 0, core, 1 - core)
        at = pl.ds(spans[0, micro, aa * 4 + bb * 2 + cc] * rows, rows)
        part = (
            nn(s.qkv[0, at, :], weight(0))
            + nn(s.qkv[1, at, :], weight(1))
            + nn(s.qkv[2, at, :], weight(2))
        )
        s.x_all[aa, bb, cc] = part.astype(BF)
        s.sums[0:1, :] += jnp.sum(part * s.u[at, :].astype(F32), axis=0, keepdims=True)
        s.sums[1:2, :] += jnp.sum(part, axis=0, keepdims=True)

        @pl.when(e == 3)
        def _():
            dh_a1().start()
            dh_b1().start()
            q_mate.wait_recv()
            q_sums(q_send)

        return carry

    lax.fori_loop(0, 8, unsort, 0)

    query_bias = jnp.sum(s.qkv[0].astype(F32), axis=0, keepdims=True)
    value_bias = jnp.sum(s.qkv[2].astype(F32), axis=0, keepdims=True)
    s.vec_grad[0:2, :] = s.sums[0:2, :]
    s.vec_grad[2:3, :] = group_spread(query_bias, j, groups)
    s.vec_grad[3:4, :] = group_spread(value_bias, j, groups)
    hidden_row = jnp.concatenate([s.hid_grad[c] for c in range(2 * depth)], axis=1)
    left, right = gather_units(s.vec_grad[...], hidden_row, n.total)
    s.sg[:, :, 0:128] = left
    s.sg[:, :, 128:256] = right
    to_all(lambda other: s.sg.at[other], s.s_sgs, s.s_sgr, s.sg_recv)
    s.sg_recv[me] = s.sg[me]

    dh_a1().wait_recv()
    for e in range(2):
        add_into(s.x_all.at[a, e, core], s.dh_a1.at[e])
    dh_a2().start()
    dh_b1().wait_recv()
    for e in range(2):
        add_into(s.x_all.at[e, b, 1 - core], s.dh_b1.at[e])
    dh_b2().start()
    dh_b2().wait_recv()
    add_into(s.x_all.at[a, b, 1 - core], s.dh_b2)
    dh_m().start()

    for k in range(1, depth):
        o = order(k)
        for p in every:
            sum_line(p, z, o).wait_recv()
    total_rows = s.gr[z, a, b, core].astype(F32)
    for k in range(1, depth):
        total_rows = total_rows + s.from_z[order(k)].astype(F32)
    f_sum[...] = total_rows

    dh_a2().wait_recv()
    dh_out[core] = s.x_all[a, b, core].astype(F32) + s.dh_a2[...].astype(F32)
    dh_m().wait_recv()
    dh_out[1 - core] = s.dh_mate[...].astype(F32)

    from_all(s.sg.at[0], s.s_sgs, s.s_sgr, s.sg_recv)
    small_sum[...] = jnp.sum(s.sg_recv[...].astype(F32), axis=0)

    def q_arrivals(at, zz):
        block = me * 3 + at
        inside = block % n.total
        from_r = (inside // n.units) * 2 + (inside % n.units) % 2
        ref = s.q_line.at[at, zz]
        come = lambda: remote(ref, ref, s.s_gqs.at[0, 0], s.s_gqr.at[at, zz], zz, from_r)
        return come, (from_r == r) & (zz == z)

    for at in range(3):
        for zz in range(depth):
            come, mine = q_arrivals(at, zz)

            @pl.when(jnp.logical_not(mine))
            def _():
                come().wait_recv()

    q_sums(q_sent)
    for at in range(3):
        part = s.q_line[at, 0].astype(F32)
        for zz in range(1, depth):
            part = part + s.q_line[at, zz].astype(F32)
        q_sum[at] = part

    for t in range(3):
        for zz in range(depth):
            go, _, mine = q_first(t, zz)

            @pl.when(jnp.logical_not(mine))
            def _():
                go().wait_send()

    def q_relayed(e, carry):
        kind, at = e // n.units, e % n.units
        owner = (kind * n.total + j * n.units + at) // 3
        unit_ref = s.wts.at[kind, at]

        @pl.when(owner % 2 == core)
        def _():
            remote(
                unit_ref, unit_ref, s.s_qcsend.at[kind, at], s.s_qrecv.at[kind, at], z, mate
            ).wait_send()

        return carry

    lax.fori_loop(0, 3 * n.units, q_relayed, 0)
    q_mate.wait_send()
    for act in (dh_a1, dh_b1, dh_a2, dh_b2, dh_m):
        act().wait_send()

    def drain(o, carry):
        for p in every:
            one(p, o).wait_send()
            for lane in range(2):
                two(p, o, r, lane).wait_send()
            for lane in range(4):
                across(p, o, r, lane).wait_send()
            sum_mate(p, o).wait_send()
            sum_first(p, o).wait_send()
            sum_second(p, o).wait_send()

            @pl.when(o != z)
            def _(p=p):
                line_move(p, z, o).wait_send()
                sum_line(p, o, z).wait_send()

        return carry

    lax.fori_loop(0, depth, drain, 0)


def run_block(n, tie_map, lens, spans, x_own, dy_own, banks):
    rows, width = n.rows, n.width
    scratch = block_scratch(n)
    outs = (
        shape((2, rows, width), BF),
        shape((2, rows, width), F32),
        shape((2, rows, width), F32),
        shape((n.packed, width), F32),
        shape((3, n.unit, width), F32),
        shape((SMALL, 256), F32),
        shape((SMALL, width), F32),
    )
    return pl.pallas_call(
        functools.partial(block_kernel, n, tuple(scratch)),
        name="block",
        out_shape=outs,
        in_specs=[smem()] * 3 + [vmem()] * 15,
        out_specs=(vmem(),) * len(outs),
        scratch_shapes=list(scratch.values()),
        compiler_params=params(1),
    )(tie_map, lens, spans, x_own, dy_own, *banks)


def final_kernel(
    n, tie, x_ref, y_ref, dh_ref, dr_ref, vec_ref, f_ref, q_ref, small_ref, y_out, dx_out, *grads
):
    g1, s1, wq, bq, bv, wo, bo, g2, s2, wu, bu, wd, bd = grads
    y_out[...] = y_ref[...]
    for m in range(x_ref.shape[0]):
        unit_rows, scale = row_norm(x_ref[m].astype(F32))
        back = norm_back(dh_ref[m] * vec_ref[0:1, :], unit_rows, scale)
        dx_out[m] = (dr_ref[m] + back).astype(BF)
    layers = wq.shape[0]
    unit, per = n.unit, n.per

    def put(ref, index, value):
        for layer in range(layers):
            ref[layer] = jnp.where(tie[index] == layer, value, 0.0)

    put(wo, 5, f_ref[0:unit, :])
    put(wu, 9, f_ref[unit : unit + per, :])
    put(wd, 11, f_ref[unit + per :, :])
    put(wq, 2, q_ref[...].reshape(3 * unit, n.width))
    names = ((g1, 0), (s1, 1), (bq, 3), (bv, 4), (bo, 6), (g2, 7), (s2, 8), (bd, 12))
    for e, (ref, index) in enumerate(names):
        for layer in range(layers):
            ref[layer : layer + 1, :] = jnp.where(
                tie[index] == layer, small_ref[e : e + 1, 0:unit], 0.0
            )
    for layer in range(layers):
        bu[layer : layer + 1, :] = jnp.where(
            tie[10] == layer, small_ref[0:1, 128 : 128 + per], 0.0
        )


def turned(bank):
    return jnp.swapaxes(bank, 1, 2)


def grouped_plan(depth, *args):
    block_input, cotangent, tie_map, seq_lengths, span_place = args[:5]
    banks = list(args[5:])
    for index in (2, 5, 9):
        banks[index] = turned(banks[index])
    x_own, dy_own = block_input[0], cotangent[0]
    n = Sizes(depth, x_own.shape[1], x_own.shape[2], banks[10].shape[1] * depth * 8)
    y, d_resid, dh, f_sum, q_sum, small_sum, vectors = run_block(
        n, tie_map, seq_lengths, span_place, x_own, dy_own, banks
    )
    outs = (shape(x_own.shape, BF),) * 2 + tuple(shape(bank.shape, F32) for bank in banks)
    final = pl.pallas_call(
        functools.partial(final_kernel, n),
        name="finish",
        out_shape=outs,
        in_specs=[smem()] + [vmem()] * 8,
        out_specs=(vmem(),) * len(outs),
        compiler_params=params(),
    )(tie_map, x_own, y, dh, d_resid, vectors, f_sum, q_sum, small_sum)
    grads = list(final[2:])
    for index in (2, 5, 9):
        grads[index] = turned(grads[index])
    return (final[0][None], final[1][None]) + tuple(grads)


def fits_grouped(mesh, block_input, span_place, qkv_weight):
    width = qkv_weight.shape[1]
    rows = block_input.shape[2] // mesh.shape["ctx"]
    total = mesh.shape["ctx"] * mesh.shape["dp"]
    return (
        mesh.shape["ctx"] == 8
        and block_input.shape[1] == 2
        and HEADS % 4 == 0
        and HEADS * HD == width
        and rows % 16 == 0
        and block_input.shape[2] % KCOLS == 0
        and width % total == 0
        and (width // total) % 8 == 0
        and (width // 4) % (2 * (width // total)) == 0
    )


def solution(mesh):
    replicated_rows = P("dp", None, "ctx", None)
    vector = P(None, ("dp", "ctx"))
    columns = P(None, None, ("dp", "ctx"))
    bank_specs = (
        vector,
        vector,
        columns,
        vector,
        vector,
        columns,
        vector,
        vector,
        vector,
        columns,
        vector,
        P(None, ("dp", "ctx"), None),
        vector,
    )

    def step(*args):
        if fits_grouped(mesh, args[0], args[4], args[7]):
            plan = functools.partial(grouped_plan, mesh.shape["dp"])
        else:
            plan = general_plan
        return jax.shard_map(
            plan,
            mesh=mesh,
            in_specs=(
                replicated_rows,
                replicated_rows,
                P(),
                P("dp", None, None),
                P("dp", None, None),
            )
            + bank_specs,
            out_specs=(replicated_rows, replicated_rows) + bank_specs,
            check_vma=False,
        )(*args)

    return step
```

```python
import functools
import math
import types

import jax
import jax.numpy as jnp
from jax import lax
from jax.experimental import pallas as pl
from jax.experimental.pallas import tpu as pltpu
from jax.sharding import PartitionSpec as P

HEADS = 12
HD = 64


epsilon = 1e-05
masked_score = -1e30
score_scale = 0.125
key_block = 1024


def layer_norm(inputs, norm_gain, norm_shift):
    average = jnp.mean(inputs, axis=-1, keepdims=True)
    centered = inputs - average
    variance = jnp.mean(centered * centered, axis=-1, keepdims=True)
    return centered * lax.rsqrt(variance + epsilon) * norm_gain + norm_shift


def gelu_tanh(inputs):
    return jax.nn.gelu(inputs, approximate=True)


def stream_positions(row_index, span_row, rows_each):
    owner_lane = row_index // rows_each
    lane_ids = jnp.arange(span_row.shape[0], dtype=jnp.int32)
    span_ids = jnp.sum(
        jnp.where(owner_lane[:, None] == lane_ids[None, :], span_row[None, :], 0), axis=1
    )
    return span_ids * rows_each + row_index % rows_each


def segment_ids(positions, seq_ends):
    return jnp.sum((positions[:, None] >= seq_ends[None, :]).astype(jnp.int32), axis=1)


def over_blocks(step_fn, state, pieces):
    piece_rows = pieces[0].shape[0]
    block_rows = math.gcd(piece_rows, key_block)
    stacked = tuple(
        (
            member.reshape((piece_rows // block_rows, block_rows) + member.shape[1:])
            for member in pieces
        )
    )

    def inner_step(running, scan_item):
        block_index, sliced = scan_item
        return (step_fn(running, sliced, block_index * block_rows), None)

    finished, ignored = lax.scan(
        inner_step, state, (jnp.arange(piece_rows // block_rows, dtype=jnp.int32), stacked)
    )
    return finished


def score_probs(
    query_heads,
    grad_heads,
    lse_heads,
    delta_heads,
    query_pos,
    query_seg,
    key_heads,
    value_heads,
    key_pos,
    key_seg,
):
    allowed = (query_seg[:, None] == key_seg[None, :]) & (key_pos[None, :] <= query_pos[:, None])
    scores = (
        jnp.einsum("qhd,khd->hqk", query_heads, key_heads, preferred_element_type=jnp.float32)
        * score_scale
    )
    probs = jnp.where(allowed[None], jnp.exp(scores - lse_heads[:, :, None]), 0.0)
    dprobs = jnp.einsum("qhd,khd->hqk", grad_heads, value_heads, preferred_element_type=jnp.float32)
    dscores = (probs * (dprobs - delta_heads[:, :, None])).astype(jnp.bfloat16)
    return (probs.astype(jnp.bfloat16), dscores)


def general_plan(
    block_input,
    cotangent,
    tie_map,
    seq_lengths,
    span_place,
    first_gain,
    first_shift,
    qkv_weight,
    query_bias,
    value_bias,
    out_weight,
    out_bias,
    second_gain,
    second_shift,
    up_weight,
    up_bias,
    down_weight,
    down_bias,
):
    banks = (
        first_gain,
        first_shift,
        qkv_weight,
        query_bias,
        value_bias,
        out_weight,
        out_bias,
        second_gain,
        second_shift,
        up_weight,
        up_bias,
        down_weight,
        down_bias,
    )
    shards = tuple(
        (
            lax.dynamic_index_in_dim(weight_bank, tie_map[bank_number], 0, keepdims=False)
            for bank_number, weight_bank in enumerate(banks)
        )
    )
    micro_count = block_input.shape[1]
    row_count = block_input.shape[2]
    model_width = block_input.shape[3]
    ctx_index = lax.axis_index("ctx")
    local_rows = ctx_index * row_count + jnp.arange(row_count, dtype=jnp.int32)
    totals = None
    outputs = []
    input_grads = []
    for micro_step in range(micro_count):
        params = (
            lax.all_gather(shards[0], ("dp", "ctx"), axis=0, tiled=True),
            lax.all_gather(shards[1], ("dp", "ctx"), axis=0, tiled=True),
            lax.all_gather(shards[2], ("dp", "ctx"), axis=1, tiled=True),
            lax.all_gather(shards[3], ("dp", "ctx"), axis=0, tiled=True),
            lax.all_gather(shards[4], ("dp", "ctx"), axis=0, tiled=True),
            lax.all_gather(shards[5], ("dp", "ctx"), axis=1, tiled=True),
            lax.all_gather(shards[6], ("dp", "ctx"), axis=0, tiled=True),
            lax.all_gather(shards[7], ("dp", "ctx"), axis=0, tiled=True),
            lax.all_gather(shards[8], ("dp", "ctx"), axis=0, tiled=True),
            lax.all_gather(shards[9], ("dp", "ctx"), axis=1, tiled=True),
            lax.all_gather(shards[10], ("dp", "ctx"), axis=0, tiled=True),
            lax.all_gather(shards[11], ("dp", "ctx"), axis=0, tiled=True),
            lax.all_gather(shards[12], ("dp", "ctx"), axis=0, tiled=True),
        )
        (
            gain_before,
            shift_before,
            qkv_full,
            query_add,
            value_add,
            out_full,
            out_add,
            gain_after,
            shift_after,
            up_full,
            up_add,
            down_full,
            down_add,
        ) = params
        span_row = span_place[0, micro_step]
        seq_ends = jnp.cumsum(seq_lengths[0, micro_step])
        query_pos = stream_positions(local_rows, span_row, row_count)
        query_seg = segment_ids(query_pos, seq_ends)
        inputs_wide = block_input[0, micro_step].astype(jnp.float32)
        first_norm = layer_norm(
            inputs_wide, gain_before.astype(jnp.float32), shift_before.astype(jnp.float32)
        ).astype(jnp.bfloat16)
        projected = jnp.dot(first_norm, qkv_full, preferred_element_type=jnp.float32)
        queries = (projected[:, :model_width] + query_add.astype(jnp.float32)).astype(jnp.bfloat16)
        key_rows = projected[:, model_width : 2 * model_width].astype(jnp.bfloat16)
        value_rows = (projected[:, 2 * model_width :] + value_add.astype(jnp.float32)).astype(
            jnp.bfloat16
        )
        query_heads = queries.reshape(row_count, HEADS, HD)
        key_heads_own = key_rows.reshape(row_count, HEADS, HD)
        value_heads_own = value_rows.reshape(row_count, HEADS, HD)

        def attend(state, pieces, offset):
            row_max, row_sum, accumulated = state
            key_part, value_part = pieces
            piece_rows = key_part.shape[0]
            key_pos = stream_positions(
                offset + jnp.arange(piece_rows, dtype=jnp.int32), span_row, row_count
            )
            key_seg = segment_ids(key_pos, seq_ends)
            allowed = (query_seg[:, None] == key_seg[None, :]) & (
                key_pos[None, :] <= query_pos[:, None]
            )
            scores = (
                jnp.einsum(
                    "qhd,khd->hqk",
                    query_heads,
                    key_part.reshape(piece_rows, HEADS, HD),
                    preferred_element_type=jnp.float32,
                )
                * score_scale
            )
            scores = jnp.where(allowed[None], scores, masked_score)
            new_max = jnp.maximum(row_max, jnp.max(scores, axis=2))
            exp_scores = jnp.where(allowed[None], jnp.exp(scores - new_max[:, :, None]), 0.0)
            factor = jnp.exp(row_max - new_max)
            row_sum = row_sum * factor + jnp.sum(exp_scores, axis=2)
            accumulated = accumulated * factor.T[:, :, None] + jnp.einsum(
                "hqk,khd->qhd",
                exp_scores.astype(jnp.bfloat16),
                value_part.reshape(piece_rows, HEADS, HD),
                preferred_element_type=jnp.float32,
            )
            return (new_max, row_sum, accumulated)

        start_state = (
            jnp.full((HEADS, row_count), masked_score, jnp.float32),
            jnp.zeros((HEADS, row_count), jnp.float32),
            jnp.zeros((row_count, HEADS, HD), jnp.float32),
        )
        row_max, row_sum, accumulated = over_blocks(
            attend,
            start_state,
            (
                lax.all_gather(key_rows, "ctx", axis=0, tiled=True),
                lax.all_gather(value_rows, "ctx", axis=0, tiled=True),
            ),
        )
        attended_wide = accumulated / row_sum.T[:, :, None]
        log_sums = row_max + jnp.log(row_sum)
        attended = attended_wide.reshape(row_count, model_width).astype(jnp.bfloat16)
        mixed_out = jnp.dot(
            attended, out_full, preferred_element_type=jnp.float32
        ) + out_add.astype(jnp.float32)
        residual = inputs_wide + mixed_out
        second_norm = layer_norm(
            residual, gain_after.astype(jnp.float32), shift_after.astype(jnp.float32)
        ).astype(jnp.bfloat16)
        up_proj = jnp.dot(second_norm, up_full, preferred_element_type=jnp.float32) + up_add.astype(
            jnp.float32
        )
        activated = gelu_tanh(up_proj).astype(jnp.bfloat16)
        down_proj = jnp.dot(
            activated, down_full, preferred_element_type=jnp.float32
        ) + down_add.astype(jnp.float32)
        outputs.append((residual + down_proj).astype(jnp.bfloat16))
        params = (
            lax.all_gather(shards[0], ("dp", "ctx"), axis=0, tiled=True),
            lax.all_gather(shards[1], ("dp", "ctx"), axis=0, tiled=True),
            lax.all_gather(shards[2], ("dp", "ctx"), axis=1, tiled=True),
            lax.all_gather(shards[3], ("dp", "ctx"), axis=0, tiled=True),
            lax.all_gather(shards[4], ("dp", "ctx"), axis=0, tiled=True),
            lax.all_gather(shards[5], ("dp", "ctx"), axis=1, tiled=True),
            lax.all_gather(shards[6], ("dp", "ctx"), axis=0, tiled=True),
            lax.all_gather(shards[7], ("dp", "ctx"), axis=0, tiled=True),
            lax.all_gather(shards[8], ("dp", "ctx"), axis=0, tiled=True),
            lax.all_gather(shards[9], ("dp", "ctx"), axis=1, tiled=True),
            lax.all_gather(shards[10], ("dp", "ctx"), axis=0, tiled=True),
            lax.all_gather(shards[11], ("dp", "ctx"), axis=0, tiled=True),
            lax.all_gather(shards[12], ("dp", "ctx"), axis=0, tiled=True),
        )
        (
            gain_before,
            shift_before,
            qkv_full,
            query_add,
            value_add,
            out_full,
            out_add,
            gain_after,
            shift_after,
            up_full,
            up_add,
            down_full,
            down_add,
        ) = params
        grad_out = cotangent[0, micro_step].astype(jnp.float32)
        grad_down = grad_out.astype(jnp.bfloat16)
        down_weight_grad = jnp.einsum(
            "rf,rd->fd", activated, grad_down, preferred_element_type=jnp.float32
        )
        down_bias_grad = jnp.sum(grad_down.astype(jnp.float32), axis=0)
        grad_act = jnp.einsum("rd,fd->rf", grad_down, down_full, preferred_element_type=jnp.float32)
        unused_gelu, gelu_back = jax.vjp(gelu_tanh, up_proj)
        grad_up = gelu_back(grad_act)[0].astype(jnp.bfloat16)
        up_weight_grad = jnp.einsum(
            "rd,rf->df", second_norm, grad_up, preferred_element_type=jnp.float32
        )
        up_bias_grad = jnp.sum(grad_up.astype(jnp.float32), axis=0)
        grad_second = jnp.einsum("rf,df->rd", grad_up, up_full, preferred_element_type=jnp.float32)
        unused_second, second_back = jax.vjp(
            layer_norm, residual, gain_after.astype(jnp.float32), shift_after.astype(jnp.float32)
        )
        grad_resid, second_gain_grad, second_shift_grad = second_back(grad_second)
        grad_resid = grad_resid + grad_out
        grad_mixed = grad_resid.astype(jnp.bfloat16)
        out_weight_grad = jnp.einsum(
            "rc,rd->cd", attended, grad_mixed, preferred_element_type=jnp.float32
        )
        out_bias_grad = jnp.sum(grad_mixed.astype(jnp.float32), axis=0)
        grad_attended = jnp.einsum(
            "rd,cd->rc", grad_mixed, out_full, preferred_element_type=jnp.float32
        ).astype(jnp.bfloat16)
        grad_heads = grad_attended.reshape(row_count, HEADS, HD)
        delta_rows = jnp.sum(grad_heads.astype(jnp.float32) * attended_wide, axis=2)
        delta_heads = delta_rows.T
        empty_heads = jnp.zeros((row_count, HEADS, HD), jnp.float32)
        stats_whole = (
            lax.all_gather(log_sums.T, "ctx", axis=0, tiled=True),
            lax.all_gather(delta_rows, "ctx", axis=0, tiled=True),
        )

        def mutual(state, pieces, offset):
            grad_query, grad_key, grad_value = state
            key_part, value_part, query_part, gradout_part = pieces
            piece_rows = key_part.shape[0]
            lse_part = lax.dynamic_slice_in_dim(stats_whole[0], offset, piece_rows, 0)
            delta_part = lax.dynamic_slice_in_dim(stats_whole[1], offset, piece_rows, 0)
            key_pos = stream_positions(
                offset + jnp.arange(piece_rows, dtype=jnp.int32), span_row, row_count
            )
            key_seg = segment_ids(key_pos, seq_ends)
            key_part_heads = key_part.reshape(piece_rows, HEADS, HD)
            value_part_heads = value_part.reshape(piece_rows, HEADS, HD)
            query_part_heads = query_part.reshape(piece_rows, HEADS, HD)
            gradout_heads = gradout_part.reshape(piece_rows, HEADS, HD)
            probs, dscores = score_probs(
                query_heads,
                grad_heads,
                log_sums,
                delta_heads,
                query_pos,
                query_seg,
                key_part_heads,
                value_part_heads,
                key_pos,
                key_seg,
            )
            grad_query = grad_query + score_scale * jnp.einsum(
                "hqk,khd->qhd", dscores, key_part_heads, preferred_element_type=jnp.float32
            )
            probs_other, dscores_other = score_probs(
                query_part_heads,
                gradout_heads,
                lse_part.T,
                delta_part.T,
                key_pos,
                key_seg,
                key_heads_own,
                value_heads_own,
                query_pos,
                query_seg,
            )
            grad_key = grad_key + score_scale * jnp.einsum(
                "hqk,qhd->khd", dscores_other, query_part_heads, preferred_element_type=jnp.float32
            )
            grad_value = grad_value + jnp.einsum(
                "hqk,qhd->khd", probs_other, gradout_heads, preferred_element_type=jnp.float32
            )
            return (grad_query, grad_key, grad_value)

        grad_query, grad_key, grad_value = over_blocks(
            mutual,
            (empty_heads, empty_heads, empty_heads),
            (
                lax.all_gather(key_rows, "ctx", axis=0, tiled=True),
                lax.all_gather(value_rows, "ctx", axis=0, tiled=True),
                lax.all_gather(queries, "ctx", axis=0, tiled=True),
                lax.all_gather(grad_attended, "ctx", axis=0, tiled=True),
            ),
        )
        grad_proj = jnp.concatenate(
            [
                grad_query.reshape(row_count, model_width),
                grad_key.reshape(row_count, model_width),
                grad_value.reshape(row_count, model_width),
            ],
            axis=1,
        ).astype(jnp.bfloat16)
        qkv_weight_grad = jnp.einsum(
            "rc,rp->cp", first_norm, grad_proj, preferred_element_type=jnp.float32
        )
        query_bias_grad = jnp.sum(grad_proj[:, :model_width].astype(jnp.float32), axis=0)
        value_bias_grad = jnp.sum(grad_proj[:, 2 * model_width :].astype(jnp.float32), axis=0)
        grad_first = jnp.einsum(
            "rp,cp->rc", grad_proj, qkv_full, preferred_element_type=jnp.float32
        )
        unused_first, first_back = jax.vjp(
            layer_norm,
            inputs_wide,
            gain_before.astype(jnp.float32),
            shift_before.astype(jnp.float32),
        )
        grad_input, first_gain_grad, first_shift_grad = first_back(grad_first)
        input_grads.append((grad_input + grad_resid).astype(jnp.bfloat16))
        micro_grads = (
            first_gain_grad,
            first_shift_grad,
            qkv_weight_grad,
            query_bias_grad,
            value_bias_grad,
            out_weight_grad,
            out_bias_grad,
            second_gain_grad,
            second_shift_grad,
            up_weight_grad,
            up_bias_grad,
            down_weight_grad,
            down_bias_grad,
        )
        if totals is None:
            totals = micro_grads
        else:
            totals = tuple(
                (left_sum + right_sum for left_sum, right_sum in zip(totals, micro_grads))
            )
    owned = (
        lax.psum_scatter(totals[0], ("dp", "ctx"), scatter_dimension=0, tiled=True),
        lax.psum_scatter(totals[1], ("dp", "ctx"), scatter_dimension=0, tiled=True),
        lax.psum_scatter(totals[2], ("dp", "ctx"), scatter_dimension=1, tiled=True),
        lax.psum_scatter(totals[3], ("dp", "ctx"), scatter_dimension=0, tiled=True),
        lax.psum_scatter(totals[4], ("dp", "ctx"), scatter_dimension=0, tiled=True),
        lax.psum_scatter(totals[5], ("dp", "ctx"), scatter_dimension=1, tiled=True),
        lax.psum_scatter(totals[6], ("dp", "ctx"), scatter_dimension=0, tiled=True),
        lax.psum_scatter(totals[7], ("dp", "ctx"), scatter_dimension=0, tiled=True),
        lax.psum_scatter(totals[8], ("dp", "ctx"), scatter_dimension=0, tiled=True),
        lax.psum_scatter(totals[9], ("dp", "ctx"), scatter_dimension=1, tiled=True),
        lax.psum_scatter(totals[10], ("dp", "ctx"), scatter_dimension=0, tiled=True),
        lax.psum_scatter(totals[11], ("dp", "ctx"), scatter_dimension=0, tiled=True),
        lax.psum_scatter(totals[12], ("dp", "ctx"), scatter_dimension=0, tiled=True),
    )
    bank_grads = tuple(
        (
            lax.dynamic_update_index_in_dim(
                jnp.zeros(weight_bank.shape, jnp.float32), owned_piece, tie_map[bank_number], 0
            )
            for bank_number, (weight_bank, owned_piece) in enumerate(zip(banks, owned))
        )
    )
    block_output = jnp.stack(outputs)[None]
    input_grad = jnp.stack(input_grads)[None]
    return (block_output, input_grad) + bank_grads


BF = jnp.bfloat16
F32 = jnp.float32
MESH = pl.DeviceIdType.MESH
ANY = pl.ANY
SMALL = 8
VMEM_BYTES = 62 * 2**20


def params(collective_id=None):
    if collective_id is None:
        return pltpu.CompilerParams(vmem_limit_bytes=VMEM_BYTES)
    return pltpu.CompilerParams(
        vmem_limit_bytes=VMEM_BYTES, collective_id=collective_id, has_side_effects=True
    )


def vmem():
    return pl.BlockSpec(memory_space=pltpu.VMEM)


def smem():
    return pl.BlockSpec(memory_space=pltpu.SMEM)


def anywhere():
    return pl.BlockSpec(memory_space=ANY)


def shape(dims, dtype):
    return jax.ShapeDtypeStruct(dims, dtype)


def nn(left, right):
    return lax.dot_general(left, right, (((1,), (0,)), ((), ())), preferred_element_type=F32)


def nt(left, right):
    return lax.dot_general(left, right, (((1,), (1,)), ((), ())), preferred_element_type=F32)


def tn(left, right):
    return lax.dot_general(left, right, (((0,), (0,)), ((), ())), preferred_element_type=F32)


def iota(dims, axis):
    return lax.broadcasted_iota(jnp.int32, dims, axis)


class Place:
    def __init__(self, depth):
        self.depth = depth
        self.z = lax.axis_index("dp")
        self.r = lax.axis_index("ctx")
        self.core = self.r % 2
        self.j = self.r // 2
        self.a = self.r // 4
        self.b = (self.r // 2) % 2
        self.by_a = (1 - self.a) * 4 + self.b * 2 + self.core
        self.by_b = self.a * 4 + (1 - self.b) * 2 + self.core
        self.both = (1 - self.a) * 4 + (1 - self.b) * 2 + self.core
        self.mate = self.j * 2 + 1 - self.core

    def slot(self, z, r):
        return z * 8 + r


def greet_all(here):
    bar = pltpu.get_barrier_semaphore()
    total = here.depth * 8
    me = here.z * 8 + here.r

    def signal(k, carry):
        other = (me + k) % total
        pl.semaphore_signal(bar, inc=1, device_id=(other // 8, other % 8), device_id_type=MESH)
        return carry

    lax.fori_loop(1, total, signal, 0)
    pl.semaphore_wait(bar, total - 1)


def remote(source, target, send, recv, z, r):
    return pltpu.make_async_remote_copy(
        src_ref=source,
        dst_ref=target,
        send_sem=send,
        recv_sem=recv,
        device_id=(z, r),
        device_id_type=MESH,
    )


def spread_units(small, width, hidden_total):
    devices = small.shape[0]
    unit = width // devices
    per = hidden_total // devices
    flat = small.reshape(devices * SMALL, 256)
    lane = iota((128, width), 1)
    pick = (lane % unit == iota((128, width), 0)).astype(F32).astype(BF)
    tall = nn(flat[:, 0:128], pick)
    row = iota((devices * SMALL, width), 0)
    col = iota((devices * SMALL, width), 1)
    tall = jnp.where(col // unit == row // SMALL, tall, 0.0)
    vectors = jnp.sum(tall.reshape(devices, SMALL, width), axis=0)
    chosen = (
        (iota((devices, devices * SMALL), 1) == iota((devices, devices * SMALL), 0) * SMALL)
        .astype(F32)
        .astype(BF)
    )
    firsts = nn(chosen, flat[:, 128:256]).astype(BF)
    lane = iota((128, hidden_total), 1)
    pick = (lane % per == iota((128, hidden_total), 0)).astype(F32).astype(BF)
    wide = nn(firsts, pick)
    keep = iota((devices, hidden_total), 1) // per == iota((devices, hidden_total), 0)
    return vectors, jnp.sum(jnp.where(keep, wide, 0.0), axis=0, keepdims=True)


def gather_units(vectors, hidden_row, devices):
    width = vectors.shape[1]
    hidden_total = hidden_row.shape[1]
    unit = width // devices
    per = hidden_total // devices
    tall = jnp.broadcast_to(vectors[None], (devices, SMALL, width)).reshape(devices * SMALL, width)
    row = iota((devices * SMALL, width), 0)
    col = iota((devices * SMALL, width), 1)
    tall = jnp.where(col // unit == row // SMALL, tall, 0.0).astype(BF)
    pick = (iota((width, 128), 0) % unit == iota((width, 128), 1)).astype(F32).astype(BF)
    left = nn(tall, pick)
    wide = jnp.broadcast_to(hidden_row, (devices, hidden_total))
    keep = iota((devices, hidden_total), 1) // per == iota((devices, hidden_total), 0)
    wide = jnp.where(keep, wide, 0.0).astype(BF)
    pick = (iota((hidden_total, 128), 0) % per == iota((hidden_total, 128), 1)).astype(F32)
    firsts = nn(wide, pick.astype(BF)).astype(BF)
    chosen = (
        iota((devices * SMALL, devices), 0) == iota((devices * SMALL, devices), 1) * SMALL
    ).astype(F32).astype(BF)
    right = nn(chosen, firsts)
    return (
        left.astype(BF).reshape(devices, SMALL, 128),
        right.astype(BF).reshape(devices, SMALL, 128),
    )


def group_slice(row, j, groups):
    width = row.shape[1] // groups
    out = jnp.zeros((1, width), F32)
    for g in range(groups):
        out = jnp.where(j == g, row[:, g * width : (g + 1) * width], out)
    return out


def group_spread(part, j, groups):
    return jnp.concatenate([jnp.where(j == g, part, 0.0) for g in range(groups)], axis=1)


def block_at(place_ref, micro, position, blocks):
    found = jnp.int32(0)
    for s in range(blocks):
        found = jnp.where(place_ref[0, micro, s] == position, s, found)
    return found


def stack_heads(rows, heads):
    lane = iota(rows.shape, 1) // HD
    zero = jnp.zeros_like(rows)
    return jnp.concatenate([jnp.where(lane == h, rows, zero) for h in range(heads)], axis=0)


def unstack_heads(tall, heads):
    rows = tall.shape[0] // heads
    lane = iota((rows, tall.shape[1]), 1) // HD
    out = tall[0:rows]
    for h in range(1, heads):
        out = jnp.where(lane == h, tall[h * rows : (h + 1) * rows], out)
    return out


def visible_bias(lens, micro, start, rows, key_start, keys):
    query = start + iota((rows, 1), 0)
    begin = jnp.zeros((rows, 1), jnp.int32)
    end = jnp.int32(0)
    for s in range(lens.shape[2]):
        end = end + lens[0, micro, s]
        begin = jnp.where(query >= end, end, begin)
    key = key_start + iota((rows, keys), 1)
    return jnp.where((key >= begin) & (key <= query), 0.0, masked_score)


def row_norm(wide):
    average = jnp.mean(wide, axis=-1, keepdims=True)
    centered = wide - average
    variance = jnp.mean(centered * centered, axis=-1, keepdims=True)
    scale = lax.rsqrt(variance + epsilon)
    return centered * scale, scale


def norm_back(grad, unit, scale):
    first = jnp.mean(grad, axis=-1, keepdims=True)
    second = jnp.mean(grad * unit, axis=-1, keepdims=True)
    return (grad - first - unit * second) * scale


QROWS = 128
KCOLS = 384
GELU_A = math.sqrt(2.0 / math.pi)
GELU_B = 0.044715


class Sizes:
    def __init__(self, depth, rows, width, hidden_total):
        self.depth = depth
        self.rows = rows
        self.width = width
        self.total = depth * 8
        self.unit = width // self.total
        self.per = hidden_total // self.total
        self.group = width // 4
        self.heads = self.group // HD
        self.pack = 8 * rows
        self.packed = self.unit + 2 * self.per
        self.units = self.group // self.unit
        cut = self.per - 8
        self.parts = (
            (0, self.unit, "b"),
            (self.unit, cut, "b"),
            (self.unit + cut, 2 * self.per - cut, "a"),
        )


def block_scratch(n):
    vm = lambda dims, dtype=BF: pltpu.VMEM(dims, dtype)
    dma = lambda dims: pltpu.SemaphoreType.DMA(dims)
    d, w, g, pack, rows = n.depth, n.width, n.group, n.pack, n.rows
    p = len(n.parts)
    both = 2 * rows
    halves = 2 * d
    chunk = n.per * 4
    return {
        "f_all": vm((n.total, n.packed, w)),
        "gr": vm((d, 2, 2, 2, n.packed, w)),
        "from_mate": vm((d, 2, 2, n.packed, w)),
        "from_one": vm((d, 2, n.packed, w)),
        "from_two": vm((d, n.packed, w)),
        "from_z": vm((d, n.packed, w)),
        "q_own": vm((3, n.unit, w)),
        "wts": vm((3, n.units, n.unit, w)),
        "small_all": vm((n.total, SMALL, 256)),
        "x_all": vm((2, 2, 2, rows, w)),
        "h": vm((pack, w)),
        "u": vm((pack, w)),
        "qkv": vm((3, pack, g)),
        "o": vm((pack, -(-(g + n.heads) // 128) * 128), F32),
        "vec": vm((SMALL, w), F32),
        "hid": vm((halves, 1, chunk), F32),
        "hid_grad": vm((halves, 1, chunk), F32),
        "stage": vm((8, rows, g)),
        "at_recv": vm((8, rows, g)),
        "da_recv": vm((8, rows, g)),
        "resid": vm((both, w), F32),
        "unit2": vm((both, w), F32),
        "h2": vm((both, w)),
        "scale2": vm((both, 1), F32),
        "vec_grad": vm((SMALL, w), F32),
        "da": vm((pack, g)),
        "dk_acc": vm((pack, g), F32),
        "dv_acc": vm((pack, g), F32),
        "gq": vm((3, n.units // 2, 2, n.unit, w)),
        "q_mate": vm((3, n.units // 2, n.unit, w)),
        "q_line": vm((3, d, n.unit, w)),
        "dh_a1": vm((2, rows, w)),
        "dh_b1": vm((2, rows, w)),
        "dh_a2": vm((rows, w)),
        "dh_b2": vm((rows, w)),
        "dh_mate": vm((rows, w)),
        "sums": vm((SMALL, w), F32),
        "sg": vm((n.total, SMALL, 256)),
        "sg_recv": vm((n.total, SMALL, 256)),
        "s_zsend": dma((p, d)),
        "s_zrecv": dma((p, d)),
        "s_send1": dma((p, d)),
        "s_recv1": dma((p, d)),
        "s_send2": dma((p, d, 2)),
        "s_recv2": dma((p, d, 2)),
        "s_csend": dma((p, d, 4)),
        "s_crecv": dma((p, d, 4)),
        "s_xsend": dma((7,)),
        "s_xrecv": dma((8,)),
        "s_qsend": dma((3, d)),
        "s_qrecv": dma((3, n.units)),
        "s_qcsend": dma((3, n.units)),
        "s_smsend": dma((n.total,)),
        "s_smrecv": dma((n.total,)),
        "s_asend": dma((8,)),
        "s_arecv": dma((8,)),
        "s_dsend": dma((8,)),
        "s_drecv": dma((8,)),
        "s_rcs": dma((p, d)),
        "s_rcr": dma((p, d)),
        "s_r1s": dma((p, d)),
        "s_r1r": dma((p, d)),
        "s_r2s": dma((p, d)),
        "s_r2r": dma((p, d)),
        "s_rzs": dma((p, d)),
        "s_rzr": dma((p, d)),
        "s_gqc": dma((2,)),
        "s_gqs": dma((3, n.units // 2)),
        "s_gqr": dma((3, d)),
        "s_dhs": dma((5,)),
        "s_dhr": dma((5,)),
        "s_sgs": dma((n.total,)),
        "s_sgr": dma((n.total,)),
    }


def add_into(target, source):
    target[...] = (target[...].astype(F32) + source[...].astype(F32)).astype(BF)


def block_kernel(n, names, tie, lens, spans, x_ref, dy_ref, *refs):
    banks = refs[:13]
    y_out, dr_out, dh_out, f_sum, q_sum, small_sum, vec_out = refs[13:20]
    s = types.SimpleNamespace(**dict(zip(names, refs[20:])))
    g1, s1, wq, bq, bv, wo, bo, g2, s2, wu, bu, wd, bd = banks
    depth, unit, per, rows, width, group, heads = (
        n.depth, n.unit, n.per, n.rows, n.width, n.group, n.heads
    )
    here = Place(depth)
    z, r, a, b, core, j = here.z, here.r, here.a, here.b, here.core, here.j
    me = here.slot(z, r)
    micro = core
    mate, by_a, by_b, both = here.mate, here.by_a, here.by_b, here.both
    parts = n.parts
    main = (1, 2)
    groups = 4

    bar = pltpu.get_barrier_semaphore()

    def signal(k, carry):
        other = (me + k) % n.total
        pl.semaphore_signal(bar, inc=1, device_id=(other // 8, other % 8), device_id_type=MESH)
        return carry

    lax.fori_loop(1, n.total, signal, 0)

    f_own = s.f_all.at[me]
    f_own[0:unit, :] = wo[tie[5]]
    f_own[unit : unit + per, :] = wu[tie[9]]
    f_own[unit + per :, :] = wd[tie[11]]
    s.q_own[...] = wq[tie[2]].reshape(3, unit, width)
    chosen_rows = []
    for bank, index in ((g1, 0), (s1, 1), (bq, 3), (bv, 4), (bo, 6), (g2, 7), (s2, 8), (bd, 12)):
        wide = bank[...].astype(F32)
        chosen = jnp.zeros((1, unit), F32)
        for layer in range(bank.shape[0]):
            chosen = jnp.where(tie[index] == layer, wide[layer : layer + 1, :], chosen)
        chosen_rows.append(chosen)
    small_own = s.small_all.at[me]
    small_own[...] = jnp.zeros((SMALL, 256), BF)
    small_own[:, 0:unit] = jnp.concatenate(chosen_rows, axis=0).astype(BF)
    wide = bu[...].astype(F32)
    chosen = jnp.zeros((1, per), F32)
    for layer in range(bu.shape[0]):
        chosen = jnp.where(tie[10] == layer, wide[layer : layer + 1, :], chosen)
    tall = jnp.concatenate([chosen, jnp.zeros((SMALL - 1, per), F32)], axis=0)
    small_own[:, 128 : 128 + per] = tall.astype(BF)

    pl.semaphore_wait(bar, n.total - 1)

    def to_all(buffer_of, send, recv, target):
        def go(k, carry):
            other = (me + k) % n.total
            remote(
                buffer_of(other), target.at[me], send.at[other], recv.at[me], other // 8, other % 8
            ).start()
            return carry

        lax.fori_loop(1, n.total, go, 0)

    def from_all(buffer, send, recv, target):
        def go(k, carry):
            other = (me + k) % n.total
            remote(
                buffer, target.at[other], send.at[other], recv.at[other], other // 8, other % 8
            ).wait()
            return carry

        lax.fori_loop(1, n.total, go, 0)

    def row_block(block):
        return s.x_all.at[block // 4, (block // 2) % 2, block % 2]

    def row_move(source, block, lane, to):
        return remote(source, row_block(block), s.s_xsend.at[lane], s.s_xrecv.at[block], z, to)

    mate_a = by_a + 1 - 2 * core
    row_move(x_ref.at[1 - core], r, 0, mate).start()
    row_move(x_ref.at[core], r, 1, by_b).start()
    row_move(x_ref.at[core], r, 2, by_a).start()
    to_all(lambda other: small_own, s.s_smsend, s.s_smrecv, s.small_all)
    row_block(r)[...] = x_ref[core]

    def q_unit(t):
        block = me * 3 + t
        kind = block // n.total
        inside = block % n.total
        return kind, inside // n.units, inside % n.units

    def q_first(t, zz):
        kind, chip, at = q_unit(t)
        to = chip * 2 + core
        source, target, recv = s.q_own.at[t], s.wts.at[kind, at], s.s_qrecv.at[kind, at]
        go = lambda: remote(source, target, s.s_qsend.at[t, zz], recv, zz, to)
        stay = lambda: pltpu.make_async_copy(source, target, recv)
        return go, stay, (zz == z) & (to == r)

    for t in range(3):
        for zz in range(depth):
            go, stay, mine = q_first(t, zz)

            @pl.when(jnp.logical_not(mine))
            def _():
                go().start()

            @pl.when(mine)
            def _():
                stay().start()

    def order(k):
        out = jnp.int32(0)
        for zz in range(depth):
            line = sorted(range(depth), key=lambda t: (abs(t - zz), t))
            for kk in range(depth):
                out = jnp.where((z == zz) & (k == kk), line[kk], out)
        return out

    def move(p, zz, rr, send, recv, to_z, to_r):
        start, count, _ = parts[p]
        ref = s.f_all.at[here.slot(zz, rr), pl.ds(start, count)]
        return remote(ref, ref, send, recv, to_z, to_r)

    def first_axis(p):
        return by_b if parts[p][2] == "b" else by_a

    def second_axis(p):
        return by_a if parts[p][2] == "b" else by_b

    def line_move(p, o, to_z):
        return move(p, o, r, s.s_zsend.at[p, to_z], s.s_zrecv.at[p, o], to_z, r)

    def one(p, o):
        return move(p, o, r, s.s_send1.at[p, o], s.s_recv1.at[p, o], z, first_axis(p))

    def two(p, o, rr, lane):
        return move(
            p, o, rr, s.s_send2.at[p, o, lane], s.s_recv2.at[p, o, lane], z, second_axis(p)
        )

    def across(p, o, rr, lane):
        return move(p, o, rr, s.s_csend.at[p, o, lane], s.s_crecv.at[p, o, lane], z, mate)

    every = range(len(parts))
    for p in every:
        for k in range(1, depth):
            line_move(p, z, order(k)).start()

    def row_arrived(block):
        row_move(x_ref.at[0], block, 0, mate).wait_recv()

    row_arrived(mate)
    row_move(row_block(mate), mate, 3, by_a).start()
    row_move(row_block(mate), mate, 4, by_b).start()
    row_arrived(by_b)
    row_move(row_block(by_b), by_b, 5, by_a).start()
    row_arrived(mate_a)
    row_move(row_block(mate_a), mate_a, 6, by_b).start()

    def q_relay(e, carry):
        kind, at = e // n.units, e % n.units
        owner = (kind * n.total + j * n.units + at) // 3
        unit_ref = s.wts.at[kind, at]

        @pl.when(owner % 2 == core)
        def _():
            pltpu.make_async_copy(unit_ref, unit_ref, s.s_qrecv.at[kind, at]).wait()
            remote(
                unit_ref, unit_ref, s.s_qcsend.at[kind, at], s.s_qrecv.at[kind, at], z, mate
            ).start()

        return carry

    lax.fori_loop(0, 3 * n.units, q_relay, 0)

    def spread_own(p):
        one(p, z).start()
        two(p, z, r, 0).start()
        across(p, z, r, 0).start()

    for p in every:
        spread_own(p)

    from_all(small_own, s.s_smsend, s.s_smrecv, s.small_all)
    vectors, hidden = spread_units(s.small_all[...], width, per * n.total)
    s.vec[...] = vectors
    vec_out[...] = vectors
    chunk = 4 * per
    for c in range(2 * depth):
        s.hid[c] = hidden[:, c * chunk : (c + 1) * chunk]

    row_arrived(by_a)
    row_arrived(both)
    row_arrived(by_b + 1 - 2 * core)
    row_arrived(both + 1 - 2 * core)

    def q_rest(e, carry):
        kind, at = e // n.units, e % n.units
        owner = (kind * n.total + j * n.units + at) // 3
        unit_ref = s.wts.at[kind, at]

        @pl.when(owner % 2 != core)
        def _():
            remote(
                unit_ref, unit_ref, s.s_qcsend.at[kind, at], s.s_qrecv.at[kind, at], z, mate
            ).wait_recv()

        return carry

    lax.fori_loop(0, 3 * n.units, q_rest, 0)

    gain, shift = s.vec[0:1, :], s.vec[1:2, :]
    query_add = group_slice(s.vec[2:3, :], j, groups)
    value_add = group_slice(s.vec[3:4, :], j, groups)

    def weight(kind):
        return s.wts[kind].reshape(group, width)

    def project(p, carry):
        source = block_at(spans, micro, p, 8)
        unit_rows, _ = row_norm(
            s.x_all[source // 4, (source // 2) % 2, source % 2].astype(F32)
        )
        normed = (unit_rows * gain + shift).astype(BF)
        at = pl.ds(pl.multiple_of(p * rows, 16), rows)
        s.u[at, :] = unit_rows.astype(BF)
        s.h[at, :] = normed
        s.qkv[0, at, :] = (nt(normed, weight(0)) + query_add).astype(BF)
        s.qkv[1, at, :] = nt(normed, weight(1)).astype(BF)
        s.qkv[2, at, :] = (nt(normed, weight(2)) + value_add).astype(BF)
        return carry

    lax.fori_loop(0, 8, project, 0)

    def line_event(k, which):
        o = order(k)
        for p in which:
            line_move(p, o, z).wait_recv()
            one(p, o).start()
            two(p, o, r, 0).start()
            across(p, o, r, 0).start()

    def first_event(k, which):
        o = order(k)
        for p in which:
            one(p, o).wait_recv()
            two(p, o, first_axis(p), 1).start()
            across(p, o, first_axis(p), 1).start()

    def second_event(o, which):
        for p in which:
            two(p, o, r, 0).wait_recv()
            across(p, o, second_axis(p), 2).start()
            two(p, o, r, 1).wait_recv()
            across(p, o, both, 3).start()

    def all_here(o, which):
        for p in which:
            for lane in range(4):
                across(p, o, r, lane).wait_recv()

    gather_events = {
        0: [lambda: line_event(1, (0,)), lambda: first_event(0, (0,))],
        1: [lambda: line_event(2, (0,)), lambda: line_event(3, (0,))],
        2: [lambda: line_event(1, main)],
        3: [lambda: first_event(1, (0,)), lambda: first_event(0, main)],
        5: [lambda: first_event(2, (0,)), lambda: first_event(3, (0,))],
        6: [lambda: first_event(1, main)],
    }

    def run_events(events, i):
        for at, acts in events.items():

            @pl.when(i == at)
            def _(acts=acts):
                for act in acts:
                    act()

    tall = heads * QROWS
    q_blocks = n.pack // QROWS

    def attend(i, carry):
        start = pl.multiple_of(i * QROWS, QROWS)
        stacked = stack_heads(s.qkv[0, pl.ds(start, QROWS), :] * BF(score_scale), heads)

        def step(kc, state):
            top, total, acc = state
            at = pl.ds(pl.multiple_of(kc * KCOLS, KCOLS), KCOLS)
            bias = visible_bias(lens, micro, start, QROWS, kc * KCOLS, KCOLS)
            scores = nt(stacked, s.qkv[1, at, :])
            scores = (scores.reshape(heads, QROWS, KCOLS) + bias[None]).reshape(tall, KCOLS)
            new_top = jnp.maximum(top, jnp.max(scores, axis=1, keepdims=True))
            probs = jnp.exp(scores - new_top)
            factor = jnp.exp(top - new_top)
            total = total * factor + jnp.sum(probs, axis=1, keepdims=True)
            acc = acc * factor + nn(probs.astype(BF), s.qkv[2, at, :])
            return new_top, total, acc

        top, total, acc = lax.fori_loop(
            0,
            (i * QROWS) // KCOLS + 1,
            step,
            (
                jnp.full((tall, 1), masked_score, F32),
                jnp.zeros((tall, 1), F32),
                jnp.zeros((tall, group), F32),
            ),
        )
        at_q = pl.ds(start, QROWS)
        s.o[at_q, 0:group] = unstack_heads(acc / total, heads)
        lse = top + jnp.log(total)
        for head in range(heads):
            s.o[at_q, group + head : group + head + 1] = lse[head * QROWS : (head + 1) * QROWS]
        run_events(gather_events, i)
        return carry

    lax.fori_loop(0, q_blocks, attend, 0)

    for e in range(8):
        at = pl.ds(spans[0, micro, e] * rows, rows)
        s.stage[e] = s.o[at, 0:group].astype(BF)

    def exchange_start(stage, target, send, recv):
        for k in range(1, 8):
            to = (r + k) % 8
            remote(stage.at[to], target.at[r], send.at[to], recv.at[r], z, to).start()
        target[r] = stage[r]

    def exchange_wait(stage, target, send, recv):
        for k in range(1, 8):
            frm = (r + k) % 8
            remote(stage.at[frm], target.at[frm], send.at[frm], recv.at[frm], z, frm).wait()

    exchange_start(s.stage, s.at_recv, s.s_asend, s.s_arecv)
    for k in range(2, depth):
        line_event(k, main)
    for k in range(depth):
        second_event(order(k), (0,))
    second_event(z, main)
    for k in range(depth):
        all_here(order(k), (0,))
    exchange_wait(s.stage, s.at_recv, s.s_asend, s.s_arecv)

    full = 2 * rows
    def attended():
        pieces = [
            jnp.concatenate([s.at_recv[2 * g], s.at_recv[2 * g + 1]], axis=0)
            for g in range(groups)
        ]
        return jnp.concatenate(pieces, axis=1)

    out_w = s.f_all[:, 0:unit, :].reshape(width, width)
    res = (
        x_ref[...].reshape(full, width).astype(F32) + nt(attended(), out_w) + s.vec[4:5, :]
    )
    s.resid[...] = res + s.vec[7:8, :]
    unit_rows, scale = row_norm(res)
    s.unit2[...] = unit_rows
    s.scale2[...] = scale
    s.h2[...] = (unit_rows * s.vec[5:6, :] + s.vec[6:7, :]).astype(BF)
    dr_out[...] = jnp.zeros_like(dr_out)

    def cut(p):
        return pl.ds(parts[p][0], parts[p][1])

    def sum_mate(p, t):
        return remote(
            s.gr.at[t, :, :, 1 - core, cut(p)],
            s.from_mate.at[t, :, :, cut(p)],
            s.s_rcs.at[p, t],
            s.s_rcr.at[p, t],
            z,
            mate,
        )

    def sum_first(p, t):
        if parts[p][2] == "b":
            source, to = s.gr.at[t, 1 - a, :, core, cut(p)], by_a
        else:
            source, to = s.gr.at[t, :, 1 - b, core, cut(p)], by_b
        target = s.from_one.at[t, :, cut(p)]
        return remote(source, target, s.s_r1s.at[p, t], s.s_r1r.at[p, t], z, to)

    def sum_second(p, t):
        if parts[p][2] == "b":
            source, to = s.gr.at[t, a, 1 - b, core, cut(p)], by_b
        else:
            source, to = s.gr.at[t, 1 - a, b, core, cut(p)], by_a
        target = s.from_two.at[t, cut(p)]
        return remote(source, target, s.s_r2s.at[p, t], s.s_r2r.at[p, t], z, to)

    def sum_line(p, t, origin):
        return remote(
            s.gr.at[t, a, b, core, cut(p)],
            s.from_z.at[origin, cut(p)],
            s.s_rzs.at[p, t],
            s.s_rzr.at[p, origin],
            t,
            r,
        )

    def start_sum(t, which):
        for p in which:
            sum_mate(p, t).start()

    def event_one(t, which):
        for p in which:
            sum_mate(p, t).wait_recv()
            for aa in range(2):
                for bb in range(2):
                    add_into(s.gr.at[t, aa, bb, core, cut(p)], s.from_mate.at[t, aa, bb, cut(p)])
            sum_first(p, t).start()

    def event_two(t, which):
        for p in which:
            sum_first(p, t).wait_recv()
            for e in range(2):
                mine = (
                    s.gr.at[t, a, e, core, cut(p)]
                    if parts[p][2] == "b"
                    else s.gr.at[t, e, b, core, cut(p)]
                )
                add_into(mine, s.from_one.at[t, e, cut(p)])
            sum_second(p, t).start()

    def event_three(t, which):
        for p in which:
            sum_second(p, t).wait_recv()
            add_into(s.gr.at[t, a, b, core, cut(p)], s.from_two.at[t, cut(p)])

            @pl.when(t != z)
            def _(p=p):
                sum_line(p, t, z).start()

    g_down = dy_ref[...].reshape(full, width)

    def feed(c, carry):
        k, half = c // 2, c % 2
        o = order(k)

        for kk in range(1, depth):

            @pl.when((half == 0) & (k == kk))
            def _(kk=kk):
                if kk + 1 < depth:
                    first_event(kk + 1, main)
                second_event(order(kk), main)

        @pl.when(half == 0)
        def _():
            all_here(o, main)

        devices = pl.ds(o * 8 + half * 4, 4)
        up_w = s.f_all[devices, unit : unit + per, :].reshape(chunk, width)
        down_w = s.f_all[devices, unit + per : unit + 2 * per, :].reshape(chunk, width)
        where = o * 2 + half
        up = nt(s.h2[...], up_w) + s.hid[where]
        square = up * up
        tanh = jnp.tanh(GELU_A * (up + GELU_B * square * up))
        side = 0.5 * (1.0 + tanh)
        act = (up * side).astype(BF)
        s.resid[...] += nn(act, down_w)
        slope = side + 0.5 * up * (1.0 - tanh * tanh) * (GELU_A * (1.0 + 3.0 * GELU_B * square))
        grad = dy_ref[...].reshape(full, width)
        d_up = (nt(grad, down_w) * slope).astype(BF)
        s.hid_grad[where] = jnp.sum(d_up.astype(F32), axis=0, keepdims=True)
        dr_out[...] += nn(d_up, up_w).reshape(2, rows, width)
        s.gr[o, half, :, :, unit : unit + per, :] = (
            tn(d_up, s.h2[...]).astype(BF).reshape(2, 2, per, width)
        )
        s.gr[o, half, :, :, unit + per : unit + 2 * per, :] = (
            tn(act, grad).astype(BF).reshape(2, 2, per, width)
        )

        @pl.when(half == 1)
        def _():
            start_sum(o, main)

            @pl.when((k > 0) & (k < depth - 1))
            def _():
                event_one(order(k - 1), main)

        return carry

    lax.fori_loop(0, 2 * depth, feed, 0)

    dy = g_down.astype(F32)
    y_out[...] = s.resid[...].astype(BF).reshape(2, rows, width)
    d_h2 = dr_out[...].reshape(full, width)
    unit_rows = s.unit2[...]
    d_res = dy + norm_back(d_h2 * s.vec[5:6, :], unit_rows, s.scale2[...])
    dr_out[...] = d_res.reshape(2, rows, width)
    g_mix = d_res.astype(BF)
    d_attn = nn(g_mix, s.f_all[:, 0:unit, :].reshape(width, width)).astype(BF)
    for m in range(2):
        for g in range(groups):
            s.stage[2 * g + m] = d_attn[
                m * rows : (m + 1) * rows, g * group : (g + 1) * group
            ]
    exchange_start(s.stage, s.da_recv, s.s_dsend, s.s_drecv)
    out_grad = tn(g_mix, attended()).astype(BF).reshape(depth, 2, 2, 2, unit, width)
    s.gr[:, :, :, :, 0:unit, :] = out_grad
    for k in range(depth):
        start_sum(order(k), (0,))
    s.vec_grad[...] = jnp.zeros_like(s.vec_grad)
    s.vec_grad[4:5, :] = jnp.sum(g_mix.astype(F32), axis=0, keepdims=True)
    s.vec_grad[5:6, :] = jnp.sum(d_h2 * unit_rows, axis=0, keepdims=True)
    s.vec_grad[6:7, :] = jnp.sum(d_h2, axis=0, keepdims=True)
    s.vec_grad[7:8, :] = jnp.sum(dy, axis=0, keepdims=True)
    event_one(order(depth - 2), main)
    event_one(order(depth - 1), main)
    exchange_wait(s.stage, s.da_recv, s.s_dsend, s.s_drecv)

    for p in range(8):
        s.da[p * rows : (p + 1) * rows, :] = s.da_recv[block_at(spans, micro, p, 8)]
    s.dk_acc[...] = jnp.zeros_like(s.dk_acc)
    s.dv_acc[...] = jnp.zeros_like(s.dv_acc)

    def out_events(act):
        def go():
            for k in range(depth):
                act(order(k), (0,))

        return go

    sum_events = {
        0: [lambda: event_two(order(0), main)],
        1: [lambda: event_two(order(1), main)],
        2: [lambda: event_two(order(2), main), lambda: event_three(order(0), main)],
        3: [out_events(event_one), lambda: event_three(order(1), main)],
        4: [lambda: event_two(order(3), main)],
        5: [out_events(event_two), lambda: event_three(order(2), main)],
        6: [lambda: event_three(order(3), main)],
        8: [out_events(event_three)],
    }

    def query_block(i, carry):
        start = pl.multiple_of(i * QROWS, QROWS)
        at_q = pl.ds(start, QROWS)
        stacked = stack_heads(s.qkv[0, at_q, :] * BF(score_scale), heads)
        d_rows = s.da[at_q, :]
        d_stacked = stack_heads(d_rows, heads)
        product = d_rows.astype(F32) * s.o[at_q, 0:group]
        delta = jnp.sum(stack_heads(product, heads), axis=1, keepdims=True)
        lse = jnp.concatenate(
            [s.o[at_q, group + head : group + head + 1] for head in range(heads)], axis=0
        )

        def step(kc, acc):
            at = pl.ds(pl.multiple_of(kc * KCOLS, KCOLS), KCOLS)
            bias = visible_bias(lens, micro, start, QROWS, kc * KCOLS, KCOLS)
            keys = s.qkv[1, at, :]
            scores = nt(stacked, keys)
            scores = (scores.reshape(heads, QROWS, KCOLS) + bias[None]).reshape(tall, KCOLS)
            probs = jnp.exp(scores - lse)
            d_probs = nt(d_stacked, s.qkv[2, at, :])
            d_scores = (probs * (d_probs - delta)).astype(BF)
            s.dk_acc[at, :] += tn(d_scores, stacked)
            s.dv_acc[at, :] += tn(probs.astype(BF), d_stacked)
            return acc + nn(d_scores, keys)

        acc = lax.fori_loop(0, (i * QROWS) // KCOLS + 1, step, jnp.zeros((tall, group), F32))
        s.qkv[0, at_q, :] = (unstack_heads(acc, heads) * score_scale).astype(BF)
        run_events(sum_events, i)
        return carry

    lax.fori_loop(0, q_blocks, query_block, 0)
    s.qkv[1] = s.dk_acc[...].astype(BF)
    s.qkv[2] = s.dv_acc[...].astype(BF)

    pairs = n.units // 2
    for kind in range(3):
        s.gq[kind] = tn(s.qkv[kind], s.h[...]).astype(BF).reshape(pairs, 2, unit, width)
    q_mate = remote(
        s.gq.at[:, :, 1 - core], s.q_mate, s.s_gqc.at[0], s.s_gqc.at[1], z, mate
    )
    q_mate.start()

    def q_route(kind, m):
        block = kind * n.total + j * n.units + m * 2 + core
        owner = block // 3
        return owner // 8, owner % 8, block % 3

    def q_out(kind, m):
        oz, orr, at = q_route(kind, m)
        source = s.gq.at[kind, m, core]
        target, send = s.q_line.at[at, z], s.s_gqs.at[kind, m]
        go = lambda: remote(source, target, send, s.s_gqr.at[at, z], oz, orr)
        stay = lambda: pltpu.make_async_copy(source, target, send)
        return go, stay, (oz == z) & (orr == r)

    def q_sums(act):
        def each(e, carry):
            kind, m = e // pairs, e % pairs
            go, stay, mine = q_out(kind, m)
            act(kind, m, go, stay, mine)
            return carry

        lax.fori_loop(0, 3 * pairs, each, 0)

    def q_send(kind, m, go, stay, mine):
        add_into(s.gq.at[kind, m, core], s.q_mate.at[kind, m])

        @pl.when(jnp.logical_not(mine))
        def _():
            go().start()

        @pl.when(mine)
        def _():
            stay().start()

    def q_sent(kind, m, go, stay, mine):
        @pl.when(jnp.logical_not(mine))
        def _():
            go().wait_send()

        @pl.when(mine)
        def _():
            stay().wait()

    for lane in range(7):
        row_move(x_ref.at[0], r, lane, mate).wait_send()
    s.sums[...] = jnp.zeros_like(s.sums)

    def dh_a1():
        return remote(s.x_all.at[1 - a, :, core], s.dh_a1, s.s_dhs.at[0], s.s_dhr.at[0], z, by_a)

    def dh_b1():
        return remote(s.x_all.at[:, 1 - b, 1 - core], s.dh_b1, s.s_dhs.at[1], s.s_dhr.at[1], z, by_b)

    def dh_a2():
        return remote(s.x_all.at[a, 1 - b, core], s.dh_a2, s.s_dhs.at[2], s.s_dhr.at[2], z, by_b)

    def dh_b2():
        return remote(s.x_all.at[1 - a, b, 1 - core], s.dh_b2, s.s_dhs.at[3], s.s_dhr.at[3], z, by_a)

    def dh_m():
        return remote(s.x_all.at[a, b, 1 - core], s.dh_mate, s.s_dhs.at[4], s.s_dhr.at[4], z, mate)

    def unsort(e, carry):
        late, kind, lane = e // 4, (e % 4) // 2, e % 2
        aa = jnp.where(kind == 0, jnp.where(late == 1, a, 1 - a), lane)
        bb = jnp.where(kind == 0, lane, jnp.where(late == 1, b, 1 - b))
        cc = jnp.where(kind == 0, core, 1 - core)
        at = pl.ds(spans[0, micro, aa * 4 + bb * 2 + cc] * rows, rows)
        part = (
            nn(s.qkv[0, at, :], weight(0))
            + nn(s.qkv[1, at, :], weight(1))
            + nn(s.qkv[2, at, :], weight(2))
        )
        s.x_all[aa, bb, cc] = part.astype(BF)
        s.sums[0:1, :] += jnp.sum(part * s.u[at, :].astype(F32), axis=0, keepdims=True)
        s.sums[1:2, :] += jnp.sum(part, axis=0, keepdims=True)

        @pl.when(e == 3)
        def _():
            dh_a1().start()
            dh_b1().start()
            q_mate.wait_recv()
            q_sums(q_send)

        return carry

    lax.fori_loop(0, 8, unsort, 0)

    query_bias = jnp.sum(s.qkv[0].astype(F32), axis=0, keepdims=True)
    value_bias = jnp.sum(s.qkv[2].astype(F32), axis=0, keepdims=True)
    s.vec_grad[0:2, :] = s.sums[0:2, :]
    s.vec_grad[2:3, :] = group_spread(query_bias, j, groups)
    s.vec_grad[3:4, :] = group_spread(value_bias, j, groups)
    hidden_row = jnp.concatenate([s.hid_grad[c] for c in range(2 * depth)], axis=1)
    left, right = gather_units(s.vec_grad[...], hidden_row, n.total)
    s.sg[:, :, 0:128] = left
    s.sg[:, :, 128:256] = right
    to_all(lambda other: s.sg.at[other], s.s_sgs, s.s_sgr, s.sg_recv)
    s.sg_recv[me] = s.sg[me]

    dh_a1().wait_recv()
    for e in range(2):
        add_into(s.x_all.at[a, e, core], s.dh_a1.at[e])
    dh_a2().start()
    dh_b1().wait_recv()
    for e in range(2):
        add_into(s.x_all.at[e, b, 1 - core], s.dh_b1.at[e])
    dh_b2().start()
    dh_b2().wait_recv()
    add_into(s.x_all.at[a, b, 1 - core], s.dh_b2)
    dh_m().start()

    for k in range(1, depth):
        o = order(k)
        for p in every:
            sum_line(p, z, o).wait_recv()
    total_rows = s.gr[z, a, b, core].astype(F32)
    for k in range(1, depth):
        total_rows = total_rows + s.from_z[order(k)].astype(F32)
    f_sum[...] = total_rows

    dh_a2().wait_recv()
    dh_out[core] = s.x_all[a, b, core].astype(F32) + s.dh_a2[...].astype(F32)
    dh_m().wait_recv()
    dh_out[1 - core] = s.dh_mate[...].astype(F32)

    from_all(s.sg.at[0], s.s_sgs, s.s_sgr, s.sg_recv)
    small_sum[...] = jnp.sum(s.sg_recv[...].astype(F32), axis=0)

    def q_arrivals(at, zz):
        block = me * 3 + at
        inside = block % n.total
        from_r = (inside // n.units) * 2 + (inside % n.units) % 2
        ref = s.q_line.at[at, zz]
        come = lambda: remote(ref, ref, s.s_gqs.at[0, 0], s.s_gqr.at[at, zz], zz, from_r)
        return come, (from_r == r) & (zz == z)

    for at in range(3):
        for zz in range(depth):
            come, mine = q_arrivals(at, zz)

            @pl.when(jnp.logical_not(mine))
            def _():
                come().wait_recv()

    q_sums(q_sent)
    for at in range(3):
        part = s.q_line[at, 0].astype(F32)
        for zz in range(1, depth):
            part = part + s.q_line[at, zz].astype(F32)
        q_sum[at] = part

    for t in range(3):
        for zz in range(depth):
            go, _, mine = q_first(t, zz)

            @pl.when(jnp.logical_not(mine))
            def _():
                go().wait_send()

    def q_relayed(e, carry):
        kind, at = e // n.units, e % n.units
        owner = (kind * n.total + j * n.units + at) // 3
        unit_ref = s.wts.at[kind, at]

        @pl.when(owner % 2 == core)
        def _():
            remote(
                unit_ref, unit_ref, s.s_qcsend.at[kind, at], s.s_qrecv.at[kind, at], z, mate
            ).wait_send()

        return carry

    lax.fori_loop(0, 3 * n.units, q_relayed, 0)
    q_mate.wait_send()
    for act in (dh_a1, dh_b1, dh_a2, dh_b2, dh_m):
        act().wait_send()

    def drain(o, carry):
        for p in every:
            one(p, o).wait_send()
            for lane in range(2):
                two(p, o, r, lane).wait_send()
            for lane in range(4):
                across(p, o, r, lane).wait_send()
            sum_mate(p, o).wait_send()
            sum_first(p, o).wait_send()
            sum_second(p, o).wait_send()

            @pl.when(o != z)
            def _(p=p):
                line_move(p, z, o).wait_send()
                sum_line(p, o, z).wait_send()

        return carry

    lax.fori_loop(0, depth, drain, 0)


def run_block(n, tie_map, lens, spans, x_own, dy_own, banks):
    rows, width = n.rows, n.width
    scratch = block_scratch(n)
    outs = (
        shape((2, rows, width), BF),
        shape((2, rows, width), F32),
        shape((2, rows, width), F32),
        shape((n.packed, width), F32),
        shape((3, n.unit, width), F32),
        shape((SMALL, 256), F32),
        shape((SMALL, width), F32),
    )
    return pl.pallas_call(
        functools.partial(block_kernel, n, tuple(scratch)),
        name="block",
        out_shape=outs,
        in_specs=[smem()] * 3 + [vmem()] * 15,
        out_specs=(vmem(),) * len(outs),
        scratch_shapes=list(scratch.values()),
        compiler_params=params(1),
    )(tie_map, lens, spans, x_own, dy_own, *banks)


def final_kernel(
    n, tie, x_ref, y_ref, dh_ref, dr_ref, vec_ref, f_ref, q_ref, small_ref, y_out, dx_out, *grads
):
    g1, s1, wq, bq, bv, wo, bo, g2, s2, wu, bu, wd, bd = grads
    y_out[...] = y_ref[...]
    for m in range(x_ref.shape[0]):
        unit_rows, scale = row_norm(x_ref[m].astype(F32))
        back = norm_back(dh_ref[m] * vec_ref[0:1, :], unit_rows, scale)
        dx_out[m] = (dr_ref[m] + back).astype(BF)
    layers = wq.shape[0]
    unit, per = n.unit, n.per

    def put(ref, index, value):
        for layer in range(layers):
            ref[layer] = jnp.where(tie[index] == layer, value, 0.0)

    put(wo, 5, f_ref[0:unit, :])
    put(wu, 9, f_ref[unit : unit + per, :])
    put(wd, 11, f_ref[unit + per :, :])
    put(wq, 2, q_ref[...].reshape(3 * unit, n.width))
    names = ((g1, 0), (s1, 1), (bq, 3), (bv, 4), (bo, 6), (g2, 7), (s2, 8), (bd, 12))
    for e, (ref, index) in enumerate(names):
        for layer in range(layers):
            ref[layer : layer + 1, :] = jnp.where(
                tie[index] == layer, small_ref[e : e + 1, 0:unit], 0.0
            )
    for layer in range(layers):
        bu[layer : layer + 1, :] = jnp.where(
            tie[10] == layer, small_ref[0:1, 128 : 128 + per], 0.0
        )


def turned(bank):
    return jnp.swapaxes(bank, 1, 2)


def grouped_plan(depth, *args):
    block_input, cotangent, tie_map, seq_lengths, span_place = args[:5]
    banks = list(args[5:])
    for index in (2, 5, 9):
        banks[index] = turned(banks[index])
    x_own, dy_own = block_input[0], cotangent[0]
    n = Sizes(depth, x_own.shape[1], x_own.shape[2], banks[10].shape[1] * depth * 8)
    y, d_resid, dh, f_sum, q_sum, small_sum, vectors = run_block(
        n, tie_map, seq_lengths, span_place, x_own, dy_own, banks
    )
    outs = (shape(x_own.shape, BF),) * 2 + tuple(shape(bank.shape, F32) for bank in banks)
    final = pl.pallas_call(
        functools.partial(final_kernel, n),
        name="finish",
        out_shape=outs,
        in_specs=[smem()] + [vmem()] * 8,
        out_specs=(vmem(),) * len(outs),
        compiler_params=params(),
    )(tie_map, x_own, y, dh, d_resid, vectors, f_sum, q_sum, small_sum)
    grads = list(final[2:])
    for index in (2, 5, 9):
        grads[index] = turned(grads[index])
    return (final[0][None], final[1][None]) + tuple(grads)


def fits_grouped(mesh, block_input, span_place, qkv_weight):
    width = qkv_weight.shape[1]
    rows = block_input.shape[2] // mesh.shape["ctx"]
    total = mesh.shape["ctx"] * mesh.shape["dp"]
    return (
        mesh.shape["ctx"] == 8
        and block_input.shape[1] == 2
        and HEADS % 4 == 0
        and HEADS * HD == width
        and rows % 16 == 0
        and block_input.shape[2] % KCOLS == 0
        and width % total == 0
        and (width // total) % 8 == 0
        and (width // 4) % (2 * (width // total)) == 0
    )


def solution(mesh):
    replicated_rows = P("dp", None, "ctx", None)
    vector = P(None, ("dp", "ctx"))
    columns = P(None, None, ("dp", "ctx"))
    bank_specs = (
        vector,
        vector,
        columns,
        vector,
        vector,
        columns,
        vector,
        vector,
        vector,
        columns,
        vector,
        P(None, ("dp", "ctx"), None),
        vector,
    )

    def step(*args):
        if fits_grouped(mesh, args[0], args[4], args[7]):
            plan = functools.partial(grouped_plan, mesh.shape["dp"])
        else:
            plan = general_plan
        return jax.shard_map(
            plan,
            mesh=mesh,
            in_specs=(
                replicated_rows,
                replicated_rows,
                P(),
                P("dp", None, None),
                P("dp", None, None),
            )
            + bank_specs,
            out_specs=(replicated_rows, replicated_rows) + bank_specs,
            check_vma=False,
        )(*args)

    return step
```

```python
import functools
import math
import types

import jax
import jax.numpy as jnp
from jax import lax
from jax.experimental import pallas as pl
from jax.experimental.pallas import tpu as pltpu
from jax.sharding import PartitionSpec as P

HEADS = 12
HD = 64


epsilon = 1e-05
masked_score = -1e30
score_scale = 0.125
key_block = 1024


def layer_norm(inputs, norm_gain, norm_shift):
    average = jnp.mean(inputs, axis=-1, keepdims=True)
    centered = inputs - average
    variance = jnp.mean(centered * centered, axis=-1, keepdims=True)
    return centered * lax.rsqrt(variance + epsilon) * norm_gain + norm_shift


def gelu_tanh(inputs):
    return jax.nn.gelu(inputs, approximate=True)


def stream_positions(row_index, span_row, rows_each):
    owner_lane = row_index // rows_each
    lane_ids = jnp.arange(span_row.shape[0], dtype=jnp.int32)
    span_ids = jnp.sum(
        jnp.where(owner_lane[:, None] == lane_ids[None, :], span_row[None, :], 0), axis=1
    )
    return span_ids * rows_each + row_index % rows_each


def segment_ids(positions, seq_ends):
    return jnp.sum((positions[:, None] >= seq_ends[None, :]).astype(jnp.int32), axis=1)


def over_blocks(step_fn, state, pieces):
    piece_rows = pieces[0].shape[0]
    block_rows = math.gcd(piece_rows, key_block)
    stacked = tuple(
        (
            member.reshape((piece_rows // block_rows, block_rows) + member.shape[1:])
            for member in pieces
        )
    )

    def inner_step(running, scan_item):
        block_index, sliced = scan_item
        return (step_fn(running, sliced, block_index * block_rows), None)

    finished, ignored = lax.scan(
        inner_step, state, (jnp.arange(piece_rows // block_rows, dtype=jnp.int32), stacked)
    )
    return finished


def score_probs(
    query_heads,
    grad_heads,
    lse_heads,
    delta_heads,
    query_pos,
    query_seg,
    key_heads,
    value_heads,
    key_pos,
    key_seg,
):
    allowed = (query_seg[:, None] == key_seg[None, :]) & (key_pos[None, :] <= query_pos[:, None])
    scores = (
        jnp.einsum("qhd,khd->hqk", query_heads, key_heads, preferred_element_type=jnp.float32)
        * score_scale
    )
    probs = jnp.where(allowed[None], jnp.exp(scores - lse_heads[:, :, None]), 0.0)
    dprobs = jnp.einsum("qhd,khd->hqk", grad_heads, value_heads, preferred_element_type=jnp.float32)
    dscores = (probs * (dprobs - delta_heads[:, :, None])).astype(jnp.bfloat16)
    return (probs.astype(jnp.bfloat16), dscores)


def general_plan(
    block_input,
    cotangent,
    tie_map,
    seq_lengths,
    span_place,
    first_gain,
    first_shift,
    qkv_weight,
    query_bias,
    value_bias,
    out_weight,
    out_bias,
    second_gain,
    second_shift,
    up_weight,
    up_bias,
    down_weight,
    down_bias,
):
    banks = (
        first_gain,
        first_shift,
        qkv_weight,
        query_bias,
        value_bias,
        out_weight,
        out_bias,
        second_gain,
        second_shift,
        up_weight,
        up_bias,
        down_weight,
        down_bias,
    )
    shards = tuple(
        (
            lax.dynamic_index_in_dim(weight_bank, tie_map[bank_number], 0, keepdims=False)
            for bank_number, weight_bank in enumerate(banks)
        )
    )
    micro_count = block_input.shape[1]
    row_count = block_input.shape[2]
    model_width = block_input.shape[3]
    ctx_index = lax.axis_index("ctx")
    local_rows = ctx_index * row_count + jnp.arange(row_count, dtype=jnp.int32)
    totals = None
    outputs = []
    input_grads = []
    for micro_step in range(micro_count):
        params = (
            lax.all_gather(shards[0], ("dp", "ctx"), axis=0, tiled=True),
            lax.all_gather(shards[1], ("dp", "ctx"), axis=0, tiled=True),
            lax.all_gather(shards[2], ("dp", "ctx"), axis=1, tiled=True),
            lax.all_gather(shards[3], ("dp", "ctx"), axis=0, tiled=True),
            lax.all_gather(shards[4], ("dp", "ctx"), axis=0, tiled=True),
            lax.all_gather(shards[5], ("dp", "ctx"), axis=1, tiled=True),
            lax.all_gather(shards[6], ("dp", "ctx"), axis=0, tiled=True),
            lax.all_gather(shards[7], ("dp", "ctx"), axis=0, tiled=True),
            lax.all_gather(shards[8], ("dp", "ctx"), axis=0, tiled=True),
            lax.all_gather(shards[9], ("dp", "ctx"), axis=1, tiled=True),
            lax.all_gather(shards[10], ("dp", "ctx"), axis=0, tiled=True),
            lax.all_gather(shards[11], ("dp", "ctx"), axis=0, tiled=True),
            lax.all_gather(shards[12], ("dp", "ctx"), axis=0, tiled=True),
        )
        (
            gain_before,
            shift_before,
            qkv_full,
            query_add,
            value_add,
            out_full,
            out_add,
            gain_after,
            shift_after,
            up_full,
            up_add,
            down_full,
            down_add,
        ) = params
        span_row = span_place[0, micro_step]
        seq_ends = jnp.cumsum(seq_lengths[0, micro_step])
        query_pos = stream_positions(local_rows, span_row, row_count)
        query_seg = segment_ids(query_pos, seq_ends)
        inputs_wide = block_input[0, micro_step].astype(jnp.float32)
        first_norm = layer_norm(
            inputs_wide, gain_before.astype(jnp.float32), shift_before.astype(jnp.float32)
        ).astype(jnp.bfloat16)
        projected = jnp.dot(first_norm, qkv_full, preferred_element_type=jnp.float32)
        queries = (projected[:, :model_width] + query_add.astype(jnp.float32)).astype(jnp.bfloat16)
        key_rows = projected[:, model_width : 2 * model_width].astype(jnp.bfloat16)
        value_rows = (projected[:, 2 * model_width :] + value_add.astype(jnp.float32)).astype(
            jnp.bfloat16
        )
        query_heads = queries.reshape(row_count, HEADS, HD)
        key_heads_own = key_rows.reshape(row_count, HEADS, HD)
        value_heads_own = value_rows.reshape(row_count, HEADS, HD)

        def attend(state, pieces, offset):
            row_max, row_sum, accumulated = state
            key_part, value_part = pieces
            piece_rows = key_part.shape[0]
            key_pos = stream_positions(
                offset + jnp.arange(piece_rows, dtype=jnp.int32), span_row, row_count
            )
            key_seg = segment_ids(key_pos, seq_ends)
            allowed = (query_seg[:, None] == key_seg[None, :]) & (
                key_pos[None, :] <= query_pos[:, None]
            )
            scores = (
                jnp.einsum(
                    "qhd,khd->hqk",
                    query_heads,
                    key_part.reshape(piece_rows, HEADS, HD),
                    preferred_element_type=jnp.float32,
                )
                * score_scale
            )
            scores = jnp.where(allowed[None], scores, masked_score)
            new_max = jnp.maximum(row_max, jnp.max(scores, axis=2))
            exp_scores = jnp.where(allowed[None], jnp.exp(scores - new_max[:, :, None]), 0.0)
            factor = jnp.exp(row_max - new_max)
            row_sum = row_sum * factor + jnp.sum(exp_scores, axis=2)
            accumulated = accumulated * factor.T[:, :, None] + jnp.einsum(
                "hqk,khd->qhd",
                exp_scores.astype(jnp.bfloat16),
                value_part.reshape(piece_rows, HEADS, HD),
                preferred_element_type=jnp.float32,
            )
            return (new_max, row_sum, accumulated)

        start_state = (
            jnp.full((HEADS, row_count), masked_score, jnp.float32),
            jnp.zeros((HEADS, row_count), jnp.float32),
            jnp.zeros((row_count, HEADS, HD), jnp.float32),
        )
        row_max, row_sum, accumulated = over_blocks(
            attend,
            start_state,
            (
                lax.all_gather(key_rows, "ctx", axis=0, tiled=True),
                lax.all_gather(value_rows, "ctx", axis=0, tiled=True),
            ),
        )
        attended_wide = accumulated / row_sum.T[:, :, None]
        log_sums = row_max + jnp.log(row_sum)
        attended = attended_wide.reshape(row_count, model_width).astype(jnp.bfloat16)
        mixed_out = jnp.dot(
            attended, out_full, preferred_element_type=jnp.float32
        ) + out_add.astype(jnp.float32)
        residual = inputs_wide + mixed_out
        second_norm = layer_norm(
            residual, gain_after.astype(jnp.float32), shift_after.astype(jnp.float32)
        ).astype(jnp.bfloat16)
        up_proj = jnp.dot(second_norm, up_full, preferred_element_type=jnp.float32) + up_add.astype(
            jnp.float32
        )
        activated = gelu_tanh(up_proj).astype(jnp.bfloat16)
        down_proj = jnp.dot(
            activated, down_full, preferred_element_type=jnp.float32
        ) + down_add.astype(jnp.float32)
        outputs.append((residual + down_proj).astype(jnp.bfloat16))
        params = (
            lax.all_gather(shards[0], ("dp", "ctx"), axis=0, tiled=True),
            lax.all_gather(shards[1], ("dp", "ctx"), axis=0, tiled=True),
            lax.all_gather(shards[2], ("dp", "ctx"), axis=1, tiled=True),
            lax.all_gather(shards[3], ("dp", "ctx"), axis=0, tiled=True),
            lax.all_gather(shards[4], ("dp", "ctx"), axis=0, tiled=True),
            lax.all_gather(shards[5], ("dp", "ctx"), axis=1, tiled=True),
            lax.all_gather(shards[6], ("dp", "ctx"), axis=0, tiled=True),
            lax.all_gather(shards[7], ("dp", "ctx"), axis=0, tiled=True),
            lax.all_gather(shards[8], ("dp", "ctx"), axis=0, tiled=True),
            lax.all_gather(shards[9], ("dp", "ctx"), axis=1, tiled=True),
            lax.all_gather(shards[10], ("dp", "ctx"), axis=0, tiled=True),
            lax.all_gather(shards[11], ("dp", "ctx"), axis=0, tiled=True),
            lax.all_gather(shards[12], ("dp", "ctx"), axis=0, tiled=True),
        )
        (
            gain_before,
            shift_before,
            qkv_full,
            query_add,
            value_add,
            out_full,
            out_add,
            gain_after,
            shift_after,
            up_full,
            up_add,
            down_full,
            down_add,
        ) = params
        grad_out = cotangent[0, micro_step].astype(jnp.float32)
        grad_down = grad_out.astype(jnp.bfloat16)
        down_weight_grad = jnp.einsum(
            "rf,rd->fd", activated, grad_down, preferred_element_type=jnp.float32
        )
        down_bias_grad = jnp.sum(grad_down.astype(jnp.float32), axis=0)
        grad_act = jnp.einsum("rd,fd->rf", grad_down, down_full, preferred_element_type=jnp.float32)
        unused_gelu, gelu_back = jax.vjp(gelu_tanh, up_proj)
        grad_up = gelu_back(grad_act)[0].astype(jnp.bfloat16)
        up_weight_grad = jnp.einsum(
            "rd,rf->df", second_norm, grad_up, preferred_element_type=jnp.float32
        )
        up_bias_grad = jnp.sum(grad_up.astype(jnp.float32), axis=0)
        grad_second = jnp.einsum("rf,df->rd", grad_up, up_full, preferred_element_type=jnp.float32)
        unused_second, second_back = jax.vjp(
            layer_norm, residual, gain_after.astype(jnp.float32), shift_after.astype(jnp.float32)
        )
        grad_resid, second_gain_grad, second_shift_grad = second_back(grad_second)
        grad_resid = grad_resid + grad_out
        grad_mixed = grad_resid.astype(jnp.bfloat16)
        out_weight_grad = jnp.einsum(
            "rc,rd->cd", attended, grad_mixed, preferred_element_type=jnp.float32
        )
        out_bias_grad = jnp.sum(grad_mixed.astype(jnp.float32), axis=0)
        grad_attended = jnp.einsum(
            "rd,cd->rc", grad_mixed, out_full, preferred_element_type=jnp.float32
        ).astype(jnp.bfloat16)
        grad_heads = grad_attended.reshape(row_count, HEADS, HD)
        delta_rows = jnp.sum(grad_heads.astype(jnp.float32) * attended_wide, axis=2)
        delta_heads = delta_rows.T
        empty_heads = jnp.zeros((row_count, HEADS, HD), jnp.float32)
        stats_whole = (
            lax.all_gather(log_sums.T, "ctx", axis=0, tiled=True),
            lax.all_gather(delta_rows, "ctx", axis=0, tiled=True),
        )

        def mutual(state, pieces, offset):
            grad_query, grad_key, grad_value = state
            key_part, value_part, query_part, gradout_part = pieces
            piece_rows = key_part.shape[0]
            lse_part = lax.dynamic_slice_in_dim(stats_whole[0], offset, piece_rows, 0)
            delta_part = lax.dynamic_slice_in_dim(stats_whole[1], offset, piece_rows, 0)
            key_pos = stream_positions(
                offset + jnp.arange(piece_rows, dtype=jnp.int32), span_row, row_count
            )
            key_seg = segment_ids(key_pos, seq_ends)
            key_part_heads = key_part.reshape(piece_rows, HEADS, HD)
            value_part_heads = value_part.reshape(piece_rows, HEADS, HD)
            query_part_heads = query_part.reshape(piece_rows, HEADS, HD)
            gradout_heads = gradout_part.reshape(piece_rows, HEADS, HD)
            probs, dscores = score_probs(
                query_heads,
                grad_heads,
                log_sums,
                delta_heads,
                query_pos,
                query_seg,
                key_part_heads,
                value_part_heads,
                key_pos,
                key_seg,
            )
            grad_query = grad_query + score_scale * jnp.einsum(
                "hqk,khd->qhd", dscores, key_part_heads, preferred_element_type=jnp.float32
            )
            probs_other, dscores_other = score_probs(
                query_part_heads,
                gradout_heads,
                lse_part.T,
                delta_part.T,
                key_pos,
                key_seg,
                key_heads_own,
                value_heads_own,
                query_pos,
                query_seg,
            )
            grad_key = grad_key + score_scale * jnp.einsum(
                "hqk,qhd->khd", dscores_other, query_part_heads, preferred_element_type=jnp.float32
            )
            grad_value = grad_value + jnp.einsum(
                "hqk,qhd->khd", probs_other, gradout_heads, preferred_element_type=jnp.float32
            )
            return (grad_query, grad_key, grad_value)

        grad_query, grad_key, grad_value = over_blocks(
            mutual,
            (empty_heads, empty_heads, empty_heads),
            (
                lax.all_gather(key_rows, "ctx", axis=0, tiled=True),
                lax.all_gather(value_rows, "ctx", axis=0, tiled=True),
                lax.all_gather(queries, "ctx", axis=0, tiled=True),
                lax.all_gather(grad_attended, "ctx", axis=0, tiled=True),
            ),
        )
        grad_proj = jnp.concatenate(
            [
                grad_query.reshape(row_count, model_width),
                grad_key.reshape(row_count, model_width),
                grad_value.reshape(row_count, model_width),
            ],
            axis=1,
        ).astype(jnp.bfloat16)
        qkv_weight_grad = jnp.einsum(
            "rc,rp->cp", first_norm, grad_proj, preferred_element_type=jnp.float32
        )
        query_bias_grad = jnp.sum(grad_proj[:, :model_width].astype(jnp.float32), axis=0)
        value_bias_grad = jnp.sum(grad_proj[:, 2 * model_width :].astype(jnp.float32), axis=0)
        grad_first = jnp.einsum(
            "rp,cp->rc", grad_proj, qkv_full, preferred_element_type=jnp.float32
        )
        unused_first, first_back = jax.vjp(
            layer_norm,
            inputs_wide,
            gain_before.astype(jnp.float32),
            shift_before.astype(jnp.float32),
        )
        grad_input, first_gain_grad, first_shift_grad = first_back(grad_first)
        input_grads.append((grad_input + grad_resid).astype(jnp.bfloat16))
        micro_grads = (
            first_gain_grad,
            first_shift_grad,
            qkv_weight_grad,
            query_bias_grad,
            value_bias_grad,
            out_weight_grad,
            out_bias_grad,
            second_gain_grad,
            second_shift_grad,
            up_weight_grad,
            up_bias_grad,
            down_weight_grad,
            down_bias_grad,
        )
        if totals is None:
            totals = micro_grads
        else:
            totals = tuple(
                (left_sum + right_sum for left_sum, right_sum in zip(totals, micro_grads))
            )
    owned = (
        lax.psum_scatter(totals[0], ("dp", "ctx"), scatter_dimension=0, tiled=True),
        lax.psum_scatter(totals[1], ("dp", "ctx"), scatter_dimension=0, tiled=True),
        lax.psum_scatter(totals[2], ("dp", "ctx"), scatter_dimension=1, tiled=True),
        lax.psum_scatter(totals[3], ("dp", "ctx"), scatter_dimension=0, tiled=True),
        lax.psum_scatter(totals[4], ("dp", "ctx"), scatter_dimension=0, tiled=True),
        lax.psum_scatter(totals[5], ("dp", "ctx"), scatter_dimension=1, tiled=True),
        lax.psum_scatter(totals[6], ("dp", "ctx"), scatter_dimension=0, tiled=True),
        lax.psum_scatter(totals[7], ("dp", "ctx"), scatter_dimension=0, tiled=True),
        lax.psum_scatter(totals[8], ("dp", "ctx"), scatter_dimension=0, tiled=True),
        lax.psum_scatter(totals[9], ("dp", "ctx"), scatter_dimension=1, tiled=True),
        lax.psum_scatter(totals[10], ("dp", "ctx"), scatter_dimension=0, tiled=True),
        lax.psum_scatter(totals[11], ("dp", "ctx"), scatter_dimension=0, tiled=True),
        lax.psum_scatter(totals[12], ("dp", "ctx"), scatter_dimension=0, tiled=True),
    )
    bank_grads = tuple(
        (
            lax.dynamic_update_index_in_dim(
                jnp.zeros(weight_bank.shape, jnp.float32), owned_piece, tie_map[bank_number], 0
            )
            for bank_number, (weight_bank, owned_piece) in enumerate(zip(banks, owned))
        )
    )
    block_output = jnp.stack(outputs)[None]
    input_grad = jnp.stack(input_grads)[None]
    return (block_output, input_grad) + bank_grads


BF = jnp.bfloat16
F32 = jnp.float32
MESH = pl.DeviceIdType.MESH
ANY = pl.ANY
SMALL = 8
VMEM_BYTES = 62 * 2**20


def params(collective_id=None):
    if collective_id is None:
        return pltpu.CompilerParams(vmem_limit_bytes=VMEM_BYTES)
    return pltpu.CompilerParams(
        vmem_limit_bytes=VMEM_BYTES, collective_id=collective_id, has_side_effects=True
    )


def vmem():
    return pl.BlockSpec(memory_space=pltpu.VMEM)


def smem():
    return pl.BlockSpec(memory_space=pltpu.SMEM)


def anywhere():
    return pl.BlockSpec(memory_space=ANY)


def shape(dims, dtype):
    return jax.ShapeDtypeStruct(dims, dtype)


def nn(left, right):
    return lax.dot_general(left, right, (((1,), (0,)), ((), ())), preferred_element_type=F32)


def nt(left, right):
    return lax.dot_general(left, right, (((1,), (1,)), ((), ())), preferred_element_type=F32)


def tn(left, right):
    return lax.dot_general(left, right, (((0,), (0,)), ((), ())), preferred_element_type=F32)


def iota(dims, axis):
    return lax.broadcasted_iota(jnp.int32, dims, axis)


class Place:
    def __init__(self, depth):
        self.depth = depth
        self.z = lax.axis_index("dp")
        self.r = lax.axis_index("ctx")
        self.core = self.r % 2
        self.j = self.r // 2
        self.a = self.r // 4
        self.b = (self.r // 2) % 2
        self.by_a = (1 - self.a) * 4 + self.b * 2 + self.core
        self.by_b = self.a * 4 + (1 - self.b) * 2 + self.core
        self.both = (1 - self.a) * 4 + (1 - self.b) * 2 + self.core
        self.mate = self.j * 2 + 1 - self.core

    def slot(self, z, r):
        return z * 8 + r


def greet_all(here):
    bar = pltpu.get_barrier_semaphore()
    total = here.depth * 8
    me = here.z * 8 + here.r

    def signal(k, carry):
        other = (me + k) % total
        pl.semaphore_signal(bar, inc=1, device_id=(other // 8, other % 8), device_id_type=MESH)
        return carry

    lax.fori_loop(1, total, signal, 0)
    pl.semaphore_wait(bar, total - 1)


def remote(source, target, send, recv, z, r):
    return pltpu.make_async_remote_copy(
        src_ref=source,
        dst_ref=target,
        send_sem=send,
        recv_sem=recv,
        device_id=(z, r),
        device_id_type=MESH,
    )


def spread_units(small, width, hidden_total):
    devices = small.shape[0]
    unit = width // devices
    per = hidden_total // devices
    flat = small.reshape(devices * SMALL, 256)
    lane = iota((128, width), 1)
    pick = (lane % unit == iota((128, width), 0)).astype(F32).astype(BF)
    tall = nn(flat[:, 0:128], pick)
    row = iota((devices * SMALL, width), 0)
    col = iota((devices * SMALL, width), 1)
    tall = jnp.where(col // unit == row // SMALL, tall, 0.0)
    vectors = jnp.sum(tall.reshape(devices, SMALL, width), axis=0)
    chosen = (
        (iota((devices, devices * SMALL), 1) == iota((devices, devices * SMALL), 0) * SMALL)
        .astype(F32)
        .astype(BF)
    )
    firsts = nn(chosen, flat[:, 128:256]).astype(BF)
    lane = iota((128, hidden_total), 1)
    pick = (lane % per == iota((128, hidden_total), 0)).astype(F32).astype(BF)
    wide = nn(firsts, pick)
    keep = iota((devices, hidden_total), 1) // per == iota((devices, hidden_total), 0)
    return vectors, jnp.sum(jnp.where(keep, wide, 0.0), axis=0, keepdims=True)


def gather_vectors(vectors, devices):
    width = vectors.shape[1]
    unit = width // devices
    tall = jnp.broadcast_to(vectors[None], (devices, SMALL, width)).reshape(devices * SMALL, width)
    row = iota((devices * SMALL, width), 0)
    col = iota((devices * SMALL, width), 1)
    tall = jnp.where(col // unit == row // SMALL, tall, 0.0).astype(BF)
    pick = (iota((width, 128), 0) % unit == iota((width, 128), 1)).astype(F32).astype(BF)
    return nn(tall, pick).astype(BF).reshape(devices, SMALL, 128)


def gather_hidden(hidden_row, devices):
    hidden_total = hidden_row.shape[1]
    per = hidden_total // devices
    wide = jnp.broadcast_to(hidden_row, (devices, hidden_total))
    keep = iota((devices, hidden_total), 1) // per == iota((devices, hidden_total), 0)
    wide = jnp.where(keep, wide, 0.0).astype(BF)
    pick = (iota((hidden_total, 128), 0) % per == iota((hidden_total, 128), 1)).astype(F32)
    firsts = nn(wide, pick.astype(BF)).astype(BF)
    chosen = (
        (iota((devices * SMALL, devices), 0) == iota((devices * SMALL, devices), 1) * SMALL)
        .astype(F32)
        .astype(BF)
    )
    return nn(chosen, firsts).astype(BF).reshape(devices, SMALL, 128)


def group_slice(row, j, groups):
    width = row.shape[1] // groups
    out = jnp.zeros((1, width), F32)
    for g in range(groups):
        out = jnp.where(j == g, row[:, g * width : (g + 1) * width], out)
    return out


def group_spread(part, j, groups):
    return jnp.concatenate([jnp.where(j == g, part, 0.0) for g in range(groups)], axis=1)


def block_at(place_ref, micro, position, blocks):
    found = jnp.int32(0)
    for s in range(blocks):
        found = jnp.where(place_ref[0, micro, s] == position, s, found)
    return found


def stack_heads(rows, heads):
    lane = iota(rows.shape, 1) // HD
    zero = jnp.zeros_like(rows)
    return jnp.concatenate([jnp.where(lane == h, rows, zero) for h in range(heads)], axis=0)


def unstack_heads(tall, heads):
    rows = tall.shape[0] // heads
    lane = iota((rows, tall.shape[1]), 1) // HD
    out = tall[0:rows]
    for h in range(1, heads):
        out = jnp.where(lane == h, tall[h * rows : (h + 1) * rows], out)
    return out


def visible_bias(lens, micro, start, rows, key_start, keys):
    query = start + iota((rows, 1), 0)
    begin = jnp.zeros((rows, 1), jnp.int32)
    end = jnp.int32(0)
    for s in range(lens.shape[2]):
        end = end + lens[0, micro, s]
        begin = jnp.where(query >= end, end, begin)
    key = key_start + iota((rows, keys), 1)
    return jnp.where((key >= begin) & (key <= query), 0.0, masked_score)


def row_norm(wide):
    average = jnp.mean(wide, axis=-1, keepdims=True)
    centered = wide - average
    variance = jnp.mean(centered * centered, axis=-1, keepdims=True)
    scale = lax.rsqrt(variance + epsilon)
    return centered * scale, scale


def norm_back(grad, unit, scale):
    first = jnp.mean(grad, axis=-1, keepdims=True)
    second = jnp.mean(grad * unit, axis=-1, keepdims=True)
    return (grad - first - unit * second) * scale


QROWS = 128
KCOLS = 384
GELU_A = math.sqrt(2.0 / math.pi)
GELU_B = 0.044715


class Sizes:
    def __init__(self, depth, rows, width, hidden_total):
        self.depth = depth
        self.rows = rows
        self.width = width
        self.total = depth * 8
        self.unit = width // self.total
        self.per = hidden_total // self.total
        self.group = width // 4
        self.heads = self.group // HD
        self.pack = 8 * rows
        self.packed = self.unit + 2 * self.per
        self.units = self.group // self.unit
        cut = self.per - 8
        self.parts = (
            (0, self.unit, "b"),
            (self.unit, cut, "b"),
            (self.unit + cut, 2 * self.per - cut, "a"),
        )


def block_scratch(n):
    vm = lambda dims, dtype=BF: pltpu.VMEM(dims, dtype)
    dma = lambda dims: pltpu.SemaphoreType.DMA(dims)
    d, w, g, pack, rows = n.depth, n.width, n.group, n.pack, n.rows
    p = len(n.parts)
    both = 2 * rows
    halves = 2 * d
    chunk = n.per * 4
    return {
        "f_all": vm((n.total, n.packed, w)),
        "gr": vm((d, 2, 2, 2, n.packed, w)),
        "from_mate": vm((d, 2, 2, n.packed, w)),
        "from_one": vm((d, 2, n.packed, w)),
        "from_two": vm((d, n.packed, w)),
        "from_z": vm((d, n.packed, w)),
        "q_own": vm((3, n.unit, w)),
        "wts": vm((3, n.units, n.unit, w)),
        "small_all": vm((n.total, SMALL, 256)),
        "x_all": vm((2, 2, 2, rows, w)),
        "h": vm((pack, w)),
        "u": vm((pack, w)),
        "qkv": vm((3, pack, g)),
        "o": vm((pack, -(-(g + n.heads) // 128) * 128), F32),
        "vec": vm((SMALL, w), F32),
        "hid": vm((halves, 1, chunk), F32),
        "hid_grad": vm((halves, 1, chunk), F32),
        "stage": vm((8, rows + rows // 2, 128)),
        "at_recv": vm((8, rows + rows // 2, 128)),
        "da_recv": vm((8, rows + rows // 2, 128)),
        "resid": vm((both, w), F32),
        "unit2": vm((both, w), F32),
        "h2": vm((both, w)),
        "scale2": vm((both, 1), F32),
        "vec_grad": vm((SMALL, w), F32),
        "da": vm((pack, g)),
        "dk_acc": vm((pack, g), F32),
        "dv_acc": vm((pack, g), F32),
        "gq": vm((3, n.units // 2, 2, n.unit, w)),
        "q_mate": vm((3, n.units // 2, n.unit, w)),
        "q_line": vm((3, d, n.unit, w)),
        "dh_a1": vm((2, rows, w)),
        "dh_b1": vm((2, rows, w)),
        "dh_a2": vm((rows, w)),
        "dh_b2": vm((rows, w)),
        "dh_mate": vm((rows, w)),
        "sums": vm((SMALL, w), F32),
        "sg": vm((n.total, SMALL, 256)),
        "sg_recv": vm((n.total, SMALL, 256)),
        "s_zsend": dma((p, d)),
        "s_zrecv": dma((p, d)),
        "s_send1": dma((p, d)),
        "s_recv1": dma((p, d)),
        "s_send2": dma((p, d, 2)),
        "s_recv2": dma((p, d, 2)),
        "s_csend": dma((p, d, 4)),
        "s_crecv": dma((p, d, 4)),
        "s_xsend": dma((7,)),
        "s_xrecv": dma((8,)),
        "s_qsend": dma((3, d)),
        "s_qrecv": dma((3, n.units)),
        "s_qcsend": dma((3, n.units)),
        "s_smsend": dma((n.total,)),
        "s_smrecv": dma((n.total,)),
        "s_asend": dma((8,)),
        "s_arecv": dma((8,)),
        "s_dsend": dma((8,)),
        "s_drecv": dma((8,)),
        "s_rcs": dma((p, d)),
        "s_rcr": dma((p, d)),
        "s_r1s": dma((p, d)),
        "s_r1r": dma((p, d)),
        "s_r2s": dma((p, d)),
        "s_r2r": dma((p, d)),
        "s_rzs": dma((p, d)),
        "s_rzr": dma((p, d)),
        "s_gqc": dma((2,)),
        "s_gqs": dma((3, n.units // 2)),
        "s_gqr": dma((3, d)),
        "s_dhs": dma((5,)),
        "s_dhr": dma((5,)),
        "s_sgs": dma((n.total,)),
        "s_sgr": dma((n.total,)),
    }


def fold(block):
    half = block.shape[0] // 2
    side = jnp.concatenate([block[:half, 128:], block[half:, 128:]], axis=1)
    return jnp.concatenate([block[:, :128], side], axis=0)


def unfold(tall):
    rows = tall.shape[0] * 2 // 3
    side = jnp.concatenate([tall[rows:, :64], tall[rows:, 64:]], axis=0)
    return jnp.concatenate([tall[:rows], side], axis=1)


def add_into(target, source):
    target[...] = (target[...].astype(F32) + source[...].astype(F32)).astype(BF)


def block_kernel(n, names, tie, lens, spans, x_ref, dy_ref, *refs):
    banks = refs[:13]
    y_out, dr_out, dh_out, f_sum, q_sum, small_sum, vec_out = refs[13:20]
    s = types.SimpleNamespace(**dict(zip(names, refs[20:])))
    g1, s1, wq, bq, bv, wo, bo, g2, s2, wu, bu, wd, bd = banks
    depth, unit, per, rows, width, group, heads = (
        n.depth, n.unit, n.per, n.rows, n.width, n.group, n.heads
    )
    here = Place(depth)
    z, r, a, b, core, j = here.z, here.r, here.a, here.b, here.core, here.j
    me = here.slot(z, r)
    micro = core
    mate, by_a, by_b, both = here.mate, here.by_a, here.by_b, here.both
    parts = n.parts
    main = (1, 2)
    groups = 4

    bar = pltpu.get_barrier_semaphore()

    def signal(k, carry):
        other = (me + k) % n.total
        pl.semaphore_signal(bar, inc=1, device_id=(other // 8, other % 8), device_id_type=MESH)
        return carry

    lax.fori_loop(1, n.total, signal, 0)

    f_own = s.f_all.at[me]
    f_own[0:unit, :] = wo[tie[5]]
    f_own[unit : unit + per, :] = wu[tie[9]]
    f_own[unit + per :, :] = wd[tie[11]]
    s.q_own[...] = wq[tie[2]].reshape(3, unit, width)
    chosen_rows = []
    for bank, index in ((g1, 0), (s1, 1), (bq, 3), (bv, 4), (bo, 6), (g2, 7), (s2, 8), (bd, 12)):
        wide = bank[...].astype(F32)
        chosen = jnp.zeros((1, unit), F32)
        for layer in range(bank.shape[0]):
            chosen = jnp.where(tie[index] == layer, wide[layer : layer + 1, :], chosen)
        chosen_rows.append(chosen)
    small_own = s.small_all.at[me]
    small_own[...] = jnp.zeros((SMALL, 256), BF)
    small_own[:, 0:unit] = jnp.concatenate(chosen_rows, axis=0).astype(BF)
    wide = bu[...].astype(F32)
    chosen = jnp.zeros((1, per), F32)
    for layer in range(bu.shape[0]):
        chosen = jnp.where(tie[10] == layer, wide[layer : layer + 1, :], chosen)
    tall = jnp.concatenate([chosen, jnp.zeros((SMALL - 1, per), F32)], axis=0)
    small_own[:, 128 : 128 + per] = tall.astype(BF)

    pl.semaphore_wait(bar, n.total - 1)

    def to_all(buffer_of, send, recv, target):
        def go(k, carry):
            other = (me + k) % n.total
            remote(
                buffer_of(other), target.at[me], send.at[other], recv.at[me], other // 8, other % 8
            ).start()
            return carry

        lax.fori_loop(1, n.total, go, 0)

    def from_all(buffer, send, recv, target):
        def go(k, carry):
            other = (me + k) % n.total
            remote(
                buffer, target.at[other], send.at[other], recv.at[other], other // 8, other % 8
            ).wait()
            return carry

        lax.fori_loop(1, n.total, go, 0)

    def row_block(block):
        return s.x_all.at[block // 4, (block // 2) % 2, block % 2]

    def row_move(source, block, lane, to):
        return remote(source, row_block(block), s.s_xsend.at[lane], s.s_xrecv.at[block], z, to)

    mate_a = by_a + 1 - 2 * core
    row_move(x_ref.at[1 - core], r, 0, mate).start()
    row_move(x_ref.at[core], r, 1, by_b).start()
    row_move(x_ref.at[core], r, 2, by_a).start()
    to_all(lambda other: small_own, s.s_smsend, s.s_smrecv, s.small_all)
    row_block(r)[...] = x_ref[core]

    def q_unit(t):
        block = me * 3 + t
        kind = block // n.total
        inside = block % n.total
        return kind, inside // n.units, inside % n.units

    def q_first(t, zz):
        kind, chip, at = q_unit(t)
        to = chip * 2 + core
        source, target, recv = s.q_own.at[t], s.wts.at[kind, at], s.s_qrecv.at[kind, at]
        go = lambda: remote(source, target, s.s_qsend.at[t, zz], recv, zz, to)
        stay = lambda: pltpu.make_async_copy(source, target, recv)
        return go, stay, (zz == z) & (to == r)

    for t in range(3):
        for zz in range(depth):
            go, stay, mine = q_first(t, zz)

            @pl.when(jnp.logical_not(mine))
            def _():
                go().start()

            @pl.when(mine)
            def _():
                stay().start()

    def order(k):
        out = jnp.int32(0)
        for zz in range(depth):
            line = sorted(range(depth), key=lambda t: (abs(t - zz), t))
            for kk in range(depth):
                out = jnp.where((z == zz) & (k == kk), line[kk], out)
        return out

    def move(p, zz, rr, send, recv, to_z, to_r):
        start, count, _ = parts[p]
        ref = s.f_all.at[here.slot(zz, rr), pl.ds(start, count)]
        return remote(ref, ref, send, recv, to_z, to_r)

    def first_axis(p):
        return by_b if parts[p][2] == "b" else by_a

    def second_axis(p):
        return by_a if parts[p][2] == "b" else by_b

    def line_move(p, o, to_z):
        return move(p, o, r, s.s_zsend.at[p, to_z], s.s_zrecv.at[p, o], to_z, r)

    def one(p, o):
        return move(p, o, r, s.s_send1.at[p, o], s.s_recv1.at[p, o], z, first_axis(p))

    def two(p, o, rr, lane):
        return move(
            p, o, rr, s.s_send2.at[p, o, lane], s.s_recv2.at[p, o, lane], z, second_axis(p)
        )

    def across(p, o, rr, lane):
        return move(p, o, rr, s.s_csend.at[p, o, lane], s.s_crecv.at[p, o, lane], z, mate)

    every = range(len(parts))
    for p in every:
        for k in range(1, depth):
            line_move(p, z, order(k)).start()

    def row_arrived(block):
        row_move(x_ref.at[0], block, 0, mate).wait_recv()

    row_arrived(mate)
    row_move(row_block(mate), mate, 3, by_a).start()
    row_move(row_block(mate), mate, 4, by_b).start()
    row_arrived(by_b)
    row_move(row_block(by_b), by_b, 5, by_a).start()
    row_arrived(mate_a)
    row_move(row_block(mate_a), mate_a, 6, by_b).start()

    def q_relay(e, carry):
        kind, at = e // n.units, e % n.units
        owner = (kind * n.total + j * n.units + at) // 3
        unit_ref = s.wts.at[kind, at]

        @pl.when(owner % 2 == core)
        def _():
            pltpu.make_async_copy(unit_ref, unit_ref, s.s_qrecv.at[kind, at]).wait()
            remote(
                unit_ref, unit_ref, s.s_qcsend.at[kind, at], s.s_qrecv.at[kind, at], z, mate
            ).start()

        return carry

    lax.fori_loop(0, 3 * n.units, q_relay, 0)

    def spread_own(p):
        one(p, z).start()
        two(p, z, r, 0).start()
        across(p, z, r, 0).start()

    for p in every:
        spread_own(p)

    from_all(small_own, s.s_smsend, s.s_smrecv, s.small_all)
    vectors, hidden = spread_units(s.small_all[...], width, per * n.total)
    s.vec[...] = vectors
    vec_out[...] = vectors
    chunk = 4 * per
    for c in range(2 * depth):
        s.hid[c] = hidden[:, c * chunk : (c + 1) * chunk]

    row_arrived(by_a)
    row_arrived(both)
    row_arrived(by_b + 1 - 2 * core)
    row_arrived(both + 1 - 2 * core)

    def q_rest(e, carry):
        kind, at = e // n.units, e % n.units
        owner = (kind * n.total + j * n.units + at) // 3
        unit_ref = s.wts.at[kind, at]

        @pl.when(owner % 2 != core)
        def _():
            remote(
                unit_ref, unit_ref, s.s_qcsend.at[kind, at], s.s_qrecv.at[kind, at], z, mate
            ).wait_recv()

        return carry

    lax.fori_loop(0, 3 * n.units, q_rest, 0)

    gain, shift = s.vec[0:1, :], s.vec[1:2, :]
    query_add = group_slice(s.vec[2:3, :], j, groups)
    value_add = group_slice(s.vec[3:4, :], j, groups)

    def weight(kind):
        return s.wts[kind].reshape(group, width)

    def project(p, carry):
        source = block_at(spans, micro, p, 8)
        unit_rows, _ = row_norm(
            s.x_all[source // 4, (source // 2) % 2, source % 2].astype(F32)
        )
        normed = (unit_rows * gain + shift).astype(BF)
        at = pl.ds(pl.multiple_of(p * rows, 16), rows)
        s.u[at, :] = unit_rows.astype(BF)
        s.h[at, :] = normed
        s.qkv[0, at, :] = (nt(normed, weight(0)) + query_add).astype(BF)
        s.qkv[1, at, :] = nt(normed, weight(1)).astype(BF)
        s.qkv[2, at, :] = (nt(normed, weight(2)) + value_add).astype(BF)
        return carry

    lax.fori_loop(0, 8, project, 0)

    def line_event(k, which):
        o = order(k)
        for p in which:
            line_move(p, o, z).wait_recv()
            one(p, o).start()
            two(p, o, r, 0).start()
            across(p, o, r, 0).start()

    def first_event(k, which):
        o = order(k)
        for p in which:
            one(p, o).wait_recv()
            two(p, o, first_axis(p), 1).start()
            across(p, o, first_axis(p), 1).start()

    def second_event(o, which):
        for p in which:
            two(p, o, r, 0).wait_recv()
            across(p, o, second_axis(p), 2).start()
            two(p, o, r, 1).wait_recv()
            across(p, o, both, 3).start()

    def all_here(o, which):
        for p in which:
            for lane in range(4):
                across(p, o, r, lane).wait_recv()

    gather_events = {
        0: [lambda: line_event(1, (0,)), lambda: first_event(0, (0,))],
        1: [lambda: line_event(2, (0,)), lambda: line_event(3, (0,))],
        2: [lambda: line_event(1, main)],
        3: [lambda: first_event(1, (0,)), lambda: first_event(0, main)],
        5: [lambda: first_event(2, (0,)), lambda: first_event(3, (0,))],
        6: [lambda: first_event(1, main)],
    }

    def run_events(events, i):
        for at, acts in events.items():

            @pl.when(i == at)
            def _(acts=acts):
                for act in acts:
                    act()

    tall = heads * QROWS
    q_blocks = n.pack // QROWS

    def attend(i, carry):
        start = pl.multiple_of(i * QROWS, QROWS)
        stacked = stack_heads(s.qkv[0, pl.ds(start, QROWS), :] * BF(score_scale), heads)

        def step(kc, state):
            top, total, acc = state
            at = pl.ds(pl.multiple_of(kc * KCOLS, KCOLS), KCOLS)
            bias = visible_bias(lens, micro, start, QROWS, kc * KCOLS, KCOLS)
            scores = nt(stacked, s.qkv[1, at, :])
            scores = (scores.reshape(heads, QROWS, KCOLS) + bias[None]).reshape(tall, KCOLS)
            new_top = jnp.maximum(top, jnp.max(scores, axis=1, keepdims=True))
            probs = jnp.exp(scores - new_top)
            factor = jnp.exp(top - new_top)
            total = total * factor + jnp.sum(probs, axis=1, keepdims=True)
            acc = acc * factor + nn(probs.astype(BF), s.qkv[2, at, :])
            return new_top, total, acc

        top, total, acc = lax.fori_loop(
            0,
            (i * QROWS) // KCOLS + 1,
            step,
            (
                jnp.full((tall, 1), masked_score, F32),
                jnp.zeros((tall, 1), F32),
                jnp.zeros((tall, group), F32),
            ),
        )
        at_q = pl.ds(start, QROWS)
        s.o[at_q, 0:group] = unstack_heads(acc / total, heads)
        lse = top + jnp.log(total)
        for head in range(heads):
            s.o[at_q, group + head : group + head + 1] = lse[head * QROWS : (head + 1) * QROWS]
        run_events(gather_events, i)
        return carry

    lax.fori_loop(0, q_blocks, attend, 0)

    for e in range(8):
        at = pl.ds(spans[0, micro, e] * rows, rows)
        s.stage[e] = fold(s.o[at, 0:group].astype(BF))

    def exchange_start(stage, target, send, recv):
        for k in range(1, 8):
            to = (r + k) % 8
            remote(stage.at[to], target.at[r], send.at[to], recv.at[r], z, to).start()
        target[r] = stage[r]

    def exchange_wait(stage, target, send, recv):
        for k in range(1, 8):
            frm = (r + k) % 8
            remote(stage.at[frm], target.at[frm], send.at[frm], recv.at[frm], z, frm).wait()

    exchange_start(s.stage, s.at_recv, s.s_asend, s.s_arecv)
    for k in range(2, depth):
        line_event(k, main)
    for k in range(depth):
        second_event(order(k), (0,))
    second_event(z, main)
    for k in range(depth):
        all_here(order(k), (0,))
    exchange_wait(s.stage, s.at_recv, s.s_asend, s.s_arecv)

    full = 2 * rows
    def attended():
        pieces = [
            jnp.concatenate([unfold(s.at_recv[2 * g]), unfold(s.at_recv[2 * g + 1])], axis=0)
            for g in range(groups)
        ]
        return jnp.concatenate(pieces, axis=1)

    out_w = s.f_all[:, 0:unit, :].reshape(width, width)
    res = (
        x_ref[...].reshape(full, width).astype(F32) + nt(attended(), out_w) + s.vec[4:5, :]
    )
    s.resid[...] = res + s.vec[7:8, :]
    unit_rows, scale = row_norm(res)
    s.unit2[...] = unit_rows
    s.scale2[...] = scale
    s.h2[...] = (unit_rows * s.vec[5:6, :] + s.vec[6:7, :]).astype(BF)
    dr_out[...] = jnp.zeros_like(dr_out)

    def cut(p):
        return pl.ds(parts[p][0], parts[p][1])

    def sum_mate(p, t):
        return remote(
            s.gr.at[t, :, :, 1 - core, cut(p)],
            s.from_mate.at[t, :, :, cut(p)],
            s.s_rcs.at[p, t],
            s.s_rcr.at[p, t],
            z,
            mate,
        )

    def sum_first(p, t):
        if parts[p][2] == "b":
            source, to = s.gr.at[t, 1 - a, :, core, cut(p)], by_a
        else:
            source, to = s.gr.at[t, :, 1 - b, core, cut(p)], by_b
        target = s.from_one.at[t, :, cut(p)]
        return remote(source, target, s.s_r1s.at[p, t], s.s_r1r.at[p, t], z, to)

    def sum_second(p, t):
        if parts[p][2] == "b":
            source, to = s.gr.at[t, a, 1 - b, core, cut(p)], by_b
        else:
            source, to = s.gr.at[t, 1 - a, b, core, cut(p)], by_a
        target = s.from_two.at[t, cut(p)]
        return remote(source, target, s.s_r2s.at[p, t], s.s_r2r.at[p, t], z, to)

    def sum_line(p, t, origin):
        return remote(
            s.gr.at[t, a, b, core, cut(p)],
            s.from_z.at[origin, cut(p)],
            s.s_rzs.at[p, t],
            s.s_rzr.at[p, origin],
            t,
            r,
        )

    def start_sum(t, which):
        for p in which:
            sum_mate(p, t).start()

    def event_one(t, which):
        for p in which:
            sum_mate(p, t).wait_recv()
            for aa in range(2):
                for bb in range(2):
                    add_into(s.gr.at[t, aa, bb, core, cut(p)], s.from_mate.at[t, aa, bb, cut(p)])
            sum_first(p, t).start()

    def event_two(t, which):
        for p in which:
            sum_first(p, t).wait_recv()
            for e in range(2):
                mine = (
                    s.gr.at[t, a, e, core, cut(p)]
                    if parts[p][2] == "b"
                    else s.gr.at[t, e, b, core, cut(p)]
                )
                add_into(mine, s.from_one.at[t, e, cut(p)])
            sum_second(p, t).start()

    def event_three(t, which):
        for p in which:
            sum_second(p, t).wait_recv()
            add_into(s.gr.at[t, a, b, core, cut(p)], s.from_two.at[t, cut(p)])

            @pl.when(t != z)
            def _(p=p):
                sum_line(p, t, z).start()

    g_down = dy_ref[...].reshape(full, width)

    def feed(c, carry):
        k, half = c // 2, c % 2
        o = order(k)

        for kk in range(1, depth):

            @pl.when((half == 0) & (k == kk))
            def _(kk=kk):
                if kk + 1 < depth:
                    first_event(kk + 1, main)
                second_event(order(kk), main)

        @pl.when(half == 0)
        def _():
            all_here(o, main)

        devices = pl.ds(o * 8 + half * 4, 4)
        up_w = s.f_all[devices, unit : unit + per, :].reshape(chunk, width)
        down_w = s.f_all[devices, unit + per : unit + 2 * per, :].reshape(chunk, width)
        where = o * 2 + half
        up = nt(s.h2[...], up_w) + s.hid[where]
        square = up * up
        tanh = jnp.tanh(GELU_A * (up + GELU_B * square * up))
        side = 0.5 * (1.0 + tanh)
        act = (up * side).astype(BF)
        s.resid[...] += nn(act, down_w)
        slope = side + 0.5 * up * (1.0 - tanh * tanh) * (GELU_A * (1.0 + 3.0 * GELU_B * square))
        grad = dy_ref[...].reshape(full, width)
        d_up = (nt(grad, down_w) * slope).astype(BF)
        s.hid_grad[where] = jnp.sum(d_up.astype(F32), axis=0, keepdims=True)
        dr_out[...] += nn(d_up, up_w).reshape(2, rows, width)
        s.gr[o, half, :, :, unit : unit + per, :] = (
            tn(d_up, s.h2[...]).astype(BF).reshape(2, 2, per, width)
        )
        s.gr[o, half, :, :, unit + per : unit + 2 * per, :] = (
            tn(act, grad).astype(BF).reshape(2, 2, per, width)
        )

        @pl.when(half == 1)
        def _():
            start_sum(o, main)

            @pl.when(k > 0)
            def _():
                event_one(order(k - 1), main)

        return carry

    lax.fori_loop(0, 2 * depth, feed, 0)

    dy = g_down.astype(F32)
    d_h2 = dr_out[...].reshape(full, width)
    unit_rows = s.unit2[...]
    d_res = dy + norm_back(d_h2 * s.vec[5:6, :], unit_rows, s.scale2[...])
    dr_out[...] = d_res.reshape(2, rows, width)
    g_mix = d_res.astype(BF)
    d_attn = nn(g_mix, s.f_all[:, 0:unit, :].reshape(width, width)).astype(BF)
    for m in range(2):
        for g in range(groups):
            s.stage[2 * g + m] = fold(
                d_attn[m * rows : (m + 1) * rows, g * group : (g + 1) * group]
            )
    exchange_start(s.stage, s.da_recv, s.s_dsend, s.s_drecv)
    y_out[...] = s.resid[...].astype(BF).reshape(2, rows, width)
    out_grad = tn(g_mix, attended()).astype(BF).reshape(depth, 2, 2, 2, unit, width)
    s.gr[:, :, :, :, 0:unit, :] = out_grad
    for k in range(depth):
        start_sum(order(k), (0,))
    s.vec_grad[...] = jnp.zeros_like(s.vec_grad)
    s.vec_grad[4:5, :] = jnp.sum(g_mix.astype(F32), axis=0, keepdims=True)
    s.vec_grad[5:6, :] = jnp.sum(d_h2 * unit_rows, axis=0, keepdims=True)
    s.vec_grad[6:7, :] = jnp.sum(d_h2, axis=0, keepdims=True)
    s.vec_grad[7:8, :] = jnp.sum(dy, axis=0, keepdims=True)
    event_one(order(depth - 1), main)
    hidden_row = jnp.concatenate([s.hid_grad[c] for c in range(2 * depth)], axis=1)
    s.sg[:, :, 128:256] = gather_hidden(hidden_row, n.total)
    exchange_wait(s.stage, s.da_recv, s.s_dsend, s.s_drecv)

    for p in range(8):
        s.da[p * rows : (p + 1) * rows, :] = unfold(s.da_recv[block_at(spans, micro, p, 8)])
    s.dk_acc[...] = jnp.zeros_like(s.dk_acc)
    s.dv_acc[...] = jnp.zeros_like(s.dv_acc)

    def out_events(act):
        def go():
            for k in range(depth):
                act(order(k), (0,))

        return go

    sum_events = {
        0: [lambda: event_two(order(1), main)],
        1: [lambda: event_two(order(2), main)],
        3: [lambda: event_three(order(1), main), out_events(event_one)],
        5: [lambda: event_two(order(3), main)],
        6: [lambda: event_three(order(2), main), out_events(event_two)],
        7: [lambda: event_two(order(0), main)],
        8: [lambda: event_three(order(3), main), out_events(event_three), lambda: event_three(order(0), main)],
    }

    def query_block(i, carry):
        start = pl.multiple_of(i * QROWS, QROWS)
        at_q = pl.ds(start, QROWS)
        stacked = stack_heads(s.qkv[0, at_q, :] * BF(score_scale), heads)
        d_rows = s.da[at_q, :]
        d_stacked = stack_heads(d_rows, heads)
        product = d_rows.astype(F32) * s.o[at_q, 0:group]
        delta = jnp.sum(stack_heads(product, heads), axis=1, keepdims=True)
        lse = jnp.concatenate(
            [s.o[at_q, group + head : group + head + 1] for head in range(heads)], axis=0
        )

        def step(kc, acc):
            at = pl.ds(pl.multiple_of(kc * KCOLS, KCOLS), KCOLS)
            bias = visible_bias(lens, micro, start, QROWS, kc * KCOLS, KCOLS)
            keys = s.qkv[1, at, :]
            scores = nt(stacked, keys)
            scores = (scores.reshape(heads, QROWS, KCOLS) + bias[None]).reshape(tall, KCOLS)
            probs = jnp.exp(scores - lse)
            d_probs = nt(d_stacked, s.qkv[2, at, :])
            d_scores = (probs * (d_probs - delta)).astype(BF)
            s.dk_acc[at, :] += tn(d_scores, stacked)
            s.dv_acc[at, :] += tn(probs.astype(BF), d_stacked)
            return acc + nn(d_scores, keys)

        acc = lax.fori_loop(0, (i * QROWS) // KCOLS + 1, step, jnp.zeros((tall, group), F32))
        s.qkv[0, at_q, :] = (unstack_heads(acc, heads) * score_scale).astype(BF)
        run_events(sum_events, i)
        return carry

    lax.fori_loop(0, q_blocks, query_block, 0)
    s.qkv[1] = s.dk_acc[...].astype(BF)
    s.qkv[2] = s.dv_acc[...].astype(BF)

    pairs = n.units // 2
    for kind in range(3):
        s.gq[kind] = tn(s.qkv[kind], s.h[...]).astype(BF).reshape(pairs, 2, unit, width)
    q_mate = remote(
        s.gq.at[:, :, 1 - core], s.q_mate, s.s_gqc.at[0], s.s_gqc.at[1], z, mate
    )
    q_mate.start()

    def q_route(kind, m):
        block = kind * n.total + j * n.units + m * 2 + core
        owner = block // 3
        return owner // 8, owner % 8, block % 3

    def q_out(kind, m):
        oz, orr, at = q_route(kind, m)
        source = s.gq.at[kind, m, core]
        target, send = s.q_line.at[at, z], s.s_gqs.at[kind, m]
        go = lambda: remote(source, target, send, s.s_gqr.at[at, z], oz, orr)
        stay = lambda: pltpu.make_async_copy(source, target, send)
        return go, stay, (oz == z) & (orr == r)

    def q_sums(act):
        def each(e, carry):
            kind, m = e // pairs, e % pairs
            go, stay, mine = q_out(kind, m)
            act(kind, m, go, stay, mine)
            return carry

        lax.fori_loop(0, 3 * pairs, each, 0)

    def q_send(kind, m, go, stay, mine):
        add_into(s.gq.at[kind, m, core], s.q_mate.at[kind, m])

        @pl.when(jnp.logical_not(mine))
        def _():
            go().start()

        @pl.when(mine)
        def _():
            stay().start()

    def q_sent(kind, m, go, stay, mine):
        @pl.when(jnp.logical_not(mine))
        def _():
            go().wait_send()

        @pl.when(mine)
        def _():
            stay().wait()

    for lane in range(7):
        row_move(x_ref.at[0], r, lane, mate).wait_send()
    s.sums[...] = jnp.zeros_like(s.sums)

    def dh_a1():
        return remote(s.x_all.at[1 - a, :, core], s.dh_a1, s.s_dhs.at[0], s.s_dhr.at[0], z, by_a)

    def dh_b1():
        return remote(s.x_all.at[:, 1 - b, 1 - core], s.dh_b1, s.s_dhs.at[1], s.s_dhr.at[1], z, by_b)

    def dh_a2():
        return remote(s.x_all.at[a, 1 - b, core], s.dh_a2, s.s_dhs.at[2], s.s_dhr.at[2], z, by_b)

    def dh_b2():
        return remote(s.x_all.at[1 - a, b, 1 - core], s.dh_b2, s.s_dhs.at[3], s.s_dhr.at[3], z, by_a)

    def dh_m():
        return remote(s.x_all.at[a, b, 1 - core], s.dh_mate, s.s_dhs.at[4], s.s_dhr.at[4], z, mate)


    def unsort(e, carry):
        late, kind, lane = e // 4, (e % 4) // 2, e % 2
        aa = jnp.where(kind == 0, jnp.where(late == 1, a, 1 - a), lane)
        bb = jnp.where(kind == 0, lane, jnp.where(late == 1, b, 1 - b))
        cc = jnp.where(kind == 0, core, 1 - core)
        at = pl.ds(spans[0, micro, aa * 4 + bb * 2 + cc] * rows, rows)
        part = (
            nn(s.qkv[0, at, :], weight(0))
            + nn(s.qkv[1, at, :], weight(1))
            + nn(s.qkv[2, at, :], weight(2))
        )
        s.x_all[aa, bb, cc] = part.astype(BF)
        s.sums[0:1, :] += jnp.sum(part * s.u[at, :].astype(F32), axis=0, keepdims=True)
        s.sums[1:2, :] += jnp.sum(part, axis=0, keepdims=True)

        @pl.when(e == 3)
        def _():
            dh_a1().start()
            dh_b1().start()
            q_mate.wait_recv()
            q_sums(q_send)

        return carry

    lax.fori_loop(0, 8, unsort, 0)

    query_bias = jnp.sum(s.qkv[0].astype(F32), axis=0, keepdims=True)
    value_bias = jnp.sum(s.qkv[2].astype(F32), axis=0, keepdims=True)
    s.vec_grad[0:2, :] = s.sums[0:2, :]
    s.vec_grad[2:3, :] = group_spread(query_bias, j, groups)
    s.vec_grad[3:4, :] = group_spread(value_bias, j, groups)
    s.sg[:, :, 0:128] = gather_vectors(s.vec_grad[...], n.total)
    to_all(lambda other: s.sg.at[other], s.s_sgs, s.s_sgr, s.sg_recv)
    s.sg_recv[me] = s.sg[me]

    dh_a1().wait_recv()
    for e in range(2):
        add_into(s.x_all.at[a, e, core], s.dh_a1.at[e])
    dh_a2().start()
    dh_b1().wait_recv()
    for e in range(2):
        add_into(s.x_all.at[e, b, 1 - core], s.dh_b1.at[e])
    dh_b2().start()
    dh_b2().wait_recv()
    add_into(s.x_all.at[a, b, 1 - core], s.dh_b2)
    dh_m().start()

    for k in range(1, depth):
        o = order(k)
        for p in every:
            sum_line(p, z, o).wait_recv()
    total_rows = s.gr[z, a, b, core].astype(F32)
    for k in range(1, depth):
        total_rows = total_rows + s.from_z[order(k)].astype(F32)
    f_sum[...] = total_rows

    dh_a2().wait_recv()
    dh_out[core] = s.x_all[a, b, core].astype(F32) + s.dh_a2[...].astype(F32)
    dh_m().wait_recv()
    dh_out[1 - core] = s.dh_mate[...].astype(F32)

    from_all(s.sg.at[0], s.s_sgs, s.s_sgr, s.sg_recv)
    small_sum[...] = jnp.sum(s.sg_recv[...].astype(F32), axis=0)

    def q_arrivals(at, zz):
        block = me * 3 + at
        inside = block % n.total
        from_r = (inside // n.units) * 2 + (inside % n.units) % 2
        ref = s.q_line.at[at, zz]
        come = lambda: remote(ref, ref, s.s_gqs.at[0, 0], s.s_gqr.at[at, zz], zz, from_r)
        return come, (from_r == r) & (zz == z)

    for at in range(3):
        for zz in range(depth):
            come, mine = q_arrivals(at, zz)

            @pl.when(jnp.logical_not(mine))
            def _():
                come().wait_recv()

    q_sums(q_sent)
    for at in range(3):
        part = s.q_line[at, 0].astype(F32)
        for zz in range(1, depth):
            part = part + s.q_line[at, zz].astype(F32)
        q_sum[at] = part

    for t in range(3):
        for zz in range(depth):
            go, _, mine = q_first(t, zz)

            @pl.when(jnp.logical_not(mine))
            def _():
                go().wait_send()

    def q_relayed(e, carry):
        kind, at = e // n.units, e % n.units
        owner = (kind * n.total + j * n.units + at) // 3
        unit_ref = s.wts.at[kind, at]

        @pl.when(owner % 2 == core)
        def _():
            remote(
                unit_ref, unit_ref, s.s_qcsend.at[kind, at], s.s_qrecv.at[kind, at], z, mate
            ).wait_send()

        return carry

    lax.fori_loop(0, 3 * n.units, q_relayed, 0)
    q_mate.wait_send()
    for act in (dh_a1, dh_b1, dh_a2, dh_b2, dh_m):
        act().wait_send()

    def drain(o, carry):
        for p in every:
            one(p, o).wait_send()
            for lane in range(2):
                two(p, o, r, lane).wait_send()
            for lane in range(4):
                across(p, o, r, lane).wait_send()
            sum_mate(p, o).wait_send()
            sum_first(p, o).wait_send()
            sum_second(p, o).wait_send()

            @pl.when(o != z)
            def _(p=p):
                line_move(p, z, o).wait_send()
                sum_line(p, o, z).wait_send()

        return carry

    lax.fori_loop(0, depth, drain, 0)


def run_block(n, tie_map, lens, spans, x_own, dy_own, banks):
    rows, width = n.rows, n.width
    scratch = block_scratch(n)
    outs = (
        shape((2, rows, width), BF),
        shape((2, rows, width), F32),
        shape((2, rows, width), F32),
        shape((n.packed, width), F32),
        shape((3, n.unit, width), F32),
        shape((SMALL, 256), F32),
        shape((SMALL, width), F32),
    )
    return pl.pallas_call(
        functools.partial(block_kernel, n, tuple(scratch)),
        name="block",
        out_shape=outs,
        in_specs=[smem()] * 3 + [vmem()] * 15,
        out_specs=(vmem(),) * len(outs),
        scratch_shapes=list(scratch.values()),
        compiler_params=params(1),
    )(tie_map, lens, spans, x_own, dy_own, *banks)


def final_kernel(
    n, tie, x_ref, y_ref, dh_ref, dr_ref, vec_ref, f_ref, q_ref, small_ref, y_out, dx_out, *grads
):
    g1, s1, wq, bq, bv, wo, bo, g2, s2, wu, bu, wd, bd = grads
    y_out[...] = y_ref[...]
    for m in range(x_ref.shape[0]):
        unit_rows, scale = row_norm(x_ref[m].astype(F32))
        back = norm_back(dh_ref[m] * vec_ref[0:1, :], unit_rows, scale)
        dx_out[m] = (dr_ref[m] + back).astype(BF)
    layers = wq.shape[0]
    unit, per = n.unit, n.per

    def put(ref, index, value):
        for layer in range(layers):
            ref[layer] = jnp.where(tie[index] == layer, value, 0.0)

    put(wo, 5, f_ref[0:unit, :])
    put(wu, 9, f_ref[unit : unit + per, :])
    put(wd, 11, f_ref[unit + per :, :])
    put(wq, 2, q_ref[...].reshape(3 * unit, n.width))
    names = ((g1, 0), (s1, 1), (bq, 3), (bv, 4), (bo, 6), (g2, 7), (s2, 8), (bd, 12))
    for e, (ref, index) in enumerate(names):
        for layer in range(layers):
            ref[layer : layer + 1, :] = jnp.where(
                tie[index] == layer, small_ref[e : e + 1, 0:unit], 0.0
            )
    for layer in range(layers):
        bu[layer : layer + 1, :] = jnp.where(
            tie[10] == layer, small_ref[0:1, 128 : 128 + per], 0.0
        )


def turned(bank):
    return jnp.swapaxes(bank, 1, 2)


def grouped_plan(depth, *args):
    block_input, cotangent, tie_map, seq_lengths, span_place = args[:5]
    banks = list(args[5:])
    for index in (2, 5, 9):
        banks[index] = turned(banks[index])
    x_own, dy_own = block_input[0], cotangent[0]
    n = Sizes(depth, x_own.shape[1], x_own.shape[2], banks[10].shape[1] * depth * 8)
    y, d_resid, dh, f_sum, q_sum, small_sum, vectors = run_block(
        n, tie_map, seq_lengths, span_place, x_own, dy_own, banks
    )
    outs = (shape(x_own.shape, BF),) * 2 + tuple(shape(bank.shape, F32) for bank in banks)
    final = pl.pallas_call(
        functools.partial(final_kernel, n),
        name="finish",
        out_shape=outs,
        in_specs=[smem()] + [vmem()] * 8,
        out_specs=(vmem(),) * len(outs),
        compiler_params=params(),
    )(tie_map, x_own, y, dh, d_resid, vectors, f_sum, q_sum, small_sum)
    grads = list(final[2:])
    for index in (2, 5, 9):
        grads[index] = turned(grads[index])
    return (final[0][None], final[1][None]) + tuple(grads)


def fits_grouped(mesh, block_input, span_place, qkv_weight):
    width = qkv_weight.shape[1]
    rows = block_input.shape[2] // mesh.shape["ctx"]
    total = mesh.shape["ctx"] * mesh.shape["dp"]
    return (
        mesh.shape["ctx"] == 8
        and block_input.shape[1] == 2
        and HEADS % 4 == 0
        and HEADS * HD == width
        and rows % 16 == 0
        and width // 4 == 192
        and block_input.shape[2] % KCOLS == 0
        and width % total == 0
        and (width // total) % 8 == 0
        and (width // 4) % (2 * (width // total)) == 0
    )


def solution(mesh):
    replicated_rows = P("dp", None, "ctx", None)
    vector = P(None, ("dp", "ctx"))
    columns = P(None, None, ("dp", "ctx"))
    bank_specs = (
        vector,
        vector,
        columns,
        vector,
        vector,
        columns,
        vector,
        vector,
        vector,
        columns,
        vector,
        P(None, ("dp", "ctx"), None),
        vector,
    )

    def step(*args):
        if fits_grouped(mesh, args[0], args[4], args[7]):
            plan = functools.partial(grouped_plan, mesh.shape["dp"])
        else:
            plan = general_plan
        return jax.shard_map(
            plan,
            mesh=mesh,
            in_specs=(
                replicated_rows,
                replicated_rows,
                P(),
                P("dp", None, None),
                P("dp", None, None),
            )
            + bank_specs,
            out_specs=(replicated_rows, replicated_rows) + bank_specs,
            check_vma=False,
        )(*args)

    return step
```

```python
import functools
import math
import types

import jax
import jax.numpy as jnp
from jax import lax
from jax.experimental import pallas as pl
from jax.experimental.pallas import tpu as pltpu
from jax.sharding import PartitionSpec as P

HEADS = 12
HD = 64


epsilon = 1e-05
masked_score = -1e30
score_scale = 0.125
key_block = 1024


def layer_norm(inputs, norm_gain, norm_shift):
    average = jnp.mean(inputs, axis=-1, keepdims=True)
    centered = inputs - average
    variance = jnp.mean(centered * centered, axis=-1, keepdims=True)
    return centered * lax.rsqrt(variance + epsilon) * norm_gain + norm_shift


def gelu_tanh(inputs):
    return jax.nn.gelu(inputs, approximate=True)


def stream_positions(row_index, span_row, rows_each):
    owner_lane = row_index // rows_each
    lane_ids = jnp.arange(span_row.shape[0], dtype=jnp.int32)
    span_ids = jnp.sum(
        jnp.where(owner_lane[:, None] == lane_ids[None, :], span_row[None, :], 0), axis=1
    )
    return span_ids * rows_each + row_index % rows_each


def segment_ids(positions, seq_ends):
    return jnp.sum((positions[:, None] >= seq_ends[None, :]).astype(jnp.int32), axis=1)


def over_blocks(step_fn, state, pieces):
    piece_rows = pieces[0].shape[0]
    block_rows = math.gcd(piece_rows, key_block)
    stacked = tuple(
        (
            member.reshape((piece_rows // block_rows, block_rows) + member.shape[1:])
            for member in pieces
        )
    )

    def inner_step(running, scan_item):
        block_index, sliced = scan_item
        return (step_fn(running, sliced, block_index * block_rows), None)

    finished, ignored = lax.scan(
        inner_step, state, (jnp.arange(piece_rows // block_rows, dtype=jnp.int32), stacked)
    )
    return finished


def score_probs(
    query_heads,
    grad_heads,
    lse_heads,
    delta_heads,
    query_pos,
    query_seg,
    key_heads,
    value_heads,
    key_pos,
    key_seg,
):
    allowed = (query_seg[:, None] == key_seg[None, :]) & (key_pos[None, :] <= query_pos[:, None])
    scores = (
        jnp.einsum("qhd,khd->hqk", query_heads, key_heads, preferred_element_type=jnp.float32)
        * score_scale
    )
    probs = jnp.where(allowed[None], jnp.exp(scores - lse_heads[:, :, None]), 0.0)
    dprobs = jnp.einsum("qhd,khd->hqk", grad_heads, value_heads, preferred_element_type=jnp.float32)
    dscores = (probs * (dprobs - delta_heads[:, :, None])).astype(jnp.bfloat16)
    return (probs.astype(jnp.bfloat16), dscores)


def general_plan(
    block_input,
    cotangent,
    tie_map,
    seq_lengths,
    span_place,
    first_gain,
    first_shift,
    qkv_weight,
    query_bias,
    value_bias,
    out_weight,
    out_bias,
    second_gain,
    second_shift,
    up_weight,
    up_bias,
    down_weight,
    down_bias,
):
    banks = (
        first_gain,
        first_shift,
        qkv_weight,
        query_bias,
        value_bias,
        out_weight,
        out_bias,
        second_gain,
        second_shift,
        up_weight,
        up_bias,
        down_weight,
        down_bias,
    )
    shards = tuple(
        (
            lax.dynamic_index_in_dim(weight_bank, tie_map[bank_number], 0, keepdims=False)
            for bank_number, weight_bank in enumerate(banks)
        )
    )
    micro_count = block_input.shape[1]
    row_count = block_input.shape[2]
    model_width = block_input.shape[3]
    ctx_index = lax.axis_index("ctx")
    local_rows = ctx_index * row_count + jnp.arange(row_count, dtype=jnp.int32)
    totals = None
    outputs = []
    input_grads = []
    for micro_step in range(micro_count):
        params = (
            lax.all_gather(shards[0], ("dp", "ctx"), axis=0, tiled=True),
            lax.all_gather(shards[1], ("dp", "ctx"), axis=0, tiled=True),
            lax.all_gather(shards[2], ("dp", "ctx"), axis=1, tiled=True),
            lax.all_gather(shards[3], ("dp", "ctx"), axis=0, tiled=True),
            lax.all_gather(shards[4], ("dp", "ctx"), axis=0, tiled=True),
            lax.all_gather(shards[5], ("dp", "ctx"), axis=1, tiled=True),
            lax.all_gather(shards[6], ("dp", "ctx"), axis=0, tiled=True),
            lax.all_gather(shards[7], ("dp", "ctx"), axis=0, tiled=True),
            lax.all_gather(shards[8], ("dp", "ctx"), axis=0, tiled=True),
            lax.all_gather(shards[9], ("dp", "ctx"), axis=1, tiled=True),
            lax.all_gather(shards[10], ("dp", "ctx"), axis=0, tiled=True),
            lax.all_gather(shards[11], ("dp", "ctx"), axis=0, tiled=True),
            lax.all_gather(shards[12], ("dp", "ctx"), axis=0, tiled=True),
        )
        (
            gain_before,
            shift_before,
            qkv_full,
            query_add,
            value_add,
            out_full,
            out_add,
            gain_after,
            shift_after,
            up_full,
            up_add,
            down_full,
            down_add,
        ) = params
        span_row = span_place[0, micro_step]
        seq_ends = jnp.cumsum(seq_lengths[0, micro_step])
        query_pos = stream_positions(local_rows, span_row, row_count)
        query_seg = segment_ids(query_pos, seq_ends)
        inputs_wide = block_input[0, micro_step].astype(jnp.float32)
        first_norm = layer_norm(
            inputs_wide, gain_before.astype(jnp.float32), shift_before.astype(jnp.float32)
        ).astype(jnp.bfloat16)
        projected = jnp.dot(first_norm, qkv_full, preferred_element_type=jnp.float32)
        queries = (projected[:, :model_width] + query_add.astype(jnp.float32)).astype(jnp.bfloat16)
        key_rows = projected[:, model_width : 2 * model_width].astype(jnp.bfloat16)
        value_rows = (projected[:, 2 * model_width :] + value_add.astype(jnp.float32)).astype(
            jnp.bfloat16
        )
        query_heads = queries.reshape(row_count, HEADS, HD)
        key_heads_own = key_rows.reshape(row_count, HEADS, HD)
        value_heads_own = value_rows.reshape(row_count, HEADS, HD)

        def attend(state, pieces, offset):
            row_max, row_sum, accumulated = state
            key_part, value_part = pieces
            piece_rows = key_part.shape[0]
            key_pos = stream_positions(
                offset + jnp.arange(piece_rows, dtype=jnp.int32), span_row, row_count
            )
            key_seg = segment_ids(key_pos, seq_ends)
            allowed = (query_seg[:, None] == key_seg[None, :]) & (
                key_pos[None, :] <= query_pos[:, None]
            )
            scores = (
                jnp.einsum(
                    "qhd,khd->hqk",
                    query_heads,
                    key_part.reshape(piece_rows, HEADS, HD),
                    preferred_element_type=jnp.float32,
                )
                * score_scale
            )
            scores = jnp.where(allowed[None], scores, masked_score)
            new_max = jnp.maximum(row_max, jnp.max(scores, axis=2))
            exp_scores = jnp.where(allowed[None], jnp.exp(scores - new_max[:, :, None]), 0.0)
            factor = jnp.exp(row_max - new_max)
            row_sum = row_sum * factor + jnp.sum(exp_scores, axis=2)
            accumulated = accumulated * factor.T[:, :, None] + jnp.einsum(
                "hqk,khd->qhd",
                exp_scores.astype(jnp.bfloat16),
                value_part.reshape(piece_rows, HEADS, HD),
                preferred_element_type=jnp.float32,
            )
            return (new_max, row_sum, accumulated)

        start_state = (
            jnp.full((HEADS, row_count), masked_score, jnp.float32),
            jnp.zeros((HEADS, row_count), jnp.float32),
            jnp.zeros((row_count, HEADS, HD), jnp.float32),
        )
        row_max, row_sum, accumulated = over_blocks(
            attend,
            start_state,
            (
                lax.all_gather(key_rows, "ctx", axis=0, tiled=True),
                lax.all_gather(value_rows, "ctx", axis=0, tiled=True),
            ),
        )
        attended_wide = accumulated / row_sum.T[:, :, None]
        log_sums = row_max + jnp.log(row_sum)
        attended = attended_wide.reshape(row_count, model_width).astype(jnp.bfloat16)
        mixed_out = jnp.dot(
            attended, out_full, preferred_element_type=jnp.float32
        ) + out_add.astype(jnp.float32)
        residual = inputs_wide + mixed_out
        second_norm = layer_norm(
            residual, gain_after.astype(jnp.float32), shift_after.astype(jnp.float32)
        ).astype(jnp.bfloat16)
        up_proj = jnp.dot(second_norm, up_full, preferred_element_type=jnp.float32) + up_add.astype(
            jnp.float32
        )
        activated = gelu_tanh(up_proj).astype(jnp.bfloat16)
        down_proj = jnp.dot(
            activated, down_full, preferred_element_type=jnp.float32
        ) + down_add.astype(jnp.float32)
        outputs.append((residual + down_proj).astype(jnp.bfloat16))
        params = (
            lax.all_gather(shards[0], ("dp", "ctx"), axis=0, tiled=True),
            lax.all_gather(shards[1], ("dp", "ctx"), axis=0, tiled=True),
            lax.all_gather(shards[2], ("dp", "ctx"), axis=1, tiled=True),
            lax.all_gather(shards[3], ("dp", "ctx"), axis=0, tiled=True),
            lax.all_gather(shards[4], ("dp", "ctx"), axis=0, tiled=True),
            lax.all_gather(shards[5], ("dp", "ctx"), axis=1, tiled=True),
            lax.all_gather(shards[6], ("dp", "ctx"), axis=0, tiled=True),
            lax.all_gather(shards[7], ("dp", "ctx"), axis=0, tiled=True),
            lax.all_gather(shards[8], ("dp", "ctx"), axis=0, tiled=True),
            lax.all_gather(shards[9], ("dp", "ctx"), axis=1, tiled=True),
            lax.all_gather(shards[10], ("dp", "ctx"), axis=0, tiled=True),
            lax.all_gather(shards[11], ("dp", "ctx"), axis=0, tiled=True),
            lax.all_gather(shards[12], ("dp", "ctx"), axis=0, tiled=True),
        )
        (
            gain_before,
            shift_before,
            qkv_full,
            query_add,
            value_add,
            out_full,
            out_add,
            gain_after,
            shift_after,
            up_full,
            up_add,
            down_full,
            down_add,
        ) = params
        grad_out = cotangent[0, micro_step].astype(jnp.float32)
        grad_down = grad_out.astype(jnp.bfloat16)
        down_weight_grad = jnp.einsum(
            "rf,rd->fd", activated, grad_down, preferred_element_type=jnp.float32
        )
        down_bias_grad = jnp.sum(grad_down.astype(jnp.float32), axis=0)
        grad_act = jnp.einsum("rd,fd->rf", grad_down, down_full, preferred_element_type=jnp.float32)
        unused_gelu, gelu_back = jax.vjp(gelu_tanh, up_proj)
        grad_up = gelu_back(grad_act)[0].astype(jnp.bfloat16)
        up_weight_grad = jnp.einsum(
            "rd,rf->df", second_norm, grad_up, preferred_element_type=jnp.float32
        )
        up_bias_grad = jnp.sum(grad_up.astype(jnp.float32), axis=0)
        grad_second = jnp.einsum("rf,df->rd", grad_up, up_full, preferred_element_type=jnp.float32)
        unused_second, second_back = jax.vjp(
            layer_norm, residual, gain_after.astype(jnp.float32), shift_after.astype(jnp.float32)
        )
        grad_resid, second_gain_grad, second_shift_grad = second_back(grad_second)
        grad_resid = grad_resid + grad_out
        grad_mixed = grad_resid.astype(jnp.bfloat16)
        out_weight_grad = jnp.einsum(
            "rc,rd->cd", attended, grad_mixed, preferred_element_type=jnp.float32
        )
        out_bias_grad = jnp.sum(grad_mixed.astype(jnp.float32), axis=0)
        grad_attended = jnp.einsum(
            "rd,cd->rc", grad_mixed, out_full, preferred_element_type=jnp.float32
        ).astype(jnp.bfloat16)
        grad_heads = grad_attended.reshape(row_count, HEADS, HD)
        delta_rows = jnp.sum(grad_heads.astype(jnp.float32) * attended_wide, axis=2)
        delta_heads = delta_rows.T
        empty_heads = jnp.zeros((row_count, HEADS, HD), jnp.float32)
        stats_whole = (
            lax.all_gather(log_sums.T, "ctx", axis=0, tiled=True),
            lax.all_gather(delta_rows, "ctx", axis=0, tiled=True),
        )

        def mutual(state, pieces, offset):
            grad_query, grad_key, grad_value = state
            key_part, value_part, query_part, gradout_part = pieces
            piece_rows = key_part.shape[0]
            lse_part = lax.dynamic_slice_in_dim(stats_whole[0], offset, piece_rows, 0)
            delta_part = lax.dynamic_slice_in_dim(stats_whole[1], offset, piece_rows, 0)
            key_pos = stream_positions(
                offset + jnp.arange(piece_rows, dtype=jnp.int32), span_row, row_count
            )
            key_seg = segment_ids(key_pos, seq_ends)
            key_part_heads = key_part.reshape(piece_rows, HEADS, HD)
            value_part_heads = value_part.reshape(piece_rows, HEADS, HD)
            query_part_heads = query_part.reshape(piece_rows, HEADS, HD)
            gradout_heads = gradout_part.reshape(piece_rows, HEADS, HD)
            probs, dscores = score_probs(
                query_heads,
                grad_heads,
                log_sums,
                delta_heads,
                query_pos,
                query_seg,
                key_part_heads,
                value_part_heads,
                key_pos,
                key_seg,
            )
            grad_query = grad_query + score_scale * jnp.einsum(
                "hqk,khd->qhd", dscores, key_part_heads, preferred_element_type=jnp.float32
            )
            probs_other, dscores_other = score_probs(
                query_part_heads,
                gradout_heads,
                lse_part.T,
                delta_part.T,
                key_pos,
                key_seg,
                key_heads_own,
                value_heads_own,
                query_pos,
                query_seg,
            )
            grad_key = grad_key + score_scale * jnp.einsum(
                "hqk,qhd->khd", dscores_other, query_part_heads, preferred_element_type=jnp.float32
            )
            grad_value = grad_value + jnp.einsum(
                "hqk,qhd->khd", probs_other, gradout_heads, preferred_element_type=jnp.float32
            )
            return (grad_query, grad_key, grad_value)

        grad_query, grad_key, grad_value = over_blocks(
            mutual,
            (empty_heads, empty_heads, empty_heads),
            (
                lax.all_gather(key_rows, "ctx", axis=0, tiled=True),
                lax.all_gather(value_rows, "ctx", axis=0, tiled=True),
                lax.all_gather(queries, "ctx", axis=0, tiled=True),
                lax.all_gather(grad_attended, "ctx", axis=0, tiled=True),
            ),
        )
        grad_proj = jnp.concatenate(
            [
                grad_query.reshape(row_count, model_width),
                grad_key.reshape(row_count, model_width),
                grad_value.reshape(row_count, model_width),
            ],
            axis=1,
        ).astype(jnp.bfloat16)
        qkv_weight_grad = jnp.einsum(
            "rc,rp->cp", first_norm, grad_proj, preferred_element_type=jnp.float32
        )
        query_bias_grad = jnp.sum(grad_proj[:, :model_width].astype(jnp.float32), axis=0)
        value_bias_grad = jnp.sum(grad_proj[:, 2 * model_width :].astype(jnp.float32), axis=0)
        grad_first = jnp.einsum(
            "rp,cp->rc", grad_proj, qkv_full, preferred_element_type=jnp.float32
        )
        unused_first, first_back = jax.vjp(
            layer_norm,
            inputs_wide,
            gain_before.astype(jnp.float32),
            shift_before.astype(jnp.float32),
        )
        grad_input, first_gain_grad, first_shift_grad = first_back(grad_first)
        input_grads.append((grad_input + grad_resid).astype(jnp.bfloat16))
        micro_grads = (
            first_gain_grad,
            first_shift_grad,
            qkv_weight_grad,
            query_bias_grad,
            value_bias_grad,
            out_weight_grad,
            out_bias_grad,
            second_gain_grad,
            second_shift_grad,
            up_weight_grad,
            up_bias_grad,
            down_weight_grad,
            down_bias_grad,
        )
        if totals is None:
            totals = micro_grads
        else:
            totals = tuple(
                (left_sum + right_sum for left_sum, right_sum in zip(totals, micro_grads))
            )
    owned = (
        lax.psum_scatter(totals[0], ("dp", "ctx"), scatter_dimension=0, tiled=True),
        lax.psum_scatter(totals[1], ("dp", "ctx"), scatter_dimension=0, tiled=True),
        lax.psum_scatter(totals[2], ("dp", "ctx"), scatter_dimension=1, tiled=True),
        lax.psum_scatter(totals[3], ("dp", "ctx"), scatter_dimension=0, tiled=True),
        lax.psum_scatter(totals[4], ("dp", "ctx"), scatter_dimension=0, tiled=True),
        lax.psum_scatter(totals[5], ("dp", "ctx"), scatter_dimension=1, tiled=True),
        lax.psum_scatter(totals[6], ("dp", "ctx"), scatter_dimension=0, tiled=True),
        lax.psum_scatter(totals[7], ("dp", "ctx"), scatter_dimension=0, tiled=True),
        lax.psum_scatter(totals[8], ("dp", "ctx"), scatter_dimension=0, tiled=True),
        lax.psum_scatter(totals[9], ("dp", "ctx"), scatter_dimension=1, tiled=True),
        lax.psum_scatter(totals[10], ("dp", "ctx"), scatter_dimension=0, tiled=True),
        lax.psum_scatter(totals[11], ("dp", "ctx"), scatter_dimension=0, tiled=True),
        lax.psum_scatter(totals[12], ("dp", "ctx"), scatter_dimension=0, tiled=True),
    )
    bank_grads = tuple(
        (
            lax.dynamic_update_index_in_dim(
                jnp.zeros(weight_bank.shape, jnp.float32), owned_piece, tie_map[bank_number], 0
            )
            for bank_number, (weight_bank, owned_piece) in enumerate(zip(banks, owned))
        )
    )
    block_output = jnp.stack(outputs)[None]
    input_grad = jnp.stack(input_grads)[None]
    return (block_output, input_grad) + bank_grads


BF = jnp.bfloat16
F32 = jnp.float32
MESH = pl.DeviceIdType.MESH
ANY = pl.ANY
SMALL = 8
VMEM_BYTES = 62 * 2**20


def params(collective_id=None):
    if collective_id is None:
        return pltpu.CompilerParams(vmem_limit_bytes=VMEM_BYTES)
    return pltpu.CompilerParams(
        vmem_limit_bytes=VMEM_BYTES, collective_id=collective_id, has_side_effects=True
    )


def vmem():
    return pl.BlockSpec(memory_space=pltpu.VMEM)


def smem():
    return pl.BlockSpec(memory_space=pltpu.SMEM)


def anywhere():
    return pl.BlockSpec(memory_space=ANY)


def shape(dims, dtype):
    return jax.ShapeDtypeStruct(dims, dtype)


def nn(left, right):
    return lax.dot_general(left, right, (((1,), (0,)), ((), ())), preferred_element_type=F32)


def nt(left, right):
    return lax.dot_general(left, right, (((1,), (1,)), ((), ())), preferred_element_type=F32)


def tn(left, right):
    return lax.dot_general(left, right, (((0,), (0,)), ((), ())), preferred_element_type=F32)


def iota(dims, axis):
    return lax.broadcasted_iota(jnp.int32, dims, axis)


class Place:
    def __init__(self, depth):
        self.depth = depth
        self.z = lax.axis_index("dp")
        self.r = lax.axis_index("ctx")
        self.core = self.r % 2
        self.j = self.r // 2
        self.a = self.r // 4
        self.b = (self.r // 2) % 2
        self.by_a = (1 - self.a) * 4 + self.b * 2 + self.core
        self.by_b = self.a * 4 + (1 - self.b) * 2 + self.core
        self.both = (1 - self.a) * 4 + (1 - self.b) * 2 + self.core
        self.mate = self.j * 2 + 1 - self.core

    def slot(self, z, r):
        return z * 8 + r


def greet_all(here):
    bar = pltpu.get_barrier_semaphore()
    total = here.depth * 8
    me = here.z * 8 + here.r

    def signal(k, carry):
        other = (me + k) % total
        pl.semaphore_signal(bar, inc=1, device_id=(other // 8, other % 8), device_id_type=MESH)
        return carry

    lax.fori_loop(1, total, signal, 0)
    pl.semaphore_wait(bar, total - 1)


def remote(source, target, send, recv, z, r):
    return pltpu.make_async_remote_copy(
        src_ref=source,
        dst_ref=target,
        send_sem=send,
        recv_sem=recv,
        device_id=(z, r),
        device_id_type=MESH,
    )


def spread_units(small, width, hidden_total):
    devices = small.shape[0]
    unit = width // devices
    per = hidden_total // devices
    flat = small.reshape(devices * SMALL, 256)
    lane = iota((128, width), 1)
    pick = (lane % unit == iota((128, width), 0)).astype(F32).astype(BF)
    tall = nn(flat[:, 0:128], pick)
    row = iota((devices * SMALL, width), 0)
    col = iota((devices * SMALL, width), 1)
    tall = jnp.where(col // unit == row // SMALL, tall, 0.0)
    vectors = jnp.sum(tall.reshape(devices, SMALL, width), axis=0)
    chosen = (
        (iota((devices, devices * SMALL), 1) == iota((devices, devices * SMALL), 0) * SMALL)
        .astype(F32)
        .astype(BF)
    )
    firsts = nn(chosen, flat[:, 128:256]).astype(BF)
    lane = iota((128, hidden_total), 1)
    pick = (lane % per == iota((128, hidden_total), 0)).astype(F32).astype(BF)
    wide = nn(firsts, pick)
    keep = iota((devices, hidden_total), 1) // per == iota((devices, hidden_total), 0)
    return vectors, jnp.sum(jnp.where(keep, wide, 0.0), axis=0, keepdims=True)


def gather_vectors(vectors, devices):
    width = vectors.shape[1]
    unit = width // devices
    tall = jnp.broadcast_to(vectors[None], (devices, SMALL, width)).reshape(devices * SMALL, width)
    row = iota((devices * SMALL, width), 0)
    col = iota((devices * SMALL, width), 1)
    tall = jnp.where(col // unit == row // SMALL, tall, 0.0).astype(BF)
    pick = (iota((width, 128), 0) % unit == iota((width, 128), 1)).astype(F32).astype(BF)
    return nn(tall, pick).astype(BF).reshape(devices, SMALL, 128)


def gather_hidden(hidden_row, devices):
    hidden_total = hidden_row.shape[1]
    per = hidden_total // devices
    wide = jnp.broadcast_to(hidden_row, (devices, hidden_total))
    keep = iota((devices, hidden_total), 1) // per == iota((devices, hidden_total), 0)
    wide = jnp.where(keep, wide, 0.0).astype(BF)
    pick = (iota((hidden_total, 128), 0) % per == iota((hidden_total, 128), 1)).astype(F32)
    firsts = nn(wide, pick.astype(BF)).astype(BF)
    chosen = (
        (iota((devices * SMALL, devices), 0) == iota((devices * SMALL, devices), 1) * SMALL)
        .astype(F32)
        .astype(BF)
    )
    return nn(chosen, firsts).astype(BF).reshape(devices, SMALL, 128)


def group_slice(row, j, groups):
    width = row.shape[1] // groups
    out = jnp.zeros((1, width), F32)
    for g in range(groups):
        out = jnp.where(j == g, row[:, g * width : (g + 1) * width], out)
    return out


def group_spread(part, j, groups):
    return jnp.concatenate([jnp.where(j == g, part, 0.0) for g in range(groups)], axis=1)


def block_at(place_ref, micro, position, blocks):
    found = jnp.int32(0)
    for s in range(blocks):
        found = jnp.where(place_ref[0, micro, s] == position, s, found)
    return found


def stack_heads(rows, heads):
    lane = iota(rows.shape, 1) // HD
    zero = jnp.zeros_like(rows)
    return jnp.concatenate([jnp.where(lane == h, rows, zero) for h in range(heads)], axis=0)


def unstack_heads(tall, heads):
    rows = tall.shape[0] // heads
    lane = iota((rows, tall.shape[1]), 1) // HD
    out = tall[0:rows]
    for h in range(1, heads):
        out = jnp.where(lane == h, tall[h * rows : (h + 1) * rows], out)
    return out


def visible_bias(lens, micro, start, rows, key_start, keys):
    query = start + iota((rows, 1), 0)
    begin = jnp.zeros((rows, 1), jnp.int32)
    end = jnp.int32(0)
    for s in range(lens.shape[2]):
        end = end + lens[0, micro, s]
        begin = jnp.where(query >= end, end, begin)
    key = key_start + iota((rows, keys), 1)
    return jnp.where((key >= begin) & (key <= query), 0.0, masked_score)


def row_norm(wide):
    average = jnp.mean(wide, axis=-1, keepdims=True)
    centered = wide - average
    variance = jnp.mean(centered * centered, axis=-1, keepdims=True)
    scale = lax.rsqrt(variance + epsilon)
    return centered * scale, scale


def norm_back(grad, unit, scale):
    first = jnp.mean(grad, axis=-1, keepdims=True)
    second = jnp.mean(grad * unit, axis=-1, keepdims=True)
    return (grad - first - unit * second) * scale


QROWS = 128
KCOLS = 384
GELU_A = math.sqrt(2.0 / math.pi)
GELU_B = 0.044715


class Sizes:
    def __init__(self, depth, rows, width, hidden_total):
        self.depth = depth
        self.rows = rows
        self.width = width
        self.total = depth * 8
        self.unit = width // self.total
        self.per = hidden_total // self.total
        self.group = width // 4
        self.heads = self.group // HD
        self.pack = 8 * rows
        self.packed = self.unit + 2 * self.per
        self.units = self.group // self.unit
        cut = self.per
        self.parts = (
            (0, self.unit, "b"),
            (self.unit, cut, "b"),
            (self.unit + cut, 2 * self.per - cut, "a"),
        )


def block_scratch(n):
    vm = lambda dims, dtype=BF: pltpu.VMEM(dims, dtype)
    dma = lambda dims: pltpu.SemaphoreType.DMA(dims)
    d, w, g, pack, rows = n.depth, n.width, n.group, n.pack, n.rows
    p = len(n.parts)
    both = 2 * rows
    halves = 2 * d
    chunk = n.per * 4
    return {
        "f_all": vm((n.total, n.packed, w)),
        "gr": vm((d, 2, 2, 2, n.packed, w)),
        "from_mate": vm((d, 2, 2, n.packed, w)),
        "from_one": vm((d, 2, n.packed, w)),
        "from_two": vm((d, n.packed, w)),
        "from_z": vm((d, n.packed, w)),
        "q_own": vm((3, n.unit, w)),
        "wts": vm((3, n.units, n.unit, w)),
        "small_all": vm((n.total, SMALL, 256)),
        "x_all": vm((2, 2, 2, rows, w)),
        "h": vm((pack, w)),
        "u": vm((pack, w)),
        "qkv": vm((3, pack, g)),
        "o": vm((pack, -(-(g + n.heads) // 128) * 128), F32),
        "vec": vm((SMALL, w), F32),
        "hid": vm((halves, 1, chunk), F32),
        "hid_grad": vm((halves, 1, chunk), F32),
        "stage": vm((8, rows + rows // 2, 128)),
        "at_recv": vm((8, rows + rows // 2, 128)),
        "da_recv": vm((8, rows + rows // 2, 128)),
        "resid": vm((both, w), F32),
        "unit2": vm((both, w), F32),
        "h2": vm((both, w)),
        "scale2": vm((both, 1), F32),
        "vec_grad": vm((SMALL, w), F32),
        "da": vm((pack, g)),
        "dk_acc": vm((pack, g), F32),
        "dv_acc": vm((pack, g), F32),
        "gq": vm((3, n.units // 2, 2, n.unit, w)),
        "q_mate": vm((3, n.units // 2, n.unit, w)),
        "q_line": vm((3, d, n.unit, w)),
        "dh_a1": vm((2, rows, w)),
        "dh_b1": vm((2, rows, w)),
        "dh_a2": vm((rows, w)),
        "dh_b2": vm((rows, w)),
        "dh_mate": vm((rows, w)),
        "sums": vm((SMALL, w), F32),
        "sg": vm((n.total, SMALL, 256)),
        "sg_recv": vm((n.total, SMALL, 256)),
        "s_zsend": dma((p, d)),
        "s_zrecv": dma((p, d)),
        "s_send1": dma((p, d)),
        "s_recv1": dma((p, d)),
        "s_send2": dma((p, d, 2)),
        "s_recv2": dma((p, d, 2)),
        "s_csend": dma((p, d, 4)),
        "s_crecv": dma((p, d, 4)),
        "s_xsend": dma((7,)),
        "s_xrecv": dma((8,)),
        "s_qsend": dma((3, d)),
        "s_qrecv": dma((3, n.units)),
        "s_qcsend": dma((3, n.units)),
        "s_smsend": dma((n.total,)),
        "s_smrecv": dma((n.total,)),
        "s_asend": dma((8,)),
        "s_arecv": dma((8,)),
        "s_dsend": dma((8,)),
        "s_drecv": dma((8,)),
        "s_rcs": dma((p, d)),
        "s_rcr": dma((p, d)),
        "s_r1s": dma((p, d)),
        "s_r1r": dma((p, d)),
        "s_r2s": dma((p, d)),
        "s_r2r": dma((p, d)),
        "s_rzs": dma((p, d)),
        "s_rzr": dma((p, d)),
        "s_gqc": dma((2,)),
        "s_gqs": dma((3, n.units // 2)),
        "s_gqr": dma((3, d)),
        "s_dhs": dma((5,)),
        "s_dhr": dma((5,)),
        "s_sgs": dma((n.total,)),
        "s_sgr": dma((n.total,)),
    }


def fold(block):
    half = block.shape[0] // 2
    side = jnp.concatenate([block[:half, 128:], block[half:, 128:]], axis=1)
    return jnp.concatenate([block[:, :128], side], axis=0)


def unfold(tall):
    rows = tall.shape[0] * 2 // 3
    side = jnp.concatenate([tall[rows:, :64], tall[rows:, 64:]], axis=0)
    return jnp.concatenate([tall[:rows], side], axis=1)


def add_into(target, source):
    target[...] = (target[...].astype(F32) + source[...].astype(F32)).astype(BF)


def block_kernel(n, names, tie, lens, spans, x_ref, dy_ref, *refs):
    banks = refs[:13]
    y_out, dr_out, dh_out, f_sum, q_sum, small_sum, vec_out = refs[13:20]
    s = types.SimpleNamespace(**dict(zip(names, refs[20:])))
    g1, s1, wq, bq, bv, wo, bo, g2, s2, wu, bu, wd, bd = banks
    depth, unit, per, rows, width, group, heads = (
        n.depth, n.unit, n.per, n.rows, n.width, n.group, n.heads
    )
    here = Place(depth)
    z, r, a, b, core, j = here.z, here.r, here.a, here.b, here.core, here.j
    me = here.slot(z, r)
    micro = core
    mate, by_a, by_b, both = here.mate, here.by_a, here.by_b, here.both
    parts = n.parts
    main = (1, 2)
    groups = 4

    bar = pltpu.get_barrier_semaphore()

    def signal(k, carry):
        other = (me + k) % n.total
        pl.semaphore_signal(bar, inc=1, device_id=(other // 8, other % 8), device_id_type=MESH)
        return carry

    lax.fori_loop(1, n.total, signal, 0)

    f_own = s.f_all.at[me]
    f_own[0:unit, :] = wo[tie[5]]
    f_own[unit : unit + per, :] = wu[tie[9]]
    f_own[unit + per :, :] = wd[tie[11]]
    s.q_own[...] = wq[tie[2]].reshape(3, unit, width)
    chosen_rows = []
    for bank, index in ((g1, 0), (s1, 1), (bq, 3), (bv, 4), (bo, 6), (g2, 7), (s2, 8), (bd, 12)):
        wide = bank[...].astype(F32)
        chosen = jnp.zeros((1, unit), F32)
        for layer in range(bank.shape[0]):
            chosen = jnp.where(tie[index] == layer, wide[layer : layer + 1, :], chosen)
        chosen_rows.append(chosen)
    small_own = s.small_all.at[me]
    small_own[...] = jnp.zeros((SMALL, 256), BF)
    small_own[:, 0:unit] = jnp.concatenate(chosen_rows, axis=0).astype(BF)
    wide = bu[...].astype(F32)
    chosen = jnp.zeros((1, per), F32)
    for layer in range(bu.shape[0]):
        chosen = jnp.where(tie[10] == layer, wide[layer : layer + 1, :], chosen)
    tall = jnp.concatenate([chosen, jnp.zeros((SMALL - 1, per), F32)], axis=0)
    small_own[:, 128 : 128 + per] = tall.astype(BF)

    pl.semaphore_wait(bar, n.total - 1)

    def to_all(buffer_of, send, recv, target):
        def go(k, carry):
            other = (me + k) % n.total
            remote(
                buffer_of(other), target.at[me], send.at[other], recv.at[me], other // 8, other % 8
            ).start()
            return carry

        lax.fori_loop(1, n.total, go, 0)

    def from_all(buffer, send, recv, target):
        def go(k, carry):
            other = (me + k) % n.total
            remote(
                buffer, target.at[other], send.at[other], recv.at[other], other // 8, other % 8
            ).wait()
            return carry

        lax.fori_loop(1, n.total, go, 0)

    def row_block(block):
        return s.x_all.at[block // 4, (block // 2) % 2, block % 2]

    def row_move(source, block, lane, to):
        return remote(source, row_block(block), s.s_xsend.at[lane], s.s_xrecv.at[block], z, to)

    mate_a = by_a + 1 - 2 * core
    row_move(x_ref.at[1 - core], r, 0, mate).start()
    row_move(x_ref.at[core], r, 1, by_b).start()
    row_move(x_ref.at[core], r, 2, by_a).start()
    to_all(lambda other: small_own, s.s_smsend, s.s_smrecv, s.small_all)
    row_block(r)[...] = x_ref[core]

    def q_unit(t):
        block = me * 3 + t
        kind = block // n.total
        inside = block % n.total
        return kind, inside // n.units, inside % n.units

    def q_first(t, zz):
        kind, chip, at = q_unit(t)
        to = chip * 2 + core
        source, target, recv = s.q_own.at[t], s.wts.at[kind, at], s.s_qrecv.at[kind, at]
        go = lambda: remote(source, target, s.s_qsend.at[t, zz], recv, zz, to)
        stay = lambda: pltpu.make_async_copy(source, target, recv)
        return go, stay, (zz == z) & (to == r)

    for t in range(3):
        for zz in range(depth):
            go, stay, mine = q_first(t, zz)

            @pl.when(jnp.logical_not(mine))
            def _():
                go().start()

            @pl.when(mine)
            def _():
                stay().start()

    def order(k):
        out = jnp.int32(0)
        for zz in range(depth):
            line = sorted(range(depth), key=lambda t: (abs(t - zz), t))
            for kk in range(depth):
                out = jnp.where((z == zz) & (k == kk), line[kk], out)
        return out

    def move(p, zz, rr, send, recv, to_z, to_r):
        start, count, _ = parts[p]
        ref = s.f_all.at[here.slot(zz, rr), pl.ds(start, count)]
        return remote(ref, ref, send, recv, to_z, to_r)

    def first_axis(p):
        return by_b if parts[p][2] == "b" else by_a

    def second_axis(p):
        return by_a if parts[p][2] == "b" else by_b

    def line_move(p, o, to_z):
        return move(p, o, r, s.s_zsend.at[p, to_z], s.s_zrecv.at[p, o], to_z, r)

    def one(p, o):
        return move(p, o, r, s.s_send1.at[p, o], s.s_recv1.at[p, o], z, first_axis(p))

    def two(p, o, rr, lane):
        return move(
            p, o, rr, s.s_send2.at[p, o, lane], s.s_recv2.at[p, o, lane], z, second_axis(p)
        )

    def across(p, o, rr, lane):
        return move(p, o, rr, s.s_csend.at[p, o, lane], s.s_crecv.at[p, o, lane], z, mate)

    every = range(len(parts))
    for p in every:
        for k in range(1, depth):
            line_move(p, z, order(k)).start()

    def row_arrived(block):
        row_move(x_ref.at[0], block, 0, mate).wait_recv()

    row_arrived(mate)
    row_move(row_block(mate), mate, 3, by_a).start()
    row_move(row_block(mate), mate, 4, by_b).start()
    row_arrived(by_b)
    row_move(row_block(by_b), by_b, 5, by_a).start()
    row_arrived(mate_a)
    row_move(row_block(mate_a), mate_a, 6, by_b).start()

    def q_relay(e, carry):
        kind, at = e // n.units, e % n.units
        owner = (kind * n.total + j * n.units + at) // 3
        unit_ref = s.wts.at[kind, at]

        @pl.when(owner % 2 == core)
        def _():
            pltpu.make_async_copy(unit_ref, unit_ref, s.s_qrecv.at[kind, at]).wait()
            remote(
                unit_ref, unit_ref, s.s_qcsend.at[kind, at], s.s_qrecv.at[kind, at], z, mate
            ).start()

        return carry

    lax.fori_loop(0, 3 * n.units, q_relay, 0)

    def spread_own(p):
        one(p, z).start()
        two(p, z, r, 0).start()
        across(p, z, r, 0).start()

    for p in every:
        spread_own(p)

    from_all(small_own, s.s_smsend, s.s_smrecv, s.small_all)
    vectors, hidden = spread_units(s.small_all[...], width, per * n.total)
    s.vec[...] = vectors
    vec_out[...] = vectors
    chunk = 4 * per
    for c in range(2 * depth):
        s.hid[c] = hidden[:, c * chunk : (c + 1) * chunk]

    row_arrived(by_a)
    row_arrived(both)
    row_arrived(by_b + 1 - 2 * core)
    row_arrived(both + 1 - 2 * core)

    def q_rest(e, carry):
        kind, at = e // n.units, e % n.units
        owner = (kind * n.total + j * n.units + at) // 3
        unit_ref = s.wts.at[kind, at]

        @pl.when(owner % 2 != core)
        def _():
            remote(
                unit_ref, unit_ref, s.s_qcsend.at[kind, at], s.s_qrecv.at[kind, at], z, mate
            ).wait_recv()

        return carry

    lax.fori_loop(0, 3 * n.units, q_rest, 0)

    gain, shift = s.vec[0:1, :], s.vec[1:2, :]
    query_add = group_slice(s.vec[2:3, :], j, groups)
    value_add = group_slice(s.vec[3:4, :], j, groups)

    def weight(kind):
        return s.wts[kind].reshape(group, width)

    def project(p, carry):
        source = block_at(spans, micro, p, 8)
        unit_rows, _ = row_norm(
            s.x_all[source // 4, (source // 2) % 2, source % 2].astype(F32)
        )
        normed = (unit_rows * gain + shift).astype(BF)
        at = pl.ds(pl.multiple_of(p * rows, 16), rows)
        s.u[at, :] = unit_rows.astype(BF)
        s.h[at, :] = normed
        s.qkv[0, at, :] = (nt(normed, weight(0)) + query_add).astype(BF)
        s.qkv[1, at, :] = nt(normed, weight(1)).astype(BF)
        s.qkv[2, at, :] = (nt(normed, weight(2)) + value_add).astype(BF)
        return carry

    lax.fori_loop(0, 8, project, 0)

    def line_event(k, which):
        o = order(k)
        for p in which:
            line_move(p, o, z).wait_recv()
            one(p, o).start()
            two(p, o, r, 0).start()
            across(p, o, r, 0).start()

    def first_event(k, which):
        o = order(k)
        for p in which:
            one(p, o).wait_recv()
            two(p, o, first_axis(p), 1).start()
            across(p, o, first_axis(p), 1).start()

    def second_event(o, which):
        for p in which:
            two(p, o, r, 0).wait_recv()
            across(p, o, second_axis(p), 2).start()
            two(p, o, r, 1).wait_recv()
            across(p, o, both, 3).start()

    def all_here(o, which):
        for p in which:
            for lane in range(4):
                across(p, o, r, lane).wait_recv()

    gather_events = {
        0: [lambda: line_event(1, (0,)), lambda: first_event(0, (0,))],
        1: [lambda: line_event(2, (0,)), lambda: line_event(3, (0,))],
        2: [lambda: line_event(1, main)],
        3: [lambda: first_event(1, (0,)), lambda: first_event(0, main)],
        5: [lambda: first_event(2, (0,)), lambda: first_event(3, (0,))],
        6: [lambda: first_event(1, main)],
    }

    def run_events(events, i):
        for at, acts in events.items():

            @pl.when(i == at)
            def _(acts=acts):
                for act in acts:
                    act()

    tall = heads * QROWS
    q_blocks = n.pack // QROWS

    def attend(i, carry):
        start = pl.multiple_of(i * QROWS, QROWS)
        stacked = stack_heads(s.qkv[0, pl.ds(start, QROWS), :] * BF(score_scale), heads)

        def step(kc, state):
            top, total, acc = state
            at = pl.ds(pl.multiple_of(kc * KCOLS, KCOLS), KCOLS)
            bias = visible_bias(lens, micro, start, QROWS, kc * KCOLS, KCOLS)
            scores = nt(stacked, s.qkv[1, at, :])
            scores = (scores.reshape(heads, QROWS, KCOLS) + bias[None]).reshape(tall, KCOLS)
            new_top = jnp.maximum(top, jnp.max(scores, axis=1, keepdims=True))
            probs = jnp.exp(scores - new_top)
            factor = jnp.exp(top - new_top)
            total = total * factor + jnp.sum(probs, axis=1, keepdims=True)
            acc = acc * factor + nn(probs.astype(BF), s.qkv[2, at, :])
            return new_top, total, acc

        top, total, acc = lax.fori_loop(
            0,
            (i * QROWS) // KCOLS + 1,
            step,
            (
                jnp.full((tall, 1), masked_score, F32),
                jnp.zeros((tall, 1), F32),
                jnp.zeros((tall, group), F32),
            ),
        )
        at_q = pl.ds(start, QROWS)
        s.o[at_q, 0:group] = unstack_heads(acc / total, heads)
        lse = top + jnp.log(total)
        for head in range(heads):
            s.o[at_q, group + head : group + head + 1] = lse[head * QROWS : (head + 1) * QROWS]
        run_events(gather_events, i)
        return carry

    lax.fori_loop(0, q_blocks, attend, 0)

    for e in range(8):
        at = pl.ds(spans[0, micro, e] * rows, rows)
        s.stage[e] = fold(s.o[at, 0:group].astype(BF))

    def exchange_start(stage, target, send, recv):
        for k in range(1, 8):
            to = (r + k) % 8
            remote(stage.at[to], target.at[r], send.at[to], recv.at[r], z, to).start()
        target[r] = stage[r]

    def exchange_wait(stage, target, send, recv):
        for k in range(1, 8):
            frm = (r + k) % 8
            remote(stage.at[frm], target.at[frm], send.at[frm], recv.at[frm], z, frm).wait()

    exchange_start(s.stage, s.at_recv, s.s_asend, s.s_arecv)
    for k in range(2, depth):
        line_event(k, main)
    for k in range(depth):
        second_event(order(k), (0,))
    second_event(z, main)
    for k in range(depth):
        all_here(order(k), (0,))
    exchange_wait(s.stage, s.at_recv, s.s_asend, s.s_arecv)

    full = 2 * rows
    def attended():
        pieces = [
            jnp.concatenate([unfold(s.at_recv[2 * g]), unfold(s.at_recv[2 * g + 1])], axis=0)
            for g in range(groups)
        ]
        return jnp.concatenate(pieces, axis=1)

    out_w = s.f_all[:, 0:unit, :].reshape(width, width)
    res = (
        x_ref[...].reshape(full, width).astype(F32) + nt(attended(), out_w) + s.vec[4:5, :]
    )
    s.resid[...] = res + s.vec[7:8, :]
    unit_rows, scale = row_norm(res)
    s.unit2[...] = unit_rows
    s.scale2[...] = scale
    s.h2[...] = (unit_rows * s.vec[5:6, :] + s.vec[6:7, :]).astype(BF)
    dr_out[...] = jnp.zeros_like(dr_out)

    def cut(p):
        return pl.ds(parts[p][0], parts[p][1])

    def sum_mate(p, t):
        return remote(
            s.gr.at[t, :, :, 1 - core, cut(p)],
            s.from_mate.at[t, :, :, cut(p)],
            s.s_rcs.at[p, t],
            s.s_rcr.at[p, t],
            z,
            mate,
        )

    def sum_first(p, t):
        if parts[p][2] == "b":
            source, to = s.gr.at[t, 1 - a, :, core, cut(p)], by_a
        else:
            source, to = s.gr.at[t, :, 1 - b, core, cut(p)], by_b
        target = s.from_one.at[t, :, cut(p)]
        return remote(source, target, s.s_r1s.at[p, t], s.s_r1r.at[p, t], z, to)

    def sum_second(p, t):
        if parts[p][2] == "b":
            source, to = s.gr.at[t, a, 1 - b, core, cut(p)], by_b
        else:
            source, to = s.gr.at[t, 1 - a, b, core, cut(p)], by_a
        target = s.from_two.at[t, cut(p)]
        return remote(source, target, s.s_r2s.at[p, t], s.s_r2r.at[p, t], z, to)

    def sum_line(p, t, origin):
        return remote(
            s.gr.at[t, a, b, core, cut(p)],
            s.from_z.at[origin, cut(p)],
            s.s_rzs.at[p, t],
            s.s_rzr.at[p, origin],
            t,
            r,
        )

    def start_sum(t, which):
        for p in which:
            sum_mate(p, t).start()

    def event_one(t, which):
        for p in which:
            sum_mate(p, t).wait_recv()
            for aa in range(2):
                for bb in range(2):
                    add_into(s.gr.at[t, aa, bb, core, cut(p)], s.from_mate.at[t, aa, bb, cut(p)])
            sum_first(p, t).start()

    def event_two(t, which):
        for p in which:
            sum_first(p, t).wait_recv()
            for e in range(2):
                mine = (
                    s.gr.at[t, a, e, core, cut(p)]
                    if parts[p][2] == "b"
                    else s.gr.at[t, e, b, core, cut(p)]
                )
                add_into(mine, s.from_one.at[t, e, cut(p)])
            sum_second(p, t).start()

    def event_three(t, which):
        for p in which:
            sum_second(p, t).wait_recv()
            add_into(s.gr.at[t, a, b, core, cut(p)], s.from_two.at[t, cut(p)])

            @pl.when(t != z)
            def _(p=p):
                sum_line(p, t, z).start()

    g_down = dy_ref[...].reshape(full, width)

    def feed(c, carry):
        k, half = c // 2, c % 2
        o = order(k)

        for kk in range(1, depth):

            @pl.when((half == 0) & (k == kk))
            def _(kk=kk):
                if kk + 1 < depth:
                    first_event(kk + 1, main)
                second_event(order(kk), main)

        @pl.when(half == 0)
        def _():
            all_here(o, main)

        devices = pl.ds(o * 8 + half * 4, 4)
        up_w = s.f_all[devices, unit : unit + per, :].reshape(chunk, width)
        down_w = s.f_all[devices, unit + per : unit + 2 * per, :].reshape(chunk, width)
        where = o * 2 + half
        up = nt(s.h2[...], up_w) + s.hid[where]
        square = up * up
        tanh = jnp.tanh(GELU_A * (up + GELU_B * square * up))
        side = 0.5 * (1.0 + tanh)
        act = (up * side).astype(BF)
        s.resid[...] += nn(act, down_w)
        slope = side + 0.5 * up * (1.0 - tanh * tanh) * (GELU_A * (1.0 + 3.0 * GELU_B * square))
        grad = dy_ref[...].reshape(full, width)
        d_up = (nt(grad, down_w) * slope).astype(BF)
        s.hid_grad[where] = jnp.sum(d_up.astype(F32), axis=0, keepdims=True)
        dr_out[...] += nn(d_up, up_w).reshape(2, rows, width)
        s.gr[o, half, :, :, unit : unit + per, :] = (
            tn(d_up, s.h2[...]).astype(BF).reshape(2, 2, per, width)
        )
        s.gr[o, half, :, :, unit + per : unit + 2 * per, :] = (
            tn(act, grad).astype(BF).reshape(2, 2, per, width)
        )

        @pl.when(half == 1)
        def _():
            start_sum(o, main)

            @pl.when(k > 0)
            def _():
                event_one(order(k - 1), main)

        return carry

    lax.fori_loop(0, 2 * depth, feed, 0)

    dy = g_down.astype(F32)
    d_h2 = dr_out[...].reshape(full, width)
    unit_rows = s.unit2[...]
    d_res = dy + norm_back(d_h2 * s.vec[5:6, :], unit_rows, s.scale2[...])
    dr_out[...] = d_res.reshape(2, rows, width)
    g_mix = d_res.astype(BF)
    d_attn = nn(g_mix, s.f_all[:, 0:unit, :].reshape(width, width)).astype(BF)
    for m in range(2):
        for g in range(groups):
            s.stage[2 * g + m] = fold(
                d_attn[m * rows : (m + 1) * rows, g * group : (g + 1) * group]
            )
    exchange_start(s.stage, s.da_recv, s.s_dsend, s.s_drecv)
    y_out[...] = s.resid[...].astype(BF).reshape(2, rows, width)
    out_grad = tn(g_mix, attended()).astype(BF).reshape(depth, 2, 2, 2, unit, width)
    s.gr[:, :, :, :, 0:unit, :] = out_grad
    for k in range(depth):
        start_sum(order(k), (0,))
    s.vec_grad[...] = jnp.zeros_like(s.vec_grad)
    s.vec_grad[4:5, :] = jnp.sum(g_mix.astype(F32), axis=0, keepdims=True)
    s.vec_grad[5:6, :] = jnp.sum(d_h2 * unit_rows, axis=0, keepdims=True)
    s.vec_grad[6:7, :] = jnp.sum(d_h2, axis=0, keepdims=True)
    s.vec_grad[7:8, :] = jnp.sum(dy, axis=0, keepdims=True)
    event_one(order(depth - 1), main)
    hidden_row = jnp.concatenate([s.hid_grad[c] for c in range(2 * depth)], axis=1)
    s.sg[:, :, 128:256] = gather_hidden(hidden_row, n.total)
    exchange_wait(s.stage, s.da_recv, s.s_dsend, s.s_drecv)

    for p in range(8):
        s.da[p * rows : (p + 1) * rows, :] = unfold(s.da_recv[block_at(spans, micro, p, 8)])
    s.dk_acc[...] = jnp.zeros_like(s.dk_acc)
    s.dv_acc[...] = jnp.zeros_like(s.dv_acc)

    def out_events(act):
        def go():
            for k in range(depth):
                act(order(k), (0,))

        return go

    sum_events = {
        0: [lambda: event_two(order(1), main)],
        1: [lambda: event_two(order(2), main)],
        3: [lambda: event_three(order(1), main), out_events(event_one)],
        5: [lambda: event_two(order(3), main)],
        6: [lambda: event_three(order(2), main), out_events(event_two)],
        7: [lambda: event_two(order(0), main)],
        8: [lambda: event_three(order(3), main), out_events(event_three), lambda: event_three(order(0), main)],
    }

    def query_block(i, carry):
        start = pl.multiple_of(i * QROWS, QROWS)
        at_q = pl.ds(start, QROWS)
        stacked = stack_heads(s.qkv[0, at_q, :] * BF(score_scale), heads)
        d_rows = s.da[at_q, :]
        d_stacked = stack_heads(d_rows, heads)
        product = d_rows.astype(F32) * s.o[at_q, 0:group]
        delta = jnp.sum(stack_heads(product, heads), axis=1, keepdims=True)
        lse = jnp.concatenate(
            [s.o[at_q, group + head : group + head + 1] for head in range(heads)], axis=0
        )

        def step(kc, acc):
            at = pl.ds(pl.multiple_of(kc * KCOLS, KCOLS), KCOLS)
            bias = visible_bias(lens, micro, start, QROWS, kc * KCOLS, KCOLS)
            keys = s.qkv[1, at, :]
            scores = nt(stacked, keys)
            scores = (scores.reshape(heads, QROWS, KCOLS) + bias[None]).reshape(tall, KCOLS)
            probs = jnp.exp(scores - lse)
            d_probs = nt(d_stacked, s.qkv[2, at, :])
            d_scores = (probs * (d_probs - delta)).astype(BF)
            s.dk_acc[at, :] += tn(d_scores, stacked)
            s.dv_acc[at, :] += tn(probs.astype(BF), d_stacked)
            return acc + nn(d_scores, keys)

        acc = lax.fori_loop(0, (i * QROWS) // KCOLS + 1, step, jnp.zeros((tall, group), F32))
        s.qkv[0, at_q, :] = (unstack_heads(acc, heads) * score_scale).astype(BF)
        run_events(sum_events, i)
        return carry

    lax.fori_loop(0, q_blocks, query_block, 0)
    s.qkv[1] = s.dk_acc[...].astype(BF)
    s.qkv[2] = s.dv_acc[...].astype(BF)

    pairs = n.units // 2
    q_mate = remote(
        s.gq.at[:, :, 1 - core], s.q_mate, s.s_gqc.at[0], s.s_gqc.at[1], z, mate
    )

    def q_route(kind, m):
        block = kind * n.total + j * n.units + m * 2 + core
        owner = block // 3
        return owner // 8, owner % 8, block % 3

    def q_out(kind, m):
        oz, orr, at = q_route(kind, m)
        source = s.gq.at[kind, m, core]
        target, send = s.q_line.at[at, z], s.s_gqs.at[kind, m]
        go = lambda: remote(source, target, send, s.s_gqr.at[at, z], oz, orr)
        stay = lambda: pltpu.make_async_copy(source, target, send)
        return go, stay, (oz == z) & (orr == r)

    def q_sums(act):
        def each(e, carry):
            kind, m = e // pairs, e % pairs
            go, stay, mine = q_out(kind, m)
            act(kind, m, go, stay, mine)
            return carry

        lax.fori_loop(0, 3 * pairs, each, 0)

    def q_send(kind, m, go, stay, mine):
        add_into(s.gq.at[kind, m, core], s.q_mate.at[kind, m])

        @pl.when(jnp.logical_not(mine))
        def _():
            go().start()

        @pl.when(mine)
        def _():
            stay().start()

    def q_sent(kind, m, go, stay, mine):
        @pl.when(jnp.logical_not(mine))
        def _():
            go().wait_send()

        @pl.when(mine)
        def _():
            stay().wait()

    for lane in range(7):
        row_move(x_ref.at[0], r, lane, mate).wait_send()
    s.sums[...] = jnp.zeros_like(s.sums)

    def dh_a1():
        return remote(s.x_all.at[1 - a, :, core], s.dh_a1, s.s_dhs.at[0], s.s_dhr.at[0], z, by_a)

    def dh_b1():
        return remote(s.x_all.at[:, 1 - b, 1 - core], s.dh_b1, s.s_dhs.at[1], s.s_dhr.at[1], z, by_b)

    def dh_a2():
        return remote(s.x_all.at[a, 1 - b, core], s.dh_a2, s.s_dhs.at[2], s.s_dhr.at[2], z, by_b)

    def dh_b2():
        return remote(s.x_all.at[1 - a, b, 1 - core], s.dh_b2, s.s_dhs.at[3], s.s_dhr.at[3], z, by_a)

    def dh_m():
        return remote(s.x_all.at[a, b, 1 - core], s.dh_mate, s.s_dhs.at[4], s.s_dhr.at[4], z, mate)


    def unsort(e, carry):
        late, kind, lane = e // 4, (e % 4) // 2, e % 2
        aa = jnp.where(kind == 0, jnp.where(late == 1, a, 1 - a), lane)
        bb = jnp.where(kind == 0, lane, jnp.where(late == 1, b, 1 - b))
        cc = jnp.where(kind == 0, core, 1 - core)
        at = pl.ds(spans[0, micro, aa * 4 + bb * 2 + cc] * rows, rows)
        part = (
            nn(s.qkv[0, at, :], weight(0))
            + nn(s.qkv[1, at, :], weight(1))
            + nn(s.qkv[2, at, :], weight(2))
        )
        s.x_all[aa, bb, cc] = part.astype(BF)
        s.sums[0:1, :] += jnp.sum(part * s.u[at, :].astype(F32), axis=0, keepdims=True)
        s.sums[1:2, :] += jnp.sum(part, axis=0, keepdims=True)

        @pl.when(e == 3)
        def _():
            dh_a1().start()
            dh_b1().start()

        return carry

    lax.fori_loop(0, 8, unsort, 0)

    query_bias = jnp.sum(s.qkv[0].astype(F32), axis=0, keepdims=True)
    value_bias = jnp.sum(s.qkv[2].astype(F32), axis=0, keepdims=True)
    s.vec_grad[0:2, :] = s.sums[0:2, :]
    s.vec_grad[2:3, :] = group_spread(query_bias, j, groups)
    s.vec_grad[3:4, :] = group_spread(value_bias, j, groups)
    s.sg[:, :, 0:128] = gather_vectors(s.vec_grad[...], n.total)
    to_all(lambda other: s.sg.at[other], s.s_sgs, s.s_sgr, s.sg_recv)
    s.sg_recv[me] = s.sg[me]
    for kind in range(3):
        s.gq[kind] = tn(s.qkv[kind], s.h[...]).astype(BF).reshape(pairs, 2, unit, width)
    q_mate.start()

    dh_a1().wait_recv()
    for e in range(2):
        add_into(s.x_all.at[a, e, core], s.dh_a1.at[e])
    dh_a2().start()
    dh_b1().wait_recv()
    for e in range(2):
        add_into(s.x_all.at[e, b, 1 - core], s.dh_b1.at[e])
    dh_b2().start()
    q_mate.wait_recv()
    q_sums(q_send)
    dh_b2().wait_recv()
    add_into(s.x_all.at[a, b, 1 - core], s.dh_b2)
    dh_m().start()

    for k in range(1, depth):
        o = order(k)
        for p in every:
            sum_line(p, z, o).wait_recv()
    total_rows = s.gr[z, a, b, core].astype(F32)
    for k in range(1, depth):
        total_rows = total_rows + s.from_z[order(k)].astype(F32)
    f_sum[...] = total_rows

    dh_a2().wait_recv()
    dh_out[core] = s.x_all[a, b, core].astype(F32) + s.dh_a2[...].astype(F32)
    dh_m().wait_recv()
    dh_out[1 - core] = s.dh_mate[...].astype(F32)

    from_all(s.sg.at[0], s.s_sgs, s.s_sgr, s.sg_recv)
    small_sum[...] = jnp.sum(s.sg_recv[...].astype(F32), axis=0)

    def q_arrivals(at, zz):
        block = me * 3 + at
        inside = block % n.total
        from_r = (inside // n.units) * 2 + (inside % n.units) % 2
        ref = s.q_line.at[at, zz]
        come = lambda: remote(ref, ref, s.s_gqs.at[0, 0], s.s_gqr.at[at, zz], zz, from_r)
        return come, (from_r == r) & (zz == z)

    for at in range(3):
        for zz in range(depth):
            come, mine = q_arrivals(at, zz)

            @pl.when(jnp.logical_not(mine))
            def _():
                come().wait_recv()

    q_sums(q_sent)
    for at in range(3):
        part = s.q_line[at, 0].astype(F32)
        for zz in range(1, depth):
            part = part + s.q_line[at, zz].astype(F32)
        q_sum[at] = part

    for t in range(3):
        for zz in range(depth):
            go, _, mine = q_first(t, zz)

            @pl.when(jnp.logical_not(mine))
            def _():
                go().wait_send()

    def q_relayed(e, carry):
        kind, at = e // n.units, e % n.units
        owner = (kind * n.total + j * n.units + at) // 3
        unit_ref = s.wts.at[kind, at]

        @pl.when(owner % 2 == core)
        def _():
            remote(
                unit_ref, unit_ref, s.s_qcsend.at[kind, at], s.s_qrecv.at[kind, at], z, mate
            ).wait_send()

        return carry

    lax.fori_loop(0, 3 * n.units, q_relayed, 0)
    q_mate.wait_send()
    for act in (dh_a1, dh_b1, dh_a2, dh_b2, dh_m):
        act().wait_send()

    def drain(o, carry):
        for p in every:
            one(p, o).wait_send()
            for lane in range(2):
                two(p, o, r, lane).wait_send()
            for lane in range(4):
                across(p, o, r, lane).wait_send()
            sum_mate(p, o).wait_send()
            sum_first(p, o).wait_send()
            sum_second(p, o).wait_send()

            @pl.when(o != z)
            def _(p=p):
                line_move(p, z, o).wait_send()
                sum_line(p, o, z).wait_send()

        return carry

    lax.fori_loop(0, depth, drain, 0)


def run_block(n, tie_map, lens, spans, x_own, dy_own, banks):
    rows, width = n.rows, n.width
    scratch = block_scratch(n)
    outs = (
        shape((2, rows, width), BF),
        shape((2, rows, width), F32),
        shape((2, rows, width), F32),
        shape((n.packed, width), F32),
        shape((3, n.unit, width), F32),
        shape((SMALL, 256), F32),
        shape((SMALL, width), F32),
    )
    return pl.pallas_call(
        functools.partial(block_kernel, n, tuple(scratch)),
        name="block",
        out_shape=outs,
        in_specs=[smem()] * 3 + [vmem()] * 15,
        out_specs=(vmem(),) * len(outs),
        scratch_shapes=list(scratch.values()),
        compiler_params=params(1),
    )(tie_map, lens, spans, x_own, dy_own, *banks)


def final_kernel(
    n, tie, x_ref, y_ref, dh_ref, dr_ref, vec_ref, f_ref, q_ref, small_ref, y_out, dx_out, *grads
):
    g1, s1, wq, bq, bv, wo, bo, g2, s2, wu, bu, wd, bd = grads
    y_out[...] = y_ref[...]
    for m in range(x_ref.shape[0]):
        unit_rows, scale = row_norm(x_ref[m].astype(F32))
        back = norm_back(dh_ref[m] * vec_ref[0:1, :], unit_rows, scale)
        dx_out[m] = (dr_ref[m] + back).astype(BF)
    layers = wq.shape[0]
    unit, per = n.unit, n.per

    def put(ref, index, value):
        for layer in range(layers):
            ref[layer] = jnp.where(tie[index] == layer, value, 0.0)

    put(wo, 5, f_ref[0:unit, :])
    put(wu, 9, f_ref[unit : unit + per, :])
    put(wd, 11, f_ref[unit + per :, :])
    put(wq, 2, q_ref[...].reshape(3 * unit, n.width))
    names = ((g1, 0), (s1, 1), (bq, 3), (bv, 4), (bo, 6), (g2, 7), (s2, 8), (bd, 12))
    for e, (ref, index) in enumerate(names):
        for layer in range(layers):
            ref[layer : layer + 1, :] = jnp.where(
                tie[index] == layer, small_ref[e : e + 1, 0:unit], 0.0
            )
    for layer in range(layers):
        bu[layer : layer + 1, :] = jnp.where(
            tie[10] == layer, small_ref[0:1, 128 : 128 + per], 0.0
        )


def turned(bank):
    return jnp.swapaxes(bank, 1, 2)


def grouped_plan(depth, *args):
    block_input, cotangent, tie_map, seq_lengths, span_place = args[:5]
    banks = list(args[5:])
    for index in (2, 5, 9):
        banks[index] = turned(banks[index])
    x_own, dy_own = block_input[0], cotangent[0]
    n = Sizes(depth, x_own.shape[1], x_own.shape[2], banks[10].shape[1] * depth * 8)
    y, d_resid, dh, f_sum, q_sum, small_sum, vectors = run_block(
        n, tie_map, seq_lengths, span_place, x_own, dy_own, banks
    )
    outs = (shape(x_own.shape, BF),) * 2 + tuple(shape(bank.shape, F32) for bank in banks)
    final = pl.pallas_call(
        functools.partial(final_kernel, n),
        name="finish",
        out_shape=outs,
        in_specs=[smem()] + [vmem()] * 8,
        out_specs=(vmem(),) * len(outs),
        compiler_params=params(),
    )(tie_map, x_own, y, dh, d_resid, vectors, f_sum, q_sum, small_sum)
    grads = list(final[2:])
    for index in (2, 5, 9):
        grads[index] = turned(grads[index])
    return (final[0][None], final[1][None]) + tuple(grads)


def fits_grouped(mesh, block_input, span_place, qkv_weight):
    width = qkv_weight.shape[1]
    rows = block_input.shape[2] // mesh.shape["ctx"]
    total = mesh.shape["ctx"] * mesh.shape["dp"]
    return (
        mesh.shape["ctx"] == 8
        and block_input.shape[1] == 2
        and HEADS % 4 == 0
        and HEADS * HD == width
        and rows % 16 == 0
        and width // 4 == 192
        and block_input.shape[2] % KCOLS == 0
        and width % total == 0
        and (width // total) % 8 == 0
        and (width // 4) % (2 * (width // total)) == 0
    )


def solution(mesh):
    replicated_rows = P("dp", None, "ctx", None)
    vector = P(None, ("dp", "ctx"))
    columns = P(None, None, ("dp", "ctx"))
    bank_specs = (
        vector,
        vector,
        columns,
        vector,
        vector,
        columns,
        vector,
        vector,
        vector,
        columns,
        vector,
        P(None, ("dp", "ctx"), None),
        vector,
    )

    def step(*args):
        if fits_grouped(mesh, args[0], args[4], args[7]):
            plan = functools.partial(grouped_plan, mesh.shape["dp"])
        else:
            plan = general_plan
        return jax.shard_map(
            plan,
            mesh=mesh,
            in_specs=(
                replicated_rows,
                replicated_rows,
                P(),
                P("dp", None, None),
                P("dp", None, None),
            )
            + bank_specs,
            out_specs=(replicated_rows, replicated_rows) + bank_specs,
            check_vma=False,
        )(*args)

    return step
```
